32 devices in a mesh: ctx: 8 (over z, x), wsh: 4 (over y, core).
Axes of the slice: x: 2, y: 2, z: 4, core: 2. Of those that a mesh axis runs over, the one named last changes fastest.
Arguments:
- decoder_in: bfloat16 [4, 1536, 512], P('wsh', 'ctx'), may hold values from -6 to 6
- memory: bfloat16 [4, 2048, 512], P('wsh', 'ctx'), may hold values from -6 to 6
- seq_lengths: int32 [4], P('wsh'), may hold values from 384 to 1536, as said below
- mem_lengths: int32 [4], P('wsh'), may hold values from 1024 to 2048, as said below
- self_query: bfloat16 [512, 512], P('wsh'), may hold values from -0.5 to 0.5
- self_keyval: bfloat16 [512, 1024], P('wsh'), may hold values from -0.25 to 0.25
- self_out: bfloat16 [512, 512], P('wsh'), may hold values from -1.25 to 1.25
- cross_query: bfloat16 [512, 512], P('wsh'), may hold values from -0.5 to 0.5
- cross_keyval: bfloat16 [512, 1024], P('wsh'), may hold values from -0.25 to 0.25
- cross_out: bfloat16 [512, 512], P('wsh'), may hold values from -1.5 to 1.5
- ffn_in: bfloat16 [512, 2048], P('wsh'), may hold values from -0.25 to 0.25
- ffn_bias_in: bfloat16 [2048], P('wsh'), may hold values from -3 to 3
- ffn_out: bfloat16 [2048, 512], P('wsh'), may hold values from -0.125 to 0.125
- ffn_bias_out: bfloat16 [512], P('wsh'), may hold values from -3 to 3
- slot_weight: bfloat16 [1024, 512], P('wsh'), may hold values from -0.1875 to 0.1875
- norm_gain: bfloat16 [3, 512], P(None, 'wsh'), may hold values from 0.099609375 to 1.8984375
- norm_bias: bfloat16 [3, 512], P(None, 'wsh'), may hold values from -3 to 3
- cotangent: bfloat16 [4, 1536, 512], P('wsh', 'ctx'), may hold values from -6 to 6
Outputs:
- slots: bfloat16 [4, 1536, 512], P('wsh', 'ctx')
- grad_input: float32 [4, 1536, 512], P('wsh', 'ctx')
- grad_memory: float32 [4, 2048, 512], P('wsh', 'ctx')
- grad_self_query: float32 [512, 512], P('wsh')
- grad_self_keyval: float32 [512, 1024], P('wsh')
- grad_self_out: float32 [512, 512], P('wsh')
- grad_cross_query: float32 [512, 512], P('wsh')
- grad_cross_keyval: float32 [512, 1024], P('wsh')
- grad_cross_out: float32 [512, 512], P('wsh')
- grad_ffn_in: float32 [512, 2048], P('wsh')
- grad_ffn_bias_in: float32 [2048], P('wsh')
- grad_ffn_out: float32 [2048, 512], P('wsh')
- grad_ffn_bias_out: float32 [512], P('wsh')
- grad_slot_weight: float32 [1024, 512], P('wsh')
- grad_norm_gain: float32 [3, 512], P(None, 'wsh')
- grad_norm_bias: float32 [3, 512], P(None, 'wsh')
The draws below stay inside these ranges and needn't reach their ends.
Inputs may be any that keep to these rules, and one draw needn't show every extreme that they name: `seq_lengths`: some sequence has all 1536 positions live. `mem_lengths`: some sequence has all 2048 memory rows live.
All inputs are finite; a program needn't handle non-finite values.
Results may differ from the reference program's by a relative error of at most 0.034.
The reference program's roundings to bfloat16 on the way count: a program that leaves them out, or rounds other values in their place, can miss the bound.
Values may be sent and summed in bfloat16 or wider, within the bound.
No kernel may reach another device: no remote copies, remote signals or barrier semaphores. Data moves between devices by JAX's collectives and lax.ppermute only.
A program may use at most 256 MiB of HBM per device.

```python
import math
import jax
import jax.numpy as jnp
from jax import lax

D = 512
HEADS = 8
FF = 2048
MEM = 2048
SLOTS = 1536
SEQS = 4


def draw_seq_lengths(key, part):
    spread = jax.random.randint(jax.random.fold_in(key, 11), (SEQS,), SLOTS // 4, SLOTS + 1)
    chosen = jax.random.randint(jax.random.fold_in(key, 12), (), 0, SEQS)
    return jnp.where(jnp.arange(SEQS, dtype=jnp.int32) == chosen, SLOTS, spread).astype(jnp.int32)


def draw_mem_lengths(key, part):
    spread = jax.random.randint(jax.random.fold_in(key, 21), (SEQS,), MEM // 2, MEM + 1)
    chosen = jax.random.randint(jax.random.fold_in(key, 22), (), 0, SEQS)
    return jnp.where(jnp.arange(SEQS, dtype=jnp.int32) == chosen, MEM, spread).astype(jnp.int32)


def block_levels(rng, extent, pieces, least, top_value):
    gain, own = 1.0, jax.random.fold_in(rng, 6)
    for position, blocks in pieces:
        steps = jnp.exp(jax.random.uniform(jax.random.fold_in(own, position), (blocks,), jnp.float32, least / len(pieces), top_value / len(pieces)))
        gain = gain * jnp.repeat(steps, extent[position] // blocks).reshape([-1 if axis == position else 1 for axis in range(len(extent))])
    return gain


def gaussian(own_key, extent, scale, bound, shards=(), kind=jnp.bfloat16):
    loudness = block_levels(own_key, extent, shards, -0.22, 0.18) if shards else 1.0
    drawn = jax.random.normal(own_key, extent, jnp.float32) * scale * loudness
    return jnp.minimum(jnp.maximum(drawn, -bound), bound).astype(kind)


def setup_inputs(seed: int = 0) -> dict:
    keys = jax.random.split(jax.random.key(seed), 19)
    return {
        "decoder_in": gaussian(keys[0], (SEQS, SLOTS, D), 1.0, 6.0, ((0, 4), (1, 8))),
        "memory": gaussian(keys[1], (SEQS, MEM, D), 1.0, 6.0, ((0, 4), (1, 8))),
        "seq_lengths": draw_seq_lengths(jax.random.fold_in(keys[18], 71), 0),
        "mem_lengths": draw_mem_lengths(jax.random.fold_in(keys[18], 71), 0),
        "self_query": gaussian(keys[4], (D, D), (D // 4) ** -0.5, 0.5, ((0, 4),)),
        "self_keyval": gaussian(keys[5], (D, 2 * D), D ** -0.5, 0.25, ((0, 4),)),
        "self_out": gaussian(keys[6], (D, D), (max(1, D * 64 // SLOTS)) ** -0.5, 1.25, ((0, 4),)),
        "cross_query": gaussian(keys[7], (D, D), (D // 4) ** -0.5, 0.5, ((0, 4),)),
        "cross_keyval": gaussian(keys[8], (D, 2 * D), D ** -0.5, 0.25, ((0, 4),)),
        "cross_out": gaussian(keys[9], (D, D), (max(1, D * 64 // MEM)) ** -0.5, 1.5, ((0, 4),)),
        "ffn_in": gaussian(keys[10], (D, FF), D ** -0.5, 0.25, ((0, 4),)),
        "ffn_bias_in": gaussian(keys[11], (FF,), 0.5, 3.0, ((0, 4),)),
        "ffn_out": gaussian(keys[12], (FF, D), FF ** -0.5, 0.125, ((0, 4),)),
        "ffn_bias_out": gaussian(keys[13], (D,), 0.5, 3.0, ((0, 4),)),
        "slot_weight": gaussian(keys[14], (2 * D, D), (2 * D) ** -0.5, 0.1875, ((0, 4),)),
        "norm_gain": jnp.clip(1.0 + 0.18 * jax.random.normal(keys[15], (3, D), jnp.float32), 0.099609375, 1.8984375).astype(jnp.bfloat16),
        "norm_bias": gaussian(keys[16], (3, D), 0.6, 3.0, ((1, 4),)),
        "cotangent": gaussian(keys[17], (SEQS, SLOTS, D), 1.0, 6.0, ((0, 4), (1, 8))),
    }


@jax.custom_vjp
def low(v):
    return lax.optimization_barrier(v.astype(jnp.bfloat16)).astype(jnp.float32)

@jax.custom_vjp
def low_back(v):
    return v

def low_keep(v):
    return (low(v), None)

def low_pass(kept, grad):
    return (grad,)

def back_keep(v):
    return (v, None)

def back_low(kept, grad):
    return (low(grad),)
low.defvjp(low_keep, low_pass)
low_back.defvjp(back_keep, back_low)
NORM_EPS = 1e-05
MASK_FILL = -1e+30

def matmul_high(left, right):
    return jnp.dot(left, right, precision=lax.Precision.HIGHEST, preferred_element_type=jnp.float32)

def norm_rows(values, gain_row, bias_row):
    center = values - lax.optimization_barrier(jnp.mean(values, axis=-1, keepdims=True))
    spread = lax.optimization_barrier(jnp.mean(center * center, axis=-1, keepdims=True))
    return center * lax.rsqrt(spread + NORM_EPS) * gain_row + bias_row

def attend(queries, keyvals, key_valid):
    n_rows, n_width = queries.shape
    head_dim = n_width // HEADS
    scaling = head_dim ** (-0.5)
    key_part = keyvals[:, :n_width].reshape(-1, HEADS, head_dim)
    value_part = keyvals[:, n_width:].reshape(-1, HEADS, head_dim)
    stride = math.gcd(n_rows, 512)

    def one_block(query_block):
        query_heads = query_block.reshape(stride, HEADS, head_dim)
        scores = low_back(jnp.einsum('qhd,khd->hqk', query_heads, key_part, precision=lax.Precision.HIGHEST) * scaling)
        scores = jnp.where(key_valid[None, None, :], scores, MASK_FILL)
        weights = jax.nn.softmax(scores, axis=-1)
        mixed = jnp.einsum('hqk,khd->qhd', weights, value_part, precision=lax.Precision.HIGHEST)
        return mixed.reshape(stride, n_width)
    blocks = lax.map(jax.checkpoint(one_block), queries.reshape(n_rows // stride, stride, n_width))
    return low(low_back(blocks.reshape(n_rows, n_width)))

def layer(tokens, mem_rows, params, valid, mem_valid):
    w_query, w_keyval, w_out, c_query, c_keyval, c_out, w_first, b_first, w_second, b_second, w_slot, gains, biases = params
    validf = valid.astype(jnp.float32)[:, None]
    queries = low(low_back(matmul_high(tokens, w_query)))
    keyvals = low(low_back(matmul_high(tokens, w_keyval)))
    self_mixed = attend(queries, keyvals, valid)
    first_sum = tokens + low_back(matmul_high(self_mixed, w_out))
    hidden_one = norm_rows(first_sum, gains[0], biases[0])
    cross_queries = low(low_back(matmul_high(low(hidden_one), c_query)))
    mem_keyvals = low(low_back(matmul_high(mem_rows, c_keyval)))
    cross_mixed = attend(cross_queries, mem_keyvals, mem_valid)
    second_sum = hidden_one + low_back(matmul_high(cross_mixed, c_out))
    hidden_two = norm_rows(second_sum, gains[1], biases[1])
    preact = low_back(matmul_high(low(hidden_two), w_first) + b_first)
    active = low(jax.nn.gelu(preact))
    third_sum = hidden_two + low_back(matmul_high(active, w_second) + b_second)
    hidden_three = norm_rows(third_sum, gains[2], biases[2])
    masked = low(hidden_three * validf)
    neighbour = jnp.concatenate([masked[1:], jnp.zeros_like(masked[:1])], axis=0)
    paired = jnp.concatenate([masked, neighbour], axis=1)
    return matmul_high(paired, w_slot) * validf

def reference(decoder_in, memory, seq_lengths, mem_lengths, self_query, self_keyval, self_out, cross_query, cross_keyval, cross_out, ffn_in, ffn_bias_in, ffn_out, ffn_bias_out, slot_weight, norm_gain, norm_bias, cotangent):
    params = tuple((item.astype(jnp.float32) for item in (self_query, self_keyval, self_out, cross_query, cross_keyval, cross_out, ffn_in, ffn_bias_in, ffn_out, ffn_bias_out, slot_weight, norm_gain, norm_bias)))
    positions = jnp.arange(SLOTS, dtype=jnp.int32)
    mem_positions = jnp.arange(MEM, dtype=jnp.int32)

    def per_sequence(totals, items):
        tokens, mem_rows, live_count, mem_count, grad_out = items
        valid = positions < live_count.astype(jnp.int32)
        mem_valid = mem_positions < mem_count.astype(jnp.int32)

        def forward(tokens_in, mem_in, params_in):
            return layer(tokens_in, mem_in, params_in, valid, mem_valid)
        result, pull = jax.vjp(forward, tokens.astype(jnp.float32), mem_rows.astype(jnp.float32), params)
        grad_tokens, grad_mem, grad_params = pull(grad_out.astype(jnp.float32))
        totals = jax.tree.map(jnp.add, totals, grad_params)
        return (totals, (result.astype(jnp.bfloat16), grad_tokens, grad_mem))
    zeros = jax.tree.map(jnp.zeros_like, params)
    totals, (outputs, grad_tokens, grad_mem) = lax.scan(per_sequence, zeros, (decoder_in, memory, seq_lengths, mem_lengths, cotangent))
    return (outputs, grad_tokens, grad_mem, totals[0], totals[1], totals[2], totals[3], totals[4], totals[5], totals[6], totals[7], totals[8], totals[9], totals[10], totals[11], totals[12])
```

```python
import functools
import math

import jax
import jax.numpy as jnp
from jax import lax
from jax.experimental import pallas as pl
from jax.experimental.pallas import tpu as pltpu
from jax.sharding import PartitionSpec as P

HEADS = 8
NORM_EPS = 1e-05
DEAD = -1e30
EXT = 128
DEAD_LANE = 3 * HEADS
BF = jnp.bfloat16
F32 = jnp.float32
VMEM_LIMIT = 60 * 1024 * 1024


def mm(left, right):
    return lax.dot_general(left, right, (((1,), (0,)), ((), ())), preferred_element_type=F32)


def mm2(left, right):
    high = left.astype(BF)
    low = (left - high.astype(F32)).astype(BF)
    return mm(high, right) + mm(low, right)


def mm_t(left, right):
    return lax.dot_general(left, right, (((1,), (1,)), ((), ())), preferred_element_type=F32)


def t_mm(left, right):
    return lax.dot_general(left, right, (((0,), (0,)), ((), ())), preferred_element_type=F32)


def norm_stats(values):
    center = values - jnp.mean(values, axis=-1, keepdims=True)
    inverse = lax.rsqrt(jnp.mean(center * center, axis=-1, keepdims=True) + NORM_EPS)
    return center * inverse, inverse


def norm_back(grad_out, normed, inverse, gain_row):
    scaled = grad_out * gain_row
    grad_in = inverse * (
        scaled
        - jnp.mean(scaled, axis=-1, keepdims=True)
        - normed * jnp.mean(scaled * normed, axis=-1, keepdims=True)
    )
    return (
        grad_in,
        jnp.sum(grad_out * normed, axis=0, keepdims=True),
        jnp.sum(grad_out, axis=0, keepdims=True),
    )


def lanes(width=128):
    return lax.broadcasted_iota(jnp.int32, (1, width), 1)


def stack_pair(block):
    low = lanes() < 64
    zero = jnp.zeros_like(block)
    return jnp.concatenate([jnp.where(low, block, zero), jnp.where(low, zero, block)], axis=0)


def unstack_pair(stacked):
    n = stacked.shape[0] // 2
    return jnp.where(lanes() < 64, stacked[:n], stacked[n:])


def split3(value):
    high = value.astype(BF).astype(F32)
    rest = value - high
    mid = rest.astype(BF).astype(F32)
    return high, mid, (rest - mid).astype(BF).astype(F32)


def place3(table, column, head):
    where = lanes()
    for term, part in enumerate(split3(column)):
        table = jnp.where(where == 3 * head + term, part, table)
    return table


def pair_ext(table, pair):
    where = lanes()
    parts = []
    for head in (2 * pair, 2 * pair + 1):
        keep = ((where >= 3 * head) & (where < 3 * head + 3)) | (where == DEAD_LANE)
        parts.append(jnp.where(keep, table, jnp.zeros_like(table)))
    return jnp.concatenate(parts, axis=0)


def ones_ext(rows, pair):
    where = lanes()
    parts = []
    for head in (2 * pair, 2 * pair + 1):
        one = jnp.where((where >= 3 * head) & (where < 3 * head + 3), 1.0, 0.0)
        parts.append(jnp.broadcast_to(one, (rows, EXT)))
    return jnp.concatenate(parts, axis=0).astype(BF)


def row_delta(grad_low, mixed):
    product = grad_low.astype(F32) * mixed
    low = lanes() < 64
    table = jnp.zeros((mixed.shape[0], EXT), F32)
    for pair in range(HEADS // 2):
        block = product[:, 128 * pair : 128 * pair + 128]
        even = jnp.sum(jnp.where(low, block, 0.0), axis=1, keepdims=True)
        odd = jnp.sum(jnp.where(low, 0.0, block), axis=1, keepdims=True)
        table = place3(table, -even, 2 * pair)
        table = place3(table, -odd, 2 * pair + 1)
    return table.astype(BF)


def pair_slice(pair):
    return pl.ds(pl.multiple_of(pair * 128, 128), 128)


def attend_forward(q_ref, kv_ref, kext_ref, mixed_ref, state, blocks, block):
    n_rows, width = q_ref.shape
    where = lanes()
    ext = jnp.broadcast_to(jnp.where(where == DEAD_LANE, 1.0, 0.0), (2 * n_rows, EXT)).astype(BF)
    kext = kext_ref[...]

    def one_pair(pair, table):
        q2 = jnp.concatenate([stack_pair(q_ref[:, pair_slice(pair)]), ext], axis=1)
        keys = jnp.concatenate([kv_ref[:, pair_slice(pair)], kext], axis=1)
        scores = mm_t(q2, keys)
        top = jnp.max(scores, axis=1, keepdims=True)
        if blocks > 1:
            before = jnp.where(block == 0, DEAD, state[0][pair])
            top = jnp.maximum(top, before)
        powers = jnp.exp(scores - top)
        total = jnp.sum(powers, axis=1, keepdims=True)
        mixed = mm2(powers, kv_ref[:, pair_slice(pair + width // 128)])
        if blocks > 1:
            fade = jnp.exp(before - top)
            total = total + fade * jnp.where(block == 0, 0.0, state[1][pair])
            mixed = mixed + fade * jnp.where(block == 0, 0.0, state[2][pair])
            state[0][pair] = top
            state[1][pair] = total
            state[2][pair] = mixed
        mixed_ref[:, pair_slice(pair)] = unstack_pair(mixed * (1.0 / total))
        lse = -(top + jnp.log(total))
        table = place3(table, lse[:n_rows], 2 * pair)
        return place3(table, lse[n_rows:], 2 * pair + 1)

    start = jnp.broadcast_to(jnp.where(where == DEAD_LANE, 1.0, 0.0), (n_rows, EXT))
    return lax.fori_loop(0, HEADS // 2, one_pair, start, unroll=True).astype(BF)


def attend_query_back(q_ref, qext, do_ref, doext, kv_ref, kext_ref, add_pair):
    width = q_ref.shape[1]
    kext = kext_ref[...]

    def one_pair(pair, carry):
        keys = kv_ref[:, pair_slice(pair)]
        q2 = jnp.concatenate([stack_pair(q_ref[:, pair_slice(pair)]), pair_ext(qext, pair)], axis=1)
        probs = jnp.exp(mm_t(q2, jnp.concatenate([keys, kext], axis=1)))
        do2 = jnp.concatenate(
            [stack_pair(do_ref[:, pair_slice(pair)]), pair_ext(doext, pair)], axis=1
        )
        values = kv_ref[:, pair_slice(pair + width // 128)]
        d_probs = mm_t(do2, jnp.concatenate([values, kext], axis=1))
        d_scores = (probs * d_probs).astype(BF)
        add_pair(pair, unstack_pair(mm(d_scores, keys)))
        return carry

    lax.fori_loop(0, HEADS // 2, one_pair, 0, unroll=True)


def attend_key_back(kv_ref, pay_q_ref, pay_do_ref, add_pair):
    n_keys = kv_ref.shape[0]
    width = kv_ref.shape[1] // 2

    def one_pair(pair, carry):
        ones = ones_ext(n_keys, pair)
        queries = pay_q_ref[:, pair_slice(pair)]
        grads = pay_do_ref[:, pair_slice(pair)]
        k2 = jnp.concatenate([stack_pair(kv_ref[:, pair_slice(pair)]), ones], axis=1)
        probs = jnp.exp(mm_t(k2, jnp.concatenate([queries, pay_q_ref[:, width:]], axis=1)))
        v2 = jnp.concatenate([stack_pair(kv_ref[:, pair_slice(pair + width // 128)]), ones], axis=1)
        d_probs = mm_t(v2, jnp.concatenate([grads, pay_do_ref[:, width:]], axis=1))
        d_scores = (probs * d_probs).astype(BF)
        add_pair(
            pair, unstack_pair(mm(d_scores, queries)), unstack_pair(mm2(probs, grads))
        )
        return carry

    lax.fori_loop(0, HEADS // 2, one_pair, 0, unroll=True)


class Fetch:
    def __init__(self, me, sems):
        self.me, self.sems, self.used = me, sems, 0

    def start(self, slots, source, target):
        copies = []
        for slot, ref in enumerate(slots):
            quarter = jnp.bitwise_xor(self.me, slot)
            copy = pltpu.make_async_copy(source(ref), target(quarter), self.sems.at[self.used])
            self.used += 1
            copy.start()
            copies.append(copy)
        return copies

    def rows(self, slots, first, width, ref, height=128):
        copies = []
        for part in range(height // 128):
            copies += self.start(
                slots,
                lambda s, part=part: s.at[pl.ds(0, 128), pl.ds(first + part * width, width)],
                lambda quarter, part=part: ref.at[
                    pl.ds(pl.multiple_of(quarter * height + part * 128, 128), 128)
                ],
            )
        return copies

    def small(self, slots, ref):
        return self.start(
            slots,
            lambda s: s.at[pl.ds(128, 16), pl.ds(0, 128)],
            lambda quarter: ref.at[:, pl.ds(pl.multiple_of(quarter * 128, 128), 128)],
        )


def wait(copies):
    for copy in copies:
        copy.wait()


def quarter_of(ref, me, slot, width):
    start = pl.multiple_of(jnp.bitwise_xor(me, slot) * width, 128)
    return ref[:, pl.ds(start, width)]


KEPT = (0, 2)
SENT = (1, 3)


def put_blocks(keep_ref, send_ref, first, me, block_of):
    for target, slots in ((keep_ref, KEPT), (send_ref, SENT)):
        for place, slot in enumerate(slots):
            block = block_of(slot).astype(target.dtype)
            rows = block.shape[0]
            for part in range(block.shape[1] // 512):
                target[place, first + part * rows : first + (part + 1) * rows, :] = block[
                    :, 512 * part : 512 * (part + 1)
                ]


def small_row(small_ref, row):
    return small_ref[row : row + 1, :].astype(F32)


GAIN, BIAS = 5, 8


def self_forward_kernel(blocks, scal, x_ref, tok_ref, kext_ref, *refs):
    g1, g2 = refs[0:4], refs[4:8]
    kv_ref, pay_ref, mixed_ref, first_ref, cq_ref = refs[8:13]
    wq, wkv, wo, wc, small, q_ref, m_st, l_st, a_st, sems = refs[13:]
    me = scal[0]
    block = pl.program_id(0)
    width = x_ref.shape[1]

    def fetches(op):
        fetch = Fetch(me, sems)
        return (
            fetch.rows(g1, 0, width, wq),
            fetch.rows(g1, width, 2 * width, wkv),
            fetch.small(g1, small),
            fetch.rows(g2, 0, width, wo),
            fetch.rows(g2, width, width, wc),
        )

    def begin():
        c_q, c_kv, c_small, c_o, c_c = fetches(None)
        wait(c_q)
        q_ref[...] = (mm(x_ref[...], wq[...]).astype(BF).astype(F32) * 0.125).astype(BF)
        wait(c_kv)
        wait(c_small)
        wait(c_o)
        wait(c_c)

    if blocks > 1:
        pl.when(block == 0)(begin)
    else:
        begin()
    kv_ref[...] = mm(tok_ref[...], wkv[...]).astype(BF)
    table = attend_forward(
        q_ref, kv_ref, kext_ref, mixed_ref, (m_st, l_st, a_st), blocks, block
    )

    def finish():
        pay_ref[:, :width] = q_ref[...]
        pay_ref[:, width:] = table
        first = x_ref[...].astype(F32) + mm(mixed_ref[...].astype(BF), wo[...])
        first_ref[...] = first
        normed, _ = norm_stats(first)
        hidden = normed * small_row(small, GAIN) + small_row(small, BIAS)
        cq = mm(hidden.astype(BF), wc[...]).astype(BF)
        cq_ref[...] = (cq.astype(F32) * 0.125).astype(BF)

    if blocks > 1:
        pl.when(block == blocks - 1)(finish)
    else:
        finish()


def gelu_parts(value):
    coef = math.sqrt(2.0 / math.pi)
    square = value * value
    inner = coef * (value + 0.044715 * value * square)
    bend = jnp.tanh(inner)
    half = 0.5 * (1.0 + bend)
    slope = half + 0.5 * value * (1.0 - bend * bend) * coef * (1.0 + 3 * 0.044715 * square)
    return value * half, slope


def middle_kernel(scal, cq_ref, mem_ref, kext_ref, first_ref, cot_ref, prev_ref, *refs):
    g1, g2, g3 = refs[0:4], refs[4:8], refs[8:12]
    kv_ref, pay_q_ref, pay_do_ref, masked_ref, g_ref, second_ref, sums_ref, keep_ref, send_ref = (
        refs[12:21]
    )
    wkv, wo, w1, w2, ws, small, mixed, low, hid, act, sems = refs[21:]
    me, live, base = scal[0], scal[1], scal[2]
    n_rows, width = cq_ref.shape
    hidden_units = w1.shape[1]
    fetch = Fetch(me, sems)
    c_kv = fetch.rows(g2, 2 * width, 2 * width, wkv)
    c_small = fetch.small(g1, small)
    c_o = fetch.rows(g2, 4 * width, width, wo)
    c_s = fetch.rows(g3, 2 * hidden_units, width, ws, 256)
    c_1 = fetch.rows(g3, 0, hidden_units, w1)
    c_2 = fetch.rows(g3, hidden_units, width, w2, hidden_units // 4)
    wait(c_kv)
    wait(c_small)
    kv_ref[...] = mm(mem_ref[...], wkv[...]).astype(BF)
    table = attend_forward(cq_ref, kv_ref, kext_ref, mixed, None, 1, 0)
    pay_q_ref[:, :width] = cq_ref[...]
    pay_q_ref[:, width:] = table
    low[...] = mixed[...].astype(BF)
    wait(c_o)
    normed, _ = norm_stats(first_ref[...])
    hidden_one = normed * small_row(small, GAIN) + small_row(small, BIAS)
    second = hidden_one + mm(low[...], wo[...])
    normed_two, inverse_two = norm_stats(second)
    hidden_two = normed_two * small_row(small, GAIN + 1) + small_row(small, BIAS + 1)
    hid[...] = hidden_two.astype(BF)
    bias_in = jnp.concatenate(
        [
            small[r : r + 1, 128 * j : 128 * j + 128].astype(F32)
            for j in range(4)
            for r in range(4)
        ],
        axis=1,
    )
    wait(c_1)
    preact = mm(hid[...], w1[...]) + bias_in
    active, slope = gelu_parts(preact)
    act[...] = active.astype(BF)
    wait(c_2)
    third = hidden_two + mm(act[...], w2[...]) + small_row(small, 4)
    normed_three, inverse_three = norm_stats(third)
    hidden_three = normed_three * small_row(small, GAIN + 2) + small_row(small, BIAS + 2)
    places = base + lax.broadcasted_iota(jnp.int32, (n_rows, 1), 0)
    valid = places < live
    masked_ref[...] = jnp.where(valid, hidden_three, 0.0).astype(BF)

    grads = jnp.where(valid, cot_ref[...].astype(F32), 0.0).astype(BF)
    g_ref[...] = grads
    wait(c_s)
    d_own = mm_t(grads, ws[:width, :])
    before = jnp.where(base - 1 < live, prev_ref[...].astype(F32), 0.0).astype(BF)
    shifted = jnp.concatenate([before[0:1], grads[:-1].astype(BF)], axis=0)
    d_next = mm_t(shifted, ws[width:, :])
    d_three = jnp.where(valid, d_own + d_next, 0.0)
    d_third, gain_three, bias_three = norm_back(
        d_three, normed_three, inverse_three, small_row(small, GAIN + 2)
    )
    e_third = d_third.astype(BF)
    d_pre = (mm_t(e_third, w2[...]) * slope).astype(BF)
    d_two = d_third + mm_t(d_pre, w1[...])
    d_second, gain_two, bias_two = norm_back(
        d_two, normed_two, inverse_two, small_row(small, GAIN + 1)
    )
    second_ref[...] = d_second
    e_second = d_second.astype(BF)
    d_cross = mm_t(e_second, wo[...]).astype(BF)
    pay_do_ref[:, :width] = d_cross
    pay_do_ref[:, width:] = row_delta(d_cross, mixed[...])
    sums_ref[...] = jnp.zeros_like(sums_ref)
    sums_ref[0:1, :] = jnp.sum(d_pre.astype(F32), axis=0, keepdims=True)
    sums_ref[1:2, :width] = jnp.sum(e_third.astype(F32), axis=0, keepdims=True)
    sums_ref[3:4, :width] = gain_two
    sums_ref[4:5, :width] = gain_three
    sums_ref[6:7, :width] = bias_two
    sums_ref[7:8, :width] = bias_three
    put_blocks(keep_ref, send_ref, 0, me, lambda s: t_mm(quarter_of(act, me, s, hidden_units // 4), e_third))
    put_blocks(keep_ref, send_ref, 512, me, lambda s: t_mm(quarter_of(hid, me, s, 128), d_pre))
    put_blocks(keep_ref, send_ref, 1024, me, lambda s: t_mm(quarter_of(low, me, s, 128), e_second))


def cross_query_kernel(
    scal, pay_q_ref, pay_do_ref, kv_ref, kext_ref, first_ref, second_ref, mixed_ref, sums_ref, *refs
):
    g1, g2 = refs[0:4], refs[4:8]
    d_first_ref, pay_ref, keep_ref, send_ref = refs[8:12]
    wo, wc, small, dq, low, hid, sums, sems = refs[12:]
    me = scal[0]
    width = first_ref.shape[1]
    fetch = Fetch(me, sems)
    c_c = fetch.rows(g2, width, width, wc)
    c_small = fetch.small(g1, small)
    c_o = fetch.rows(g2, 0, width, wo)

    def add_pair(pair, value):
        dq[:, pair_slice(pair)] = (value * 0.125).astype(BF)

    attend_query_back(
        pay_q_ref.at[:, pl.ds(0, width)],
        pay_q_ref[:, width:],
        pay_do_ref.at[:, pl.ds(0, width)],
        pay_do_ref[:, width:],
        kv_ref,
        kext_ref,
        add_pair,
    )
    wait(c_c)
    wait(c_small)
    normed, inverse = norm_stats(first_ref[...])
    hid[...] = (normed * small_row(small, GAIN) + small_row(small, BIAS)).astype(BF)
    low[...] = mixed_ref[...].astype(BF)
    d_one = second_ref[...] + mm_t(dq[...], wc[...])
    d_first, gain_one, bias_one = norm_back(d_one, normed, inverse, small_row(small, GAIN))
    d_first_ref[...] = d_first
    e_first = d_first.astype(BF)
    wait(c_o)
    d_self = mm_t(e_first, wo[...]).astype(BF)
    pay_ref[:, :width] = d_self
    pay_ref[:, width:] = row_delta(d_self, mixed_ref[...])
    put_blocks(keep_ref, send_ref, 0, me, lambda s: t_mm(quarter_of(low, me, s, 128), e_first))
    put_blocks(keep_ref, send_ref, 128, me, lambda s: t_mm(quarter_of(hid, me, s, 128), dq[...]))
    sums[...] = sums_ref[...]
    sums[2:3, :width] = gain_one
    sums[5:6, :width] = bias_one
    quarter = sums_ref.shape[1] // 4

    def small_block(slot):
        top = quarter_of(sums, me, slot, quarter)
        rest = quarter_of(sums, me, slot, 128)
        rest = jnp.concatenate([rest, jnp.zeros((8, quarter - 128), F32)], axis=1)
        row = lax.broadcasted_iota(jnp.int32, (8, 1), 0)
        return jnp.concatenate(
            [jnp.where(row == 0, top, rest), jnp.zeros((120, quarter), F32)], axis=0
        )

    put_blocks(keep_ref, send_ref, 256, me, small_block)


def slots_kernel(scal, masked_ref, next_ref, g_ref, *refs):
    g3 = refs[0:4]
    slots_ref, keep_ref, send_ref = refs[4:7]
    ws, paired, sems = refs[7:]
    me, live, base = scal[0], scal[1], scal[2]
    n_rows, width = masked_ref.shape
    hidden_units = 4 * 512
    fetch = Fetch(me, sems)
    c_s = fetch.rows(g3, 2 * hidden_units, width, ws, 256)
    masked = masked_ref[...]
    paired[:, :width] = masked
    paired[:, width:] = jnp.concatenate([masked[1:], next_ref[0:1, :]], axis=0)
    places = base + lax.broadcasted_iota(jnp.int32, (n_rows, 1), 0)
    put_blocks(keep_ref, send_ref, 0, me, lambda s: t_mm(quarter_of(paired, me, s, 256), g_ref[...]))
    wait(c_s)
    slots_ref[...] = jnp.where(places < live, mm(paired[...], ws[...]), 0.0).astype(BF)


def cross_key_kernel(blocks, scal, mem_ref, pay_q_ref, pay_do_ref, *refs):
    g2 = refs[0:4]
    grad_ref, keep_ref, send_ref = refs[4:7]
    wkv, kv, acc, low, sems = refs[7:]
    me, live, base = scal[0], scal[3], scal[4]
    block = pl.program_id(0)
    n_rows, width = mem_ref.shape
    fetch = Fetch(me, sems)

    def begin():
        wait(fetch.rows(g2, 2 * width, 2 * width, wkv))
        kv[...] = mm(mem_ref[...], wkv[...]).astype(BF)

    key_back(blocks, block, begin, kv, acc, low, pay_q_ref, pay_do_ref, live, base)

    def finish():
        grad_ref[...] = mm_t(low[...], wkv[...])
        put_blocks(
            keep_ref, send_ref, 0, me, lambda s: t_mm(quarter_of(mem_ref, me, s, 128), low[...])
        )

    if blocks > 1:
        pl.when(block == blocks - 1)(finish)
    else:
        finish()


def key_back(blocks, block, begin, kv, acc, low, pay_q_ref, pay_do_ref, live, base):
    n_rows = kv.shape[0]
    width = kv.shape[1] // 2
    if blocks > 1:
        pl.when(block == 0)(begin)
    else:
        begin()

    def add_pair(pair, d_key, d_value):
        at_key, at_value = pair_slice(pair), pair_slice(pair + width // 128)
        if blocks > 1:
            d_key = d_key + jnp.where(block == 0, 0.0, acc[:, at_key])
            d_value = d_value + jnp.where(block == 0, 0.0, acc[:, at_value])
            acc[:, at_key] = d_key
            acc[:, at_value] = d_value
        usable = base + lax.broadcasted_iota(jnp.int32, (n_rows, 1), 0) < live
        low[:, at_key] = jnp.where(usable, d_key, 0.0).astype(BF)
        low[:, at_value] = jnp.where(usable, d_value, 0.0).astype(BF)

    attend_key_back(kv, pay_q_ref, pay_do_ref, add_pair)


def self_query_kernel(
    blocks, scal, pay_q_ref, pay_do_ref, kv_ref, kext_ref, x_ref, d_first_ref, *refs
):
    g1 = refs[0:4]
    part_ref, keep_ref, send_ref = refs[4:7]
    wq, acc, sems = refs[7:]
    me = scal[0]
    block = pl.program_id(0)
    width = x_ref.shape[1]

    def begin():
        wait(Fetch(me, sems).rows(g1, 0, width, wq))

    if blocks > 1:
        pl.when(block == 0)(begin)
    else:
        begin()

    def add_pair(pair, value):
        at = pair_slice(pair)
        if blocks > 1:
            value = value + jnp.where(block == 0, 0.0, acc[:, at])
        acc[:, at] = value

    attend_query_back(
        pay_q_ref.at[:, pl.ds(0, width)],
        pay_q_ref[:, width:],
        pay_do_ref.at[:, pl.ds(0, width)],
        pay_do_ref[:, width:],
        kv_ref,
        kext_ref,
        add_pair,
    )

    def finish():
        dq = (acc[...] * 0.125).astype(BF)
        part_ref[...] = d_first_ref[...] + mm_t(dq, wq[...])
        put_blocks(keep_ref, send_ref, 0, me, lambda s: t_mm(quarter_of(x_ref, me, s, 128), dq))

    if blocks > 1:
        pl.when(block == blocks - 1)(finish)
    else:
        finish()


def self_key_kernel(blocks, scal, x_ref, pay_q_ref, pay_do_ref, part_ref, *refs):
    g1 = refs[0:4]
    grad_ref, keep_ref, send_ref = refs[4:7]
    wkv, kv, acc, low, sems = refs[7:]
    me, live, base = scal[0], scal[1], scal[2]
    block = pl.program_id(0)
    n_rows, width = x_ref.shape
    fetch = Fetch(me, sems)

    def begin():
        wait(fetch.rows(g1, width, 2 * width, wkv))
        kv[...] = mm(x_ref[...], wkv[...]).astype(BF)

    key_back(blocks, block, begin, kv, acc, low, pay_q_ref, pay_do_ref, live, base)

    def finish():
        grad_ref[...] = part_ref[...] + mm_t(low[...], wkv[...])
        put_blocks(
            keep_ref, send_ref, 0, me, lambda s: t_mm(quarter_of(x_ref, me, s, 128), low[...])
        )

    if blocks > 1:
        pl.when(block == blocks - 1)(finish)
    else:
        finish()


def whole(array, buffers=None):
    rank = len(array.shape)
    return pl.BlockSpec(tuple(array.shape), lambda *_: (0,) * rank)


def by_rows(array, rows):
    return pl.BlockSpec((rows, array.shape[1]), lambda i: (i, 0))


ANY = pl.BlockSpec(memory_space=pl.ANY)
SMEM = pl.BlockSpec(memory_space=pltpu.SMEM)


def shape(dims, dtype):
    return jax.ShapeDtypeStruct(dims, dtype)


def call(kernel, name, grid, args, specs, outs, out_specs, scratch, copies, flops, moved):
    return pl.pallas_call(
        kernel,
        name=name,
        grid=(grid,),
        in_specs=specs,
        out_specs=out_specs,
        out_shape=outs,
        scratch_shapes=[*scratch, pltpu.SemaphoreType.DMA((copies,))],
        compiler_params=pltpu.CompilerParams(
            vmem_limit_bytes=VMEM_LIMIT, dimension_semantics=("arbitrary",)
        ),
        cost_estimate=pl.CostEstimate(flops=flops, bytes_accessed=moved, transcendentals=0),
    )(*args)


def vm(dims, dtype):
    return pltpu.VMEM(dims, dtype)


def grad_outs(rows):
    return (shape((2, rows, 512), F32), shape((2, rows, 512), BF))


def permute(value, axis, target):
    n = lax.axis_size(axis)
    pairs = [(i, target(i)) for i in range(n) if 0 <= target(i) < n]
    return lax.ppermute(value, axis, pairs)


def flip(value, axis, bits):
    return permute(value, axis, lambda i: i ^ bits)


def gather_ctx(value):
    if lax.axis_size("ctx") != 8:
        return lax.all_gather(value, "ctx", axis=0, tiled=False)
    line = [value, flip(value, "ctx", 2), flip(value, "ctx", 4), flip(value, "ctx", 6)]
    other = [flip(item, "ctx", 1) for item in line]
    return jnp.stack([line[0], other[0], line[1], other[1], line[2], other[2], line[3], other[3]])


def gather_wsh(group):
    own = group
    across = flip(own, "wsh", 2)
    return (own, flip(own, "wsh", 1), across, flip(across, "wsh", 1))


def reduce_wsh(keep, send):
    got = flip(send, "wsh", 1).astype(F32)
    half = keep + got
    return half[0] + flip(half[1].astype(BF), "wsh", 2).astype(F32)


def reduce_ctx(value):
    return lax.psum(value.astype(BF), "ctx").astype(F32)


def shards(
    decoder_in,
    memory,
    seq_lengths,
    mem_lengths,
    self_query,
    self_keyval,
    self_out,
    cross_query,
    cross_keyval,
    cross_out,
    ffn_in,
    ffn_bias_in,
    ffn_out,
    ffn_bias_out,
    slot_weight,
    norm_gain,
    norm_bias,
    cotangent,
):
    tokens, mem_rows, cot = decoder_in[0], memory[0], cotangent[0]
    n_rows, width = tokens.shape
    n_mem = mem_rows.shape[0]
    hidden_units = ffn_in.shape[1]
    ctx = lax.axis_size("ctx")
    here, me = lax.axis_index("ctx"), lax.axis_index("wsh")
    n_keys, all_mem = ctx * n_rows, ctx * n_mem
    blocks = max(1, n_keys // 1536)
    step = n_keys // blocks

    def blocks_of(array, count):
        tall = array.shape[0] // count
        return [array[i * tall : (i + 1) * tall] for i in range(count)]

    small = jnp.concatenate(
        [ffn_bias_in.reshape(4, 128), ffn_bias_out.reshape(1, 128), norm_gain, norm_bias,
         jnp.zeros((5, 128), BF)],
        axis=0,
    )
    small = jnp.concatenate([small, jnp.zeros((16, 3 * width - 128), BF)], axis=1)
    group1 = jnp.concatenate([jnp.concatenate([self_query, self_keyval], axis=1), small], axis=0)
    group2 = jnp.concatenate([self_out, cross_query, cross_keyval, cross_out], axis=1)
    group3 = jnp.concatenate(
        [ffn_in, *blocks_of(ffn_out, hidden_units // 512), *blocks_of(slot_weight, 2)], axis=1
    )
    g1 = gather_wsh(group1)
    toks = gather_ctx(tokens).reshape(n_keys, width)
    g2 = gather_wsh(group2)
    mems = gather_ctx(mem_rows).reshape(all_mem, width)
    g3 = gather_wsh(group3)
    prev_cot = permute(cot[-16:], "ctx", lambda i: i + 1)[15:16]

    live, mem_live = seq_lengths[0], mem_lengths[0]
    scal = jnp.stack(
        [me, live, here * n_rows, mem_live, here * n_mem, 0, 0, 0]
    ).astype(jnp.int32)

    def key_ext(rows, limit):
        slot = lax.broadcasted_iota(jnp.int32, (ctx * rows, EXT), 0)
        lane = lax.broadcasted_iota(jnp.int32, (ctx * rows, EXT), 1)
        device = slot // rows
        if ctx == 8:
            device = jnp.bitwise_xor(device, here)
        dead = device * rows + slot % rows >= limit
        value = jnp.where(lane < DEAD_LANE, 1.0, 0.0)
        return jnp.where((lane == DEAD_LANE) & dead, DEAD, value).astype(BF)

    kext = key_ext(n_rows, live)
    mext = key_ext(n_mem, mem_live)

    pair_rows = (HEADS // 2, 2 * n_rows)
    kv, pay_q, self_mixed, first_sum, cqs = call(
        functools.partial(self_forward_kernel, blocks), "self_forward", blocks,
        (scal, tokens, toks, kext, *g1, *g2),
        [SMEM, whole(tokens), by_rows(toks, step), by_rows(kext, step)] + [ANY] * 8,
        (shape((n_keys, 2 * width), BF), shape((n_rows, width + EXT), BF),
         shape((n_rows, width), F32), shape((n_rows, width), F32), shape((n_rows, width), BF)),
        [pl.BlockSpec((step, 2 * width), lambda i: (i, 0))]
        + [pl.BlockSpec((n_rows, w), lambda i: (0, 0)) for w in (width + EXT, width, width, width)],
        [vm((width, width), BF), vm((width, 2 * width), BF), vm((width, width), BF),
         vm((width, width), BF), vm((16, width), BF), vm((n_rows, width), BF)]
        + ([vm((*pair_rows, 1), F32), vm((*pair_rows, 1), F32), vm((*pair_rows, 128), F32)]
           if blocks > 1 else [vm((8, 128), F32)] * 3),
        20, 4 * n_rows * n_keys * width, 8 * 2**20,
    )
    memkv, pay_cq, pay_dc, masked, grads, d_second, sums, keep_a, send_a = call(
        middle_kernel, "middle", 1,
        (scal, cqs, mems, mext, first_sum, cot, prev_cot, *g1, *g2, *g3),
        [SMEM] + [whole(a) for a in (cqs, mems, mext, first_sum, cot, prev_cot)] + [ANY] * 12,
        (shape((all_mem, 2 * width), BF), shape((n_rows, width + EXT), BF),
         shape((n_rows, width + EXT), BF), shape((n_rows, width), BF), shape((n_rows, width), BF),
         shape((n_rows, width), F32), shape((8, hidden_units), F32), *grad_outs(1152)),
        [pl.BlockSpec(dims, lambda i, r=len(dims): (0,) * r) for dims in (
            (all_mem, 2 * width), (n_rows, width + EXT), (n_rows, width + EXT), (n_rows, width),
            (n_rows, width), (n_rows, width), (8, hidden_units), (2, 1152, 512), (2, 1152, 512))],
        [vm((width, 2 * width), BF), vm((width, width), BF), vm((width, hidden_units), BF),
         vm((hidden_units, width), BF), vm((2 * width, width), BF), vm((16, width), BF),
         vm((n_rows, width), F32), vm((n_rows, width), BF), vm((n_rows, width), BF),
         vm((n_rows, hidden_units), BF)],
        48, 8 * n_rows * all_mem * width, 30 * 2**20,
    )
    next_row = permute(masked[:16], "ctx", lambda i: i - 1)[:1]
    d_first, pay_ds, keep_b, send_b = call(
        cross_query_kernel, "cross_query", 1,
        (scal, pay_cq, pay_dc, memkv, mext, first_sum, d_second, self_mixed, sums, *g1, *g2),
        [SMEM] + [whole(a) for a in (pay_cq, pay_dc, memkv, mext, first_sum, d_second, self_mixed, sums)]
        + [ANY] * 8,
        (shape((n_rows, width), F32), shape((n_rows, width + EXT), BF), *grad_outs(384)),
        [pl.BlockSpec(dims, lambda i, r=len(dims): (0,) * r) for dims in (
            (n_rows, width), (n_rows, width + EXT), (2, 384, 512), (2, 384, 512))],
        [vm((width, width), BF), vm((width, width), BF), vm((16, width), BF),
         vm((n_rows, width), BF), vm((n_rows, width), BF), vm((n_rows, width), BF),
         vm((8, hidden_units), F32)],
        12, 6 * n_rows * all_mem * width, 12 * 2**20,
    )
    slots, keep_s, send_s = call(
        slots_kernel, "slots", 1,
        (scal, masked, next_row, grads, *g3),
        [SMEM, whole(masked), whole(next_row), whole(grads)] + [ANY] * 4,
        (shape((n_rows, width), BF), *grad_outs(256)),
        [pl.BlockSpec(dims, lambda i, r=len(dims): (0,) * r) for dims in (
            (n_rows, width), (2, 256, 512), (2, 256, 512))],
        [vm((2 * width, width), BF), vm((n_rows, 2 * width), BF)],
        8, 4 * n_rows * width * 2 * width, 4 * 2**20,
    )
    all_q = gather_ctx(pay_q).reshape(n_keys, width + EXT)
    all_cq = gather_ctx(pay_cq).reshape(n_keys, width + EXT)
    all_dc = gather_ctx(pay_dc).reshape(n_keys, width + EXT)
    all_ds = gather_ctx(pay_ds).reshape(n_keys, width + EXT)
    pay_block = pl.BlockSpec((step, width + EXT), lambda i: (i, 0))
    part, keep_q, send_q = call(
        functools.partial(self_query_kernel, blocks), "self_query", blocks,
        (scal, pay_q, pay_ds, kv, kext, tokens, d_first, *g1),
        [SMEM, whole(pay_q), whole(pay_ds), by_rows(kv, step), by_rows(kext, step), whole(tokens),
         whole(d_first)] + [ANY] * 4,
        (shape((n_rows, width), F32), *grad_outs(128)),
        [pl.BlockSpec(dims, lambda i, r=len(dims): (0,) * r) for dims in (
            (n_rows, width), (2, 128, 512), (2, 128, 512))],
        [vm((width, width), BF), vm((n_rows, width), F32)],
        4, 6 * n_rows * n_keys * width, 8 * 2**20,
    )
    grad_mem, keep_m, send_m = call(
        functools.partial(cross_key_kernel, blocks), "cross_key", blocks,
        (scal, mem_rows, all_cq, all_dc, *g2),
        [SMEM, whole(mem_rows), pay_block, pay_block] + [ANY] * 4,
        (shape((n_mem, width), F32), *grad_outs(256)),
        [pl.BlockSpec(dims, lambda i, r=len(dims): (0,) * r) for dims in (
            (n_mem, width), (2, 256, 512), (2, 256, 512))],
        [vm((width, 2 * width), BF), vm((n_mem, 2 * width), BF),
         vm((n_mem, 2 * width) if blocks > 1 else (8, 128), F32), vm((n_mem, 2 * width), BF)],
        4, 8 * n_mem * n_keys * width, 8 * 2**20,
    )
    grad_input, keep_k, send_k = call(
        functools.partial(self_key_kernel, blocks), "self_key", blocks,
        (scal, tokens, all_q, all_ds, part, *g1),
        [SMEM, whole(tokens), pay_block, pay_block, whole(part)] + [ANY] * 4,
        (shape((n_rows, width), F32), *grad_outs(256)),
        [pl.BlockSpec(dims, lambda i, r=len(dims): (0,) * r) for dims in (
            (n_rows, width), (2, 256, 512), (2, 256, 512))],
        [vm((width, 2 * width), BF), vm((n_rows, 2 * width), BF),
         vm((n_rows, 2 * width) if blocks > 1 else (8, 128), F32), vm((n_rows, 2 * width), BF)],
        4, 8 * n_rows * n_keys * width, 8 * 2**20,
    )

    def total(keeps, sends):
        keep = jnp.concatenate(keeps, axis=1) if len(keeps) > 1 else keeps[0]
        send = jnp.concatenate(sends, axis=1) if len(sends) > 1 else sends[0]
        return reduce_ctx(reduce_wsh(keep, send))

    sum_a = total([keep_a], [send_a])
    sum_b = total([keep_b, keep_s, keep_m], [send_b, send_s, send_m])
    sum_d = total([keep_q, keep_k], [send_q, send_k])

    def wide(array, first, count):
        return jnp.concatenate(
            [array[first + 128 * i : first + 128 * (i + 1)] for i in range(count)], axis=1
        )

    g_second, g_first, g_cout = sum_a[:512], wide(sum_a, 512, hidden_units // 512), sum_a[1024:]
    g_out, g_cq, tiny = sum_b[:128], sum_b[128:256], sum_b[256:264]
    g_slot, g_ckv = sum_b[384:640], wide(sum_b, 640, 2)
    g_q, g_kv = sum_d[:128], wide(sum_d, 128, 2)
    return (
        slots[None],
        grad_input[None],
        grad_mem[None],
        g_q,
        g_kv,
        g_out,
        g_cq,
        g_ckv,
        g_cout,
        g_first,
        tiny[0],
        g_second,
        tiny[1, :128],
        g_slot,
        tiny[2:5, :128],
        tiny[5:8, :128],
    )


def solution(mesh):
    rows, split = P("wsh", "ctx", None), P("wsh", None)
    line, side = P("wsh"), P(None, "wsh")
    in_specs = (
        rows, rows, line, line, split, split, split, split, split, split, split, line, split, line,
        split, side, side, rows,
    )
    out_specs = (
        rows, rows, rows, split, split, split, split, split, split, split, line, split, line, split,
        side, side,
    )
    return jax.shard_map(shards, mesh=mesh, in_specs=in_specs, out_specs=out_specs, check_vma=False)
```

```python
import functools
import math

import jax
import jax.numpy as jnp
from jax import lax
from jax.experimental import pallas as pl
from jax.experimental.pallas import tpu as pltpu
from jax.sharding import PartitionSpec as P

HEADS = 8
NORM_EPS = 1e-05
DEAD = -1e30
EXT = 128
DEAD_LANE = 3 * HEADS
LSE_LANE = 32
ORDER = (0, 2, 4, 6, 1, 3, 5, 7)
BF = jnp.bfloat16
F32 = jnp.float32
COST = 10**9
VMEM_LIMIT = 28 * 1024 * 1024


def mm(left, right):
    return lax.dot_general(left, right, (((1,), (0,)), ((), ())), preferred_element_type=F32)


def mm2(left, right):
    high = left.astype(BF)
    low = (left - high.astype(F32)).astype(BF)
    return mm(high, right) + mm(low, right)


def mm_t(left, right):
    return lax.dot_general(left, right, (((1,), (1,)), ((), ())), preferred_element_type=F32)


def t_mm(left, right):
    return lax.dot_general(left, right, (((0,), (0,)), ((), ())), preferred_element_type=F32)


def norm_stats(values):
    center = values - jnp.mean(values, axis=-1, keepdims=True)
    inverse = lax.rsqrt(jnp.mean(center * center, axis=-1, keepdims=True) + NORM_EPS)
    return center * inverse, inverse


def norm_back(grad_out, normed, inverse, gain_row):
    scaled = grad_out * gain_row
    grad_in = inverse * (
        scaled
        - jnp.mean(scaled, axis=-1, keepdims=True)
        - normed * jnp.mean(scaled * normed, axis=-1, keepdims=True)
    )
    return (
        grad_in,
        jnp.sum(grad_out * normed, axis=0, keepdims=True),
        jnp.sum(grad_out, axis=0, keepdims=True),
    )


def lanes(width=128):
    return lax.broadcasted_iota(jnp.int32, (1, width), 1)


def stack_pair(block):
    low = lanes() < 64
    zero = jnp.zeros_like(block)
    return jnp.concatenate([jnp.where(low, block, zero), jnp.where(low, zero, block)], axis=0)


def unstack_pair(stacked):
    n = stacked.shape[0] // 2
    return jnp.where(lanes() < 64, stacked[:n], stacked[n:])


def split3(value):
    high = value.astype(BF).astype(F32)
    rest = value - high
    mid = rest.astype(BF).astype(F32)
    return high, mid, (rest - mid).astype(BF).astype(F32)


def place3(table, column, lane):
    where = lanes()
    for term, part in enumerate(split3(column)):
        table = jnp.where(where == lane + term, part, table)
    return table


def pair_ext(table, pair, offset):
    where = lanes()
    other = jnp.where(where == DEAD_LANE, 1.0 if offset else 0.0, 0.0).astype(table.dtype)
    parts = []
    for head in (2 * pair, 2 * pair + 1):
        first = offset + 3 * head
        parts.append(jnp.where((where >= first) & (where < first + 3), table, other))
    return jnp.concatenate(parts, axis=0)


def ones_ext(rows, pair, offset):
    where = lanes()
    parts = []
    for head in (2 * pair, 2 * pair + 1):
        first = offset + 3 * head
        one = jnp.where((where >= first) & (where < first + 3), 1.0, 0.0)
        parts.append(jnp.broadcast_to(one, (rows, EXT)))
    return jnp.concatenate(parts, axis=0).astype(BF)


def add_delta(table, grad_low, mixed):
    product = grad_low.astype(F32) * mixed
    low = lanes() < 64
    table = table.astype(F32)
    for pair in range(HEADS // 2):
        block = product[:, 128 * pair : 128 * pair + 128]
        even = jnp.sum(jnp.where(low, block, 0.0), axis=1, keepdims=True)
        odd = jnp.sum(jnp.where(low, 0.0, block), axis=1, keepdims=True)
        table = place3(table, -even, 6 * pair)
        table = place3(table, -odd, 6 * pair + 3)
    return table.astype(BF)


def fill_ext(ext_ref, first, rows, here, limit, order):
    where = lanes()
    base = jnp.where(where == DEAD_LANE, 0.0, 1.0)
    for i in range(ext_ref.shape[0] // rows):
        device = jnp.bitwise_xor(here, order[i]) if order else first + i
        place = device * rows + lax.broadcasted_iota(jnp.int32, (rows, 1), 0)
        dead = (where == DEAD_LANE) & (place >= limit)
        ext_ref[i * rows : (i + 1) * rows, :] = jnp.where(dead, DEAD, base).astype(BF)


def pair_slice(pair):
    return pl.ds(pl.multiple_of(pair * 128, 128), 128)


def attend_forward(q_ref, kv_ref, kext_ref, mixed_ref, state, blocks, block):
    n_rows, width = q_ref.shape
    where = lanes()
    ext = jnp.broadcast_to(jnp.where(where == DEAD_LANE, 1.0, 0.0), (2 * n_rows, EXT)).astype(BF)
    kext = kext_ref[...]

    def one_pair(pair, table):
        q2 = jnp.concatenate([stack_pair(q_ref[:, pair_slice(pair)]), ext], axis=1)
        keys = jnp.concatenate([kv_ref[:, pair_slice(pair)], kext], axis=1)
        scores = mm_t(q2, keys)
        top = jnp.max(scores, axis=1, keepdims=True)
        if blocks > 1:
            before = jnp.where(block == 0, DEAD, state[0][pair])
            top = jnp.maximum(top, before)
        powers = jnp.exp(scores - top)
        total = jnp.sum(powers, axis=1, keepdims=True)
        mixed = mm2(powers, kv_ref[:, pair_slice(pair + width // 128)])
        if blocks > 1:
            fade = jnp.exp(before - top)
            total = total + fade * jnp.where(block == 0, 0.0, state[1][pair])
            mixed = mixed + fade * jnp.where(block == 0, 0.0, state[2][pair])
            state[0][pair] = top
            state[1][pair] = total
            state[2][pair] = mixed
        mixed_ref[:, pair_slice(pair)] = unstack_pair(mixed * (1.0 / total))
        lse = -(top + jnp.log(total))
        table = place3(table, lse[:n_rows], LSE_LANE + 6 * pair)
        return place3(table, lse[n_rows:], LSE_LANE + 6 * pair + 3)

    start = jnp.zeros((n_rows, EXT), F32)
    return lax.fori_loop(0, HEADS // 2, one_pair, start, unroll=True).astype(BF)


def attend_query_back(q_ref, pay_ref, kv_ref, kext_ref, add_pair):
    width = q_ref.shape[1]
    kext = kext_ref[...]
    ext = pay_ref[:, width:]

    def one_pair(pair, carry):
        keys = kv_ref[:, pair_slice(pair)]
        q2 = jnp.concatenate(
            [stack_pair(q_ref[:, pair_slice(pair)]), pair_ext(ext, pair, LSE_LANE)], axis=1
        )
        probs = jnp.exp(mm_t(q2, jnp.concatenate([keys, kext], axis=1)))
        do2 = jnp.concatenate(
            [stack_pair(pay_ref[:, pair_slice(pair)]), pair_ext(ext, pair, 0)], axis=1
        )
        values = kv_ref[:, pair_slice(pair + width // 128)]
        d_probs = mm_t(do2, jnp.concatenate([values, kext], axis=1))
        d_scores = (probs * d_probs).astype(BF)
        add_pair(pair, unstack_pair(mm(d_scores, keys)))
        return carry

    lax.fori_loop(0, HEADS // 2, one_pair, 0, unroll=True)


def attend_key_back(kv_ref, q_ref, pay_ref, add_pair):
    n_keys = kv_ref.shape[0]
    width = kv_ref.shape[1] // 2
    ext = pay_ref[:, width:]

    def one_pair(pair, carry):
        queries = q_ref[:, pair_slice(pair)]
        grads = pay_ref[:, pair_slice(pair)]
        k2 = jnp.concatenate(
            [stack_pair(kv_ref[:, pair_slice(pair)]), ones_ext(n_keys, pair, LSE_LANE)], axis=1
        )
        probs = jnp.exp(mm_t(k2, jnp.concatenate([queries, ext], axis=1)))
        v2 = jnp.concatenate(
            [stack_pair(kv_ref[:, pair_slice(pair + width // 128)]), ones_ext(n_keys, pair, 0)],
            axis=1,
        )
        d_probs = mm_t(v2, jnp.concatenate([grads, ext], axis=1))
        d_scores = (probs * d_probs).astype(BF)
        add_pair(pair, unstack_pair(mm(d_scores, queries)), unstack_pair(mm2(probs, grads)))
        return carry

    lax.fori_loop(0, HEADS // 2, one_pair, 0, unroll=True)


class Fetch:
    def __init__(self, me, sems):
        self.me, self.sems, self.used = me, sems, 0

    def start(self, slots, source, target):
        copies = []
        for slot, ref in enumerate(slots):
            quarter = jnp.bitwise_xor(self.me, slot)
            copy = pltpu.make_async_copy(source(ref), target(quarter), self.sems.at[self.used])
            self.used += 1
            copy.start()
            copies.append(copy)
        return copies

    def rows(self, slots, first, width, ref, height=128):
        copies = []
        for part in range(height // 128):
            copies += self.start(
                slots,
                lambda s, part=part: s.at[pl.ds(0, 128), pl.ds(first + part * width, width)],
                lambda quarter, part=part: ref.at[
                    pl.ds(pl.multiple_of(quarter * height + part * 128, 128), 128)
                ],
            )
        return copies

    def shards(self, refs, ref, block=0):
        copies = []
        if len(refs) == 1:
            tall = ref.shape[0]
            source = refs[0].at[pl.ds(pl.multiple_of(block * tall, 8), tall)]
            pieces = [(source, ref)]
        else:
            tall = ref.shape[0] // len(refs)
            pieces = [(r, ref.at[pl.ds(i * tall, tall)]) for i, r in enumerate(refs)]
        for source, target in pieces:
            copy = pltpu.make_async_copy(source, target, self.sems.at[self.used])
            self.used += 1
            copy.start()
            copies.append(copy)
        return copies

    def small(self, slots, ref):
        return self.start(
            slots,
            lambda s: s.at[pl.ds(128, 16), pl.ds(0, 128)],
            lambda quarter: ref.at[:, pl.ds(pl.multiple_of(quarter * 128, 128), 128)],
        )


def wait(copies):
    for copy in copies:
        copy.wait()


def quarter_of(ref, me, slot, width):
    start = pl.multiple_of(jnp.bitwise_xor(me, slot) * width, 128)
    return ref[:, pl.ds(start, width)]


KEPT = (0, 2)
SENT = (1, 3)


def put_blocks(keep_ref, send_ref, first, me, block_of):
    for target, slots in ((keep_ref, KEPT), (send_ref, SENT)):
        for place, slot in enumerate(slots):
            block = block_of(slot).astype(target.dtype)
            rows = block.shape[0]
            for part in range(block.shape[1] // 512):
                target[place, first + part * rows : first + (part + 1) * rows, :] = block[
                    :, 512 * part : 512 * (part + 1)
                ]


def small_row(small_ref, row):
    return small_ref[row : row + 1, :].astype(F32)


GAIN, BIAS = 5, 8
HIDDEN_QUARTER = 512


def first_last(blocks, block, at, what):
    if blocks > 1:
        pl.when(block == (0 if at == "first" else blocks - 1))(what)
    else:
        what()


def self_forward_kernel(blocks, order, n_tok, scal, x_ref, *refs):
    toks, g1 = refs[:n_tok], refs[n_tok : n_tok + 4]
    kv_ref, q_ref, ext_ref, mixed_ref = refs[n_tok + 4 : n_tok + 8]
    wq, wkv, tok, kext, m_st, l_st, a_st, sems = refs[n_tok + 8 :]
    me, live, here = scal[0], scal[1], scal[5]
    block = pl.program_id(0)
    n_rows, width = x_ref.shape
    fetch = Fetch(me, sems)
    c_tok = fetch.shards(toks, tok, block)

    def begin():
        c_q = fetch.rows(g1, 0, width, wq)
        c_kv = fetch.rows(g1, width, 2 * width, wkv)
        wait(c_q)
        q_ref[...] = (mm(x_ref[...], wq[...]).astype(BF).astype(F32) * 0.125).astype(BF)
        wait(c_kv)

    first_last(blocks, block, "first", begin)
    fill_ext(kext, block * (tok.shape[0] // n_rows), n_rows, here, live, order)
    wait(c_tok)
    kv_ref[...] = mm(tok[...], wkv[...]).astype(BF)
    table = attend_forward(q_ref, kv_ref, kext, mixed_ref, (m_st, l_st, a_st), blocks, block)

    def finish():
        ext_ref[...] = table

    first_last(blocks, block, "last", finish)


def self_dense_kernel(scal, x_ref, mixed_ref, *refs):
    g1, g2 = refs[0:4], refs[4:8]
    sum_ref, cq_ref = refs[8:10]
    wo, wc, small, sems = refs[10:]
    width = x_ref.shape[1]
    fetch = Fetch(scal[0], sems)
    c_o = fetch.rows(g2, 0, width, wo)
    c_rest = fetch.small(g1, small)
    c_rest += fetch.rows(g2, width, width, wc)
    wait(c_o)
    first = x_ref[...].astype(F32) + mm(mixed_ref[...].astype(BF), wo[...])
    sum_ref[...] = first
    wait(c_rest)
    normed, _ = norm_stats(first)
    hidden = normed * small_row(small, GAIN) + small_row(small, BIAS)
    cq = mm(hidden.astype(BF), wc[...]).astype(BF)
    cq_ref[...] = (cq.astype(F32) * 0.125).astype(BF)


def gelu_parts(value):
    coef = math.sqrt(2.0 / math.pi)
    square = value * value
    inner = coef * (value + 0.044715 * value * square)
    bend = jnp.tanh(inner)
    half = 0.5 * (1.0 + bend)
    slope = half + 0.5 * value * (1.0 - bend * bend) * coef * (1.0 + 3 * 0.044715 * square)
    return value * half, slope


def cross_forward_kernel(order, n_mem, scal, cq_ref, *refs):
    mems, g2 = refs[:n_mem], refs[n_mem : n_mem + 4]
    kv_ref, ext_ref, mixed_ref = refs[n_mem + 4 : n_mem + 7]
    wkv, mem, kext, sems = refs[n_mem + 7 :]
    me, live, here = scal[0], scal[3], scal[5]
    width = cq_ref.shape[1]
    fetch = Fetch(me, sems)
    c_kv = fetch.rows(g2, 2 * width, 2 * width, wkv)
    c_mem = fetch.shards(mems, mem)
    fill_ext(kext, 0, scal_rows(mem, order), here, live, order)
    wait(c_kv)
    wait(c_mem)
    kv_ref[...] = mm(mem[...], wkv[...]).astype(BF)
    ext_ref[...] = attend_forward(cq_ref, kv_ref, kext, mixed_ref, None, 1, 0)


def scal_rows(array, order):
    return array.shape[0] // len(order) if order else array.shape[0]


def middle_kernel(scal, mixed_ref, ext_ref, sum_ref, cot_ref, prev_ref, *refs):
    g1, g2, g3 = refs[0:4], refs[4:8], refs[8:12]
    pay_ref, masked_ref, g_ref, second_ref, sums_ref, keep_ref, send_ref = refs[12:19]
    wo, w1, w2, ws, small, low, hid, act, sems = refs[19:]
    me, live, base = scal[0], scal[1], scal[2]
    n_rows, width = sum_ref.shape
    hidden_units = w1.shape[1]
    fetch = Fetch(me, sems)
    c_small = fetch.small(g1, small)
    c_o = fetch.rows(g2, 4 * width, width, wo)
    c_1 = fetch.rows(g3, 0, hidden_units, w1)
    c_2 = fetch.rows(g3, hidden_units, width, w2, hidden_units // 4)
    c_s = fetch.rows(g3, 2 * hidden_units, width, ws, 256)
    low[...] = mixed_ref[...].astype(BF)
    wait(c_small)
    wait(c_o)
    normed, _ = norm_stats(sum_ref[...])
    hidden_one = normed * small_row(small, GAIN) + small_row(small, BIAS)
    second = hidden_one + mm(low[...], wo[...])
    normed_two, inverse_two = norm_stats(second)
    hidden_two = normed_two * small_row(small, GAIN + 1) + small_row(small, BIAS + 1)
    hid[...] = hidden_two.astype(BF)
    bias_in = jnp.concatenate(
        [
            small[r : r + 1, 128 * j : 128 * j + 128].astype(F32)
            for j in range(4)
            for r in range(4)
        ],
        axis=1,
    )
    wait(c_1)
    preact = mm(hid[...], w1[...]) + bias_in
    active, slope = gelu_parts(preact)
    act[...] = active.astype(BF)
    wait(c_2)
    third = hidden_two + mm(act[...], w2[...]) + small_row(small, 4)
    normed_three, inverse_three = norm_stats(third)
    hidden_three = normed_three * small_row(small, GAIN + 2) + small_row(small, BIAS + 2)
    places = base + lax.broadcasted_iota(jnp.int32, (n_rows, 1), 0)
    valid = places < live
    masked_ref[...] = jnp.where(valid, hidden_three, 0.0).astype(BF)

    grads = jnp.where(valid, cot_ref[...].astype(F32), 0.0).astype(BF)
    g_ref[...] = grads
    wait(c_s)
    d_own = mm_t(grads, ws[:width, :])
    before = jnp.where(base - 1 < live, prev_ref[15:16, :].astype(F32), 0.0).astype(BF)
    shifted = jnp.concatenate([before, grads[:-1]], axis=0)
    d_next = mm_t(shifted, ws[width:, :])
    d_three = jnp.where(valid, d_own + d_next, 0.0)
    d_third, gain_three, bias_three = norm_back(
        d_three, normed_three, inverse_three, small_row(small, GAIN + 2)
    )
    e_third = d_third.astype(BF)
    d_pre = (mm_t(e_third, w2[...]) * slope).astype(BF)
    d_two = d_third + mm_t(d_pre, w1[...])
    d_second, gain_two, bias_two = norm_back(
        d_two, normed_two, inverse_two, small_row(small, GAIN + 1)
    )
    second_ref[...] = d_second
    e_second = d_second.astype(BF)
    d_cross = mm_t(e_second, wo[...]).astype(BF)
    pay_ref[:, :width] = d_cross
    pay_ref[:, width:] = add_delta(ext_ref[...], d_cross, mixed_ref[...])
    sums_ref[...] = jnp.zeros_like(sums_ref)
    sums_ref[0:1, :] = jnp.sum(d_pre.astype(F32), axis=0, keepdims=True)
    sums_ref[1:2, :width] = jnp.sum(e_third.astype(F32), axis=0, keepdims=True)
    sums_ref[3:4, :width] = gain_two
    sums_ref[4:5, :width] = gain_three
    sums_ref[6:7, :width] = bias_two
    sums_ref[7:8, :width] = bias_three
    put_blocks(
        keep_ref, send_ref, 0, me, lambda s: t_mm(quarter_of(act, me, s, hidden_units // 4), e_third)
    )
    put_blocks(keep_ref, send_ref, 512, me, lambda s: t_mm(quarter_of(hid, me, s, 128), d_pre))
    put_blocks(keep_ref, send_ref, 1024, me, lambda s: t_mm(quarter_of(low, me, s, 128), e_second))


def cross_query_kernel(order, scal, cq_ref, pay_ref, kv_ref, dq_ref, kext):
    live, here = scal[3], scal[5]
    fill_ext(kext, 0, scal_rows(kext, order), here, live, order)

    def add_pair(pair, value):
        dq_ref[:, pair_slice(pair)] = (value * 0.125).astype(BF)

    attend_query_back(cq_ref, pay_ref, kv_ref, kext, add_pair)


def cross_dense_kernel(scal, dq_ref, sum_ref, second_ref, mixed_ref, ext_ref, sums_ref, *refs):
    g1, g2 = refs[0:4], refs[4:8]
    d_first_ref, pay_ref, keep_ref, send_ref = refs[8:12]
    wo, wc, small, low, hid, sums, sems = refs[12:]
    me = scal[0]
    width = sum_ref.shape[1]
    fetch = Fetch(me, sems)
    c_c = fetch.rows(g2, width, width, wc)
    c_small = fetch.small(g1, small)
    c_o = fetch.rows(g2, 0, width, wo)
    wait(c_small)
    normed, inverse = norm_stats(sum_ref[...])
    hid[...] = (normed * small_row(small, GAIN) + small_row(small, BIAS)).astype(BF)
    low[...] = mixed_ref[...].astype(BF)
    wait(c_c)
    d_one = second_ref[...] + mm_t(dq_ref[...], wc[...])
    d_first, gain_one, bias_one = norm_back(d_one, normed, inverse, small_row(small, GAIN))
    d_first_ref[...] = d_first
    e_first = d_first.astype(BF)
    wait(c_o)
    d_self = mm_t(e_first, wo[...]).astype(BF)
    pay_ref[:, :width] = d_self
    pay_ref[:, width:] = add_delta(ext_ref[...], d_self, mixed_ref[...])
    put_blocks(keep_ref, send_ref, 0, me, lambda s: t_mm(quarter_of(low, me, s, 128), e_first))
    put_blocks(keep_ref, send_ref, 128, me, lambda s: t_mm(quarter_of(hid, me, s, 128), dq_ref[...]))
    sums[...] = sums_ref[...]
    sums[2:3, :width] = gain_one
    sums[5:6, :width] = bias_one
    quarter = sums_ref.shape[1] // 4

    def small_block(slot):
        top = quarter_of(sums, me, slot, quarter)
        rest = quarter_of(sums, me, slot, 128)
        rest = jnp.concatenate([rest, jnp.zeros((8, quarter - 128), F32)], axis=1)
        row = lax.broadcasted_iota(jnp.int32, (8, 1), 0)
        return jnp.concatenate(
            [jnp.where(row == 0, top, rest), jnp.zeros((120, quarter), F32)], axis=0
        )

    put_blocks(keep_ref, send_ref, 256, me, small_block)


def self_query_kernel(
    blocks, order, scal, q_ref, pay_ref, kv_ref, x_ref, d_first_ref, masked_ref, next_ref, g_ref,
    keep_in, send_in, *refs
):
    g1, g3 = refs[0:4], refs[4:8]
    part_ref, slots_ref, keep_ref, send_ref = refs[8:12]
    wq, ws, paired, acc, kext, sems = refs[12:]
    me, live, base, here = scal[0], scal[1], scal[2], scal[5]
    block = pl.program_id(0)
    n_rows, width = x_ref.shape
    before = keep_in.shape[1]

    def begin():
        fetch = Fetch(me, sems)
        c_q = fetch.rows(g1, 0, width, wq)
        c_s = fetch.rows(g3, 2 * HIDDEN_QUARTER * 4, width, ws, 256)
        masked = masked_ref[...]
        paired[:, :width] = masked
        paired[:, width:] = jnp.concatenate([masked[1:], next_ref[0:1, :]], axis=0)
        places = base + lax.broadcasted_iota(jnp.int32, (n_rows, 1), 0)
        keep_ref[:, :before, :] = keep_in[...]
        send_ref[:, :before, :] = send_in[...]
        put_blocks(
            keep_ref, send_ref, before, me, lambda s: t_mm(quarter_of(paired, me, s, 256), g_ref[...])
        )
        wait(c_s)
        slots_ref[...] = jnp.where(places < live, mm(paired[...], ws[...]), 0.0).astype(BF)
        wait(c_q)

    first_last(blocks, block, "first", begin)
    fill_ext(kext, block * (kext.shape[0] // n_rows), n_rows, here, live, order)

    def add_pair(pair, value):
        at = pair_slice(pair)
        if blocks > 1:
            value = value + jnp.where(block == 0, 0.0, acc[:, at])
        acc[:, at] = value

    attend_query_back(q_ref, pay_ref, kv_ref, kext, add_pair)

    def finish():
        dq = (acc[...] * 0.125).astype(BF)
        part_ref[...] = d_first_ref[...] + mm_t(dq, wq[...])
        put_blocks(
            keep_ref, send_ref, before + 256, me,
            lambda s: t_mm(quarter_of(x_ref, me, s, 128), dq),
        )

    first_last(blocks, block, "last", finish)


def key_kernel(blocks, queries, first, mask, counts, scal, x_ref, *refs):
    n_q, n_pay, n_part = counts
    qs, pays = refs[:n_q], refs[n_q : n_q + n_pay]
    refs = refs[n_q + n_pay :]
    part = refs[:n_part]
    group = refs[n_part : n_part + 4]
    grad_ref, keep_ref, send_ref = refs[n_part + 4 : n_part + 7]
    wkv, wq, kv, acc, low, q_all, pay_all, sems = refs[n_part + 7 :]
    me, live, base = scal[0], scal[mask], scal[mask + 1]
    block = pl.program_id(0)
    n_rows, width = x_ref.shape
    fetch = Fetch(me, sems)
    c_q = fetch.shards(qs, q_all, block)
    c_pay = fetch.shards(pays, pay_all, block)

    def begin():
        c_w = fetch.rows(group, first, 2 * width, wkv)
        if queries:
            c_w += fetch.rows(group, 0, width, wq)
        wait(c_w)
        kv[...] = mm(x_ref[...], wkv[...]).astype(BF)

    first_last(blocks, block, "first", begin)
    wait(c_q)
    if queries:
        q_all[...] = (mm(q_all[...], wq[...]).astype(BF).astype(F32) * 0.125).astype(BF)
    wait(c_pay)

    def add_pair(pair, d_key, d_value):
        at_key, at_value = pair_slice(pair), pair_slice(pair + width // 128)
        if blocks > 1:
            d_key = d_key + jnp.where(block == 0, 0.0, acc[:, at_key])
            d_value = d_value + jnp.where(block == 0, 0.0, acc[:, at_value])
            acc[:, at_key] = d_key
            acc[:, at_value] = d_value
        usable = base + lax.broadcasted_iota(jnp.int32, (n_rows, 1), 0) < live
        low[:, at_key] = jnp.where(usable, d_key, 0.0).astype(BF)
        low[:, at_value] = jnp.where(usable, d_value, 0.0).astype(BF)

    attend_key_back(kv, q_all, pay_all, add_pair)

    def finish():
        value = mm_t(low[...], wkv[...])
        grad_ref[...] = part[0][...] + value if n_part else value
        put_blocks(keep_ref, send_ref, 0, me, lambda s: t_mm(quarter_of(x_ref, me, s, 128), low[...]))

    first_last(blocks, block, "last", finish)


def assemble_kernel(layout, full, scal, line, other, *refs):
    outs, whole_ref, sems = refs[:-2], refs[-2], refs[-1]
    here = scal[5]
    rows = whole_ref.shape[0]
    copies = []
    for i, ref in enumerate((line, other)):
        x = jnp.bitwise_xor(lax.rem(here, 2), i)
        for k in range(1 if full else 4):
            if full:
                tall, source = rows // 2, ref
                at = pl.multiple_of(x * tall, 16)
            else:
                tall, source = rows // 8, ref.at[k]
                z = jnp.bitwise_xor(lax.div(here, 2), k)
                at = pl.multiple_of(x * (rows // 2) + z * tall, 16)
            copy = pltpu.make_async_copy(source, whole_ref.at[pl.ds(at, tall)], sems.at[4 * i + k])
            copy.start()
            copies.append(copy)
    wait(copies)
    for (first, tall, parts), out in zip(layout, outs):
        for part in range(parts):
            at = first + part * tall
            out[:, 512 * part : 512 * (part + 1)] = whole_ref[at : at + tall, :].astype(F32)


def whole(array, buffers=None):
    rank = len(array.shape)
    return pl.BlockSpec(tuple(array.shape), lambda *_: (0,) * rank)


def by_rows(array, rows):
    return pl.BlockSpec((rows, array.shape[1]), lambda i: (i, 0))


ANY = pl.BlockSpec(memory_space=pltpu.HBM)
SMEM = pl.BlockSpec(memory_space=pltpu.SMEM)


def shape(dims, dtype):
    return jax.ShapeDtypeStruct(dims, dtype)


def call(kernel, name, grid, args, specs, outs, out_specs, scratch, copies, flops, moved):
    return pl.pallas_call(
        kernel,
        name=name,
        grid=(grid,),
        in_specs=specs,
        out_specs=out_specs,
        out_shape=outs,
        scratch_shapes=[*scratch] + ([pltpu.SemaphoreType.DMA((copies,))] if copies else []),
        compiler_params=pltpu.CompilerParams(
            vmem_limit_bytes=VMEM_LIMIT, dimension_semantics=("arbitrary",)
        ),
        cost_estimate=pl.CostEstimate(
            flops=flops * COST, bytes_accessed=moved // 64, transcendentals=0
        ),
    )(*args)


def vm(dims, dtype):
    return pltpu.VMEM(dims, dtype)


def grad_outs(rows):
    return (shape((2, rows, 512), F32), shape((2, rows, 512), BF))


def permute(value, axis, target):
    n = lax.axis_size(axis)
    pairs = [(i, target(i)) for i in range(n) if 0 <= target(i) < n]
    return lax.ppermute(value, axis, pairs)


def flip(value, axis, bits):
    return permute(value, axis, lambda i: i ^ bits)


def rows_of(ctx, gathered):
    return [a.reshape(-1, a.shape[-1]) for a in gathered]


def gather_line(value):
    return [value] + [flip(value, "ctx", bits) for bits in (2, 4, 6)]


def across_ctx(item):
    return flip(item, "ctx", 1)


def after(value, *others):
    return lax.optimization_barrier((value, *others))[0]


def gather_wsh(group):
    own = group
    across = flip(own, "wsh", 2)
    return (own, flip(own, "wsh", 1), across, flip(across, "wsh", 1))


def part_of(array, index, count):
    rows = array.shape[0] // count
    return lax.dynamic_slice_in_dim(array, index * rows, rows, 0)


class Clock:
    def __init__(self):
        self.last = None

    def __call__(self, *values):
        if self.last is None:
            return values
        return lax.optimization_barrier((*values, self.last))[:-1]

    def tick(self, value):
        self.last = value
        return value


class Total:
    def __init__(self, clock, name, scal, layout, keep, send, full=False):
        self.clock, self.name, self.scal, self.layout = clock, name, scal, layout
        self.keep, self.full = keep, full
        self.got = flip(send, "wsh", 1)
        self.ctx = lax.axis_size("ctx") == 8

    def across(self):
        keep, got = self.clock(self.keep, self.got)
        half = keep + got.astype(F32)
        out = self.clock.tick(half[1].astype(BF))
        self.own, self.got = half[0], flip(out, "wsh", 2)

    def side(self):
        if not self.ctx:
            return
        x = lax.axis_index("ctx") % 2
        own, got = self.clock(self.own, self.got)
        self.mine = part_of(own, x, 2) + part_of(got, x, 2).astype(F32)
        out = (part_of(own, 1 - x, 2) + part_of(got, 1 - x, 2).astype(F32)).astype(BF)
        self.got = flip(self.clock.tick(out), "ctx", 1)

    def spread(self):
        if not self.ctx:
            return
        z = lax.axis_index("ctx") // 2
        mine, got = self.clock(self.mine, self.got)
        mine = mine + got.astype(F32)
        low = mine.astype(BF)
        if self.full:
            low = self.clock.tick(low)
            self.mine = low.astype(F32)
            self.got = [flip(low, "ctx", 2 * k) for k in (1, 2, 3)]
            return
        out = [part_of(low, z ^ k, 4) for k in (1, 2, 3)]
        self.clock.tick(out[0])
        self.mine = part_of(mine, z, 4)
        self.got = [flip(out[k - 1], "ctx", 2 * k) for k in (1, 2, 3)]

    def collect(self):
        if not self.ctx:
            return
        mine, *came = self.clock(self.mine, *self.got)
        came = [item.astype(F32) for item in came]
        piece = self.clock.tick(((mine + came[0]) + (came[1] + came[2])).astype(BF))
        if self.full:
            self.got = [piece, flip(piece, "ctx", 1)]
        else:
            self.got = [piece] + [flip(piece, "ctx", 2 * k) for k in (1, 2, 3)]

    def line(self):
        if self.ctx and not self.full:
            line = self.clock.tick(jnp.stack(self.clock(*self.got)))
            self.got = [line, flip(line, "ctx", 1)]

    def finish(self):
        layout = self.layout
        if not self.ctx:
            summed = lax.psum((self.own + self.got.astype(F32)).astype(BF), "ctx").astype(F32)
            return [
                jnp.concatenate(
                    [summed[first + i * tall : first + (i + 1) * tall] for i in range(parts)],
                    axis=1,
                )
                for first, tall, parts in layout
            ]
        line, other = self.clock(*self.got)
        rows = self.own.shape[0]
        outs = tuple(shape((tall, 512 * parts), F32) for _, tall, parts in layout)
        result = call(
            functools.partial(assemble_kernel, layout, self.full), self.name, 1,
            (self.scal, line, other), [SMEM, ANY, ANY], outs,
            tuple(pl.BlockSpec(o.shape, lambda i: (0, 0)) for o in outs),
            [vm((rows, 512), BF)], 8, 2, rows * 4096,
        )
        self.clock.tick(result[0])
        return result


def shards(
    decoder_in,
    memory,
    seq_lengths,
    mem_lengths,
    self_query,
    self_keyval,
    self_out,
    cross_query,
    cross_keyval,
    cross_out,
    ffn_in,
    ffn_bias_in,
    ffn_out,
    ffn_bias_out,
    slot_weight,
    norm_gain,
    norm_bias,
    cotangent,
):
    tokens, mem_rows, cot = decoder_in[0], memory[0], cotangent[0]
    n_rows, width = tokens.shape
    n_mem = mem_rows.shape[0]
    hidden_units = ffn_in.shape[1]
    ctx = lax.axis_size("ctx")
    here, me = lax.axis_index("ctx"), lax.axis_index("wsh")
    n_keys, all_mem = ctx * n_rows, ctx * n_mem
    blocks = max(1, n_keys // 1536)
    step = n_keys // blocks

    def blocks_of(array, count):
        tall = array.shape[0] // count
        return [array[i * tall : (i + 1) * tall] for i in range(count)]

    small = jnp.concatenate(
        [ffn_bias_in.reshape(4, 128), ffn_bias_out.reshape(1, 128), norm_gain, norm_bias,
         jnp.zeros((5, 128), BF)],
        axis=0,
    )
    small = jnp.concatenate([small, jnp.zeros((16, 3 * width - 128), BF)], axis=1)
    group1 = jnp.concatenate([jnp.concatenate([self_query, self_keyval], axis=1), small], axis=0)
    group2 = jnp.concatenate([self_out, cross_query, cross_keyval, cross_out], axis=1)
    group3 = jnp.concatenate(
        [ffn_in, *blocks_of(ffn_out, hidden_units // 512), *blocks_of(slot_weight, 2)], axis=1
    )
    split = ctx == 8
    clock = Clock()
    (tokens_in,) = lax.optimization_barrier((tokens, group1))[:1]
    g1 = gather_wsh(group1)
    if split:
        line = gather_line(tokens_in)
        toks = line + [across_ctx(item) for item in line]
    else:
        toks = [lax.all_gather(tokens, "ctx", axis=0, tiled=True)]
    y2 = flip(after(group2, g1[2]), "wsh", 2)
    c2 = flip(group2, "wsh", 1)
    y3 = flip(after(group3, y2, toks[-1]), "wsh", 2)
    if split:
        mem_line = gather_line(after(mem_rows, *toks[1:4]))
        mem_side = [across_ctx(after(mem_rows, toks[-1]))]
    prev_cot = permute(after(cot[-16:], y2), "ctx", lambda i: i + 1)

    live, mem_live = seq_lengths[0], mem_lengths[0]
    scal = jnp.stack(
        [me, live, here * n_rows, mem_live, here * n_mem, here, 0, 0]
    ).astype(jnp.int32)

    order = ORDER if ctx == 8 else None

    def fixed(*dims):
        return [pl.BlockSpec(d, lambda i, r=len(d): (0,) * r) for d in dims]

    tall, pay_w = (n_rows, width), (n_rows, width + EXT)
    pair_rows = (HEADS // 2, 2 * n_rows)
    by_block = pl.BlockSpec((step, 2 * width), lambda i: (i, 0))
    tokens_now, *toks = clock(after(tokens, y2), *toks)
    kv, qs, self_ext, self_mixed = call(
        functools.partial(self_forward_kernel, blocks, order, len(toks)), "self_forward", blocks,
        (scal, tokens_now, *toks, *g1),
        [SMEM, whole(tokens)] + [ANY] * (len(toks) + 4),
        (shape((n_keys, 2 * width), BF), shape(tall, BF), shape((n_rows, EXT), BF),
         shape(tall, F32)),
        [by_block] + fixed(tall, (n_rows, EXT), tall),
        [vm((width, width), BF), vm((width, 2 * width), BF), vm((step, width), BF),
         vm((step, EXT), BF)]
        + ([vm((*pair_rows, 1), F32), vm((*pair_rows, 1), F32), vm((*pair_rows, 128), F32)]
           if blocks > 1 else [vm((8, 128), F32)] * 3),
        8 + len(toks), 11, 8 * 2**20,
    )
    clock.tick(qs)
    (y2,) = clock(y2)
    g2 = (group2, c2, y2, flip(y2, "wsh", 1))
    c3 = flip(clock(group3)[0], "wsh", 1)
    if split:
        mem_side += [across_ctx(clock(item)[0]) for item in mem_line[1:]]
        mems = mem_line + mem_side
    else:
        mems = [lax.all_gather(mem_rows, "ctx", axis=0, tiled=True)]
    self_mixed_now, *g2_now = clock(self_mixed, *g2)
    first_sum, cqs = call(
        self_dense_kernel, "self_dense", 1,
        (scal, tokens, self_mixed_now, *g1, *g2_now),
        [SMEM, whole(tokens), whole(self_mixed)] + [ANY] * 8,
        (shape(tall, F32), shape(tall, BF)), fixed(tall, tall),
        [vm((width, width), BF), vm((width, width), BF), vm((16, width), BF)],
        12, 2, 2 * 2**20,
    )
    clock.tick(cqs)
    if split:
        cq_line = gather_line(after(cqs, *mem_line[1:]))
    (cqs_now, *mems_now) = clock(cqs, *mems)
    memkv, cross_ext, cross_mixed = call(
        functools.partial(cross_forward_kernel, order, len(mems)), "cross_forward", 1,
        (scal, cqs_now, *mems_now, *g2),
        [SMEM, whole(cqs)] + [ANY] * (len(mems) + 4),
        (shape((all_mem, 2 * width), BF), shape((n_rows, EXT), BF), shape(tall, F32)),
        fixed((all_mem, 2 * width), (n_rows, EXT), tall),
        [vm((width, 2 * width), BF), vm((all_mem, width), BF), vm((all_mem, EXT), BF)],
        4 + len(mems), 12, 8 * 2**20,
    )
    clock.tick(cross_ext)
    (y3,) = clock(y3)
    g3 = (group3, c3, y3, flip(y3, "wsh", 1))
    if split:
        cq_line = clock.tick(jnp.concatenate(clock(*cq_line), axis=0))
        all_cq = [cq_line, across_ctx(cq_line)]
    else:
        all_cq = [lax.all_gather(cqs, "ctx", axis=0, tiled=True)]
    (cross_mixed_now, prev_now, *g3_now) = clock(cross_mixed, prev_cot, *g3)
    pay_dc, masked, grads, d_second, sums, keep_a, send_a = call(
        middle_kernel, "middle", 1,
        (scal, cross_mixed_now, cross_ext, first_sum, cot, prev_now, *g1, *g2, *g3_now),
        [SMEM] + [whole(a) for a in (cross_mixed, cross_ext, first_sum, cot, prev_cot)]
        + [ANY] * 12,
        (shape(pay_w, BF), shape(tall, BF), shape(tall, BF),
         shape(tall, F32), shape((8, hidden_units), F32), *grad_outs(1152)),
        fixed(pay_w, tall, tall, tall, (8, hidden_units), (2, 1152, 512), (2, 1152, 512)),
        [vm((width, width), BF), vm((width, hidden_units), BF),
         vm((hidden_units, width), BF), vm((2 * width, width), BF), vm((16, width), BF),
         vm(tall, BF), vm(tall, BF), vm((n_rows, hidden_units), BF)],
        40, 12, 20 * 2**20,
    )
    clock.tick(pay_dc)
    sum_a = Total(
        clock, "sum_a", scal,
        ((0, 512, 1), (512, 128, hidden_units // 512), (1024, 128, 1)), keep_a, send_a,
    )
    if split:
        dc_line = gather_line(pay_dc)
        dc_side = [across_ctx(pay_dc)]
    else:
        all_dc = [lax.all_gather(pay_dc, "ctx", axis=0, tiled=True)]
    next_row = permute(masked[:16], "ctx", lambda i: i - 1)
    (pay_dc_now,) = clock(pay_dc)
    (dq_cross,) = call(
        functools.partial(cross_query_kernel, order), "cross_query", 1,
        (scal, cqs, pay_dc_now, memkv),
        [SMEM] + [whole(a) for a in (cqs, pay_dc, memkv)],
        (shape(tall, BF),), tuple(fixed(tall)), [vm((all_mem, EXT), BF)], 0, 13, 5 * 2**20,
    )
    clock.tick(dq_cross)
    if split:
        dc_side += [across_ctx(clock(item)[0]) for item in dc_line[1:2]]
    sum_a.across()
    (dq_now,) = clock(dq_cross)
    d_first, pay_ds, keep_b, send_b = call(
        cross_dense_kernel, "cross_dense", 1,
        (scal, dq_now, first_sum, d_second, self_mixed, self_ext, sums, *g1, *g2),
        [SMEM]
        + [whole(a) for a in (dq_cross, first_sum, d_second, self_mixed, self_ext, sums)]
        + [ANY] * 8,
        (shape(tall, F32), shape(pay_w, BF), *grad_outs(384)),
        fixed(tall, pay_w, (2, 384, 512), (2, 384, 512)),
        [vm((width, width), BF), vm((width, width), BF), vm((16, width), BF),
         vm(tall, BF), vm(tall, BF), vm((8, hidden_units), F32)],
        12, 8, 6 * 2**20,
    )
    clock.tick(pay_ds)
    if split:
        ds_line = gather_line(pay_ds)
        dc_side += [across_ctx(clock(item)[0]) for item in dc_line[2:]]
        all_dc = dc_line + dc_side
    else:
        all_ds = [lax.all_gather(pay_ds, "ctx", axis=0, tiled=True)]
    pay_now, next_now = clock(pay_ds, next_row)
    part, slots, keep_b, send_b = call(
        functools.partial(self_query_kernel, blocks, order), "self_query", blocks,
        (scal, qs, pay_now, kv, tokens, d_first, masked, next_now, grads, keep_b, send_b, *g1, *g3),
        [SMEM, whole(qs), whole(pay_ds), by_block]
        + [whole(a) for a in (tokens, d_first, masked, next_row, grads, keep_b, send_b)] + [ANY] * 8,
        (shape(tall, F32), shape(tall, BF), *grad_outs(768)),
        fixed(tall, tall, (2, 768, 512), (2, 768, 512)),
        [vm((width, width), BF), vm((2 * width, width), BF), vm((n_rows, 2 * width), BF),
         vm(tall, F32), vm((step, EXT), BF)],
        12, 9, 8 * 2**20,
    )
    clock.tick(part)
    sum_b = Total(
        clock, "sum_b", scal,
        ((0, 128, 1), (128, 128, 1), (256, 8, 1), (384, 256, 1), (640, 128, 1)), keep_b, send_b,
    )
    if split:
        ds_side = [across_ctx(clock(item)[0]) for item in ds_line]
        all_ds = ds_line + ds_side

    def keys_back(name, x, queries, q_from, pays, extra, group, first, mask, cost):
        rows = x.shape[0]
        came = clock(*q_from, *pays)
        q_from, pays = came[: len(q_from)], came[len(q_from) :]
        result = call(
            functools.partial(
                key_kernel, blocks, queries, first, mask, (len(q_from), len(pays), len(extra))
            ),
            name, blocks,
            (scal, x, *q_from, *pays, *extra, *group),
            [SMEM, whole(x)] + [ANY] * (len(q_from) + len(pays)) + [whole(e) for e in extra]
            + [ANY] * 4,
            (shape((rows, width), F32), *grad_outs(256)),
            fixed((rows, width), (2, 256, 512), (2, 256, 512)),
            [vm((width, 2 * width), BF), vm((width, width) if queries else (16, 128), BF),
             vm((rows, 2 * width), BF),
             vm((rows, 2 * width) if blocks > 1 else (8, 128), F32), vm((rows, 2 * width), BF),
             vm((step, width), BF), vm((step, width + EXT), BF)],
            8 + len(q_from) + len(pays), cost, 8 * 2**20,
        )
        clock.tick(result[0])
        return result

    grad_mem, keep_m, send_m = keys_back(
        "cross_key", mem_rows, False, all_cq, all_dc, (), g2, 2 * width, 3, 12
    )
    sum_m = Total(clock, "sum_m", scal, ((0, 128, 2),), keep_m, send_m, True)
    sum_a.side()
    sum_b.across()
    sum_m.across()
    grad_input, keep_k, send_k = keys_back(
        "self_key", tokens, True, toks, all_ds, (part,), g1, width, 1, 11
    )
    sum_k = Total(clock, "sum_k", scal, ((0, 128, 2),), keep_k, send_k, True)
    sum_a.spread()
    sum_b.side()
    sum_k.across()
    sum_m.side()
    sum_a.collect()
    sum_b.spread()
    sum_k.side()
    sum_m.spread()
    sum_a.line()
    sum_b.collect()
    sum_k.spread()
    sum_m.collect()
    sum_b.line()
    sum_k.collect()
    g_second, g_first, g_cout = sum_a.finish()
    (g_ckv,) = sum_m.finish()
    g_out, g_cq, tiny, g_slot, g_q = sum_b.finish()
    (g_kv,) = sum_k.finish()
    return (
        slots[None],
        grad_input[None],
        grad_mem[None],
        g_q,
        g_kv,
        g_out,
        g_cq,
        g_ckv,
        g_cout,
        g_first,
        tiny[0],
        g_second,
        tiny[1, :128],
        g_slot,
        tiny[2:5, :128],
        tiny[5:8, :128],
    )


def solution(mesh):
    rows, split = P("wsh", "ctx", None), P("wsh", None)
    line, side = P("wsh"), P(None, "wsh")
    in_specs = (
        rows, rows, line, line, split, split, split, split, split, split, split, line, split, line,
        split, side, side, rows,
    )
    out_specs = (
        rows, rows, rows, split, split, split, split, split, split, split, line, split, line, split,
        side, side,
    )
    return jax.shard_map(shards, mesh=mesh, in_specs=in_specs, out_specs=out_specs, check_vma=False)
```

```python
import functools
import math

import jax
import jax.numpy as jnp
from jax import lax
from jax.experimental import pallas as pl
from jax.experimental.pallas import tpu as pltpu
from jax.sharding import PartitionSpec as P

HEADS = 8
NORM_EPS = 1e-05
DEAD = -1e30
EXT = 128
DEAD_LANE = 3 * HEADS
LSE_LANE = 32
ORDER = (0, 2, 4, 6, 1, 3, 5, 7)
BF = jnp.bfloat16
F32 = jnp.float32
COST = 10**9
GRANTS = {}


def mm(left, right):
    return lax.dot_general(left, right, (((1,), (0,)), ((), ())), preferred_element_type=F32)


def mm2(left, right):
    high = left.astype(BF)
    low = (left - high.astype(F32)).astype(BF)
    return mm(high, right) + mm(low, right)


def mm_t(left, right):
    return lax.dot_general(left, right, (((1,), (1,)), ((), ())), preferred_element_type=F32)


def t_mm(left, right):
    return lax.dot_general(left, right, (((0,), (0,)), ((), ())), preferred_element_type=F32)


def norm_stats(values):
    center = values - jnp.mean(values, axis=-1, keepdims=True)
    inverse = lax.rsqrt(jnp.mean(center * center, axis=-1, keepdims=True) + NORM_EPS)
    return center * inverse, inverse


def norm_back(grad_out, normed, inverse, gain_row):
    scaled = grad_out * gain_row
    grad_in = inverse * (
        scaled
        - jnp.mean(scaled, axis=-1, keepdims=True)
        - normed * jnp.mean(scaled * normed, axis=-1, keepdims=True)
    )
    return (
        grad_in,
        jnp.sum(grad_out * normed, axis=0, keepdims=True),
        jnp.sum(grad_out, axis=0, keepdims=True),
    )


def lanes(width=128):
    return lax.broadcasted_iota(jnp.int32, (1, width), 1)


def stack_pair(block):
    low = lanes() < 64
    zero = jnp.zeros_like(block)
    return jnp.concatenate([jnp.where(low, block, zero), jnp.where(low, zero, block)], axis=0)


def unstack_pair(stacked):
    n = stacked.shape[0] // 2
    return jnp.where(lanes() < 64, stacked[:n], stacked[n:])


def split3(value):
    high = value.astype(BF).astype(F32)
    rest = value - high
    mid = rest.astype(BF).astype(F32)
    return high, mid, (rest - mid).astype(BF).astype(F32)


def place3(table, column, lane):
    where = lanes()
    for term, part in enumerate(split3(column)):
        table = jnp.where(where == lane + term, part, table)
    return table


def pair_ext(table, pair, offset):
    where = lanes()
    other = jnp.where(where == DEAD_LANE, 1.0 if offset else 0.0, 0.0).astype(table.dtype)
    parts = []
    for head in (2 * pair, 2 * pair + 1):
        first = offset + 3 * head
        parts.append(jnp.where((where >= first) & (where < first + 3), table, other))
    return jnp.concatenate(parts, axis=0)


def ones_ext(rows, pair, offset):
    where = lanes()
    parts = []
    for head in (2 * pair, 2 * pair + 1):
        first = offset + 3 * head
        one = jnp.where((where >= first) & (where < first + 3), 1.0, 0.0)
        parts.append(jnp.broadcast_to(one, (rows, EXT)))
    return jnp.concatenate(parts, axis=0).astype(BF)


def add_delta(table, grad_low, mixed):
    product = grad_low.astype(F32) * mixed
    low = lanes() < 64
    table = table.astype(F32)
    for pair in range(HEADS // 2):
        block = product[:, 128 * pair : 128 * pair + 128]
        even = jnp.sum(jnp.where(low, block, 0.0), axis=1, keepdims=True)
        odd = jnp.sum(jnp.where(low, 0.0, block), axis=1, keepdims=True)
        table = place3(table, -even, 6 * pair)
        table = place3(table, -odd, 6 * pair + 3)
    return table.astype(BF)


def fill_ext(ext_ref, first, rows, here, limit, order):
    where = lanes()
    base = jnp.where(where == DEAD_LANE, 0.0, 1.0)
    for i in range(ext_ref.shape[0] // rows):
        device = jnp.bitwise_xor(here, order[i]) if order else first + i
        place = device * rows + lax.broadcasted_iota(jnp.int32, (rows, 1), 0)
        dead = (where == DEAD_LANE) & (place >= limit)
        ext_ref[i * rows : (i + 1) * rows, :] = jnp.where(dead, DEAD, base).astype(BF)


def pair_slice(pair):
    return pl.ds(pl.multiple_of(pair * 128, 128), 128)


def attend_forward(q_ref, kv_ref, kext_ref, mixed_ref, state, blocks, block):
    n_rows, width = q_ref.shape
    where = lanes()
    ext = jnp.broadcast_to(jnp.where(where == DEAD_LANE, 1.0, 0.0), (2 * n_rows, EXT)).astype(BF)
    kext = kext_ref[...]

    def one_pair(pair, table):
        q2 = jnp.concatenate([stack_pair(q_ref[:, pair_slice(pair)]), ext], axis=1)
        keys = jnp.concatenate([kv_ref[:, pair_slice(pair)], kext], axis=1)
        scores = mm_t(q2, keys)
        top = jnp.max(scores, axis=1, keepdims=True)
        if blocks > 1:
            before = jnp.where(block == 0, DEAD, state[0][pair])
            top = jnp.maximum(top, before)
        powers = jnp.exp(scores - top)
        total = jnp.sum(powers, axis=1, keepdims=True)
        mixed = mm2(powers, kv_ref[:, pair_slice(pair + width // 128)])
        if blocks > 1:
            fade = jnp.exp(before - top)
            total = total + fade * jnp.where(block == 0, 0.0, state[1][pair])
            mixed = mixed + fade * jnp.where(block == 0, 0.0, state[2][pair])
            state[0][pair] = top
            state[1][pair] = total
            state[2][pair] = mixed
        mixed_ref[:, pair_slice(pair)] = unstack_pair(mixed * (1.0 / total))
        lse = -(top + jnp.log(total))
        table = place3(table, lse[:n_rows], LSE_LANE + 6 * pair)
        return place3(table, lse[n_rows:], LSE_LANE + 6 * pair + 3)

    start = jnp.zeros((n_rows, EXT), F32)
    return lax.fori_loop(0, HEADS // 2, one_pair, start, unroll=True).astype(BF)


def attend_query_back(q_ref, pay_ref, kv_ref, kext_ref, add_pair):
    width = q_ref.shape[1]
    kext = kext_ref[...]
    ext = pay_ref[:, width:]

    def one_pair(pair, carry):
        keys = kv_ref[:, pair_slice(pair)]
        q2 = jnp.concatenate(
            [stack_pair(q_ref[:, pair_slice(pair)]), pair_ext(ext, pair, LSE_LANE)], axis=1
        )
        probs = jnp.exp(mm_t(q2, jnp.concatenate([keys, kext], axis=1)))
        do2 = jnp.concatenate(
            [stack_pair(pay_ref[:, pair_slice(pair)]), pair_ext(ext, pair, 0)], axis=1
        )
        values = kv_ref[:, pair_slice(pair + width // 128)]
        d_probs = mm_t(do2, jnp.concatenate([values, kext], axis=1))
        d_scores = (probs * d_probs).astype(BF)
        add_pair(pair, unstack_pair(mm(d_scores, keys)))
        return carry

    lax.fori_loop(0, HEADS // 2, one_pair, 0, unroll=True)


def attend_key_back(kv_ref, q_ref, pay_ref, add_pair):
    n_keys = kv_ref.shape[0]
    width = kv_ref.shape[1] // 2
    ext = pay_ref[:, width:]

    def one_pair(pair, carry):
        queries = q_ref[:, pair_slice(pair)]
        grads = pay_ref[:, pair_slice(pair)]
        k2 = jnp.concatenate(
            [stack_pair(kv_ref[:, pair_slice(pair)]), ones_ext(n_keys, pair, LSE_LANE)], axis=1
        )
        probs = jnp.exp(mm_t(k2, jnp.concatenate([queries, ext], axis=1)))
        v2 = jnp.concatenate(
            [stack_pair(kv_ref[:, pair_slice(pair + width // 128)]), ones_ext(n_keys, pair, 0)],
            axis=1,
        )
        d_probs = mm_t(v2, jnp.concatenate([grads, ext], axis=1))
        d_scores = (probs * d_probs).astype(BF)
        add_pair(pair, unstack_pair(mm(d_scores, queries)), unstack_pair(mm(probs.astype(BF), grads)))
        return carry

    lax.fori_loop(0, HEADS // 2, one_pair, 0, unroll=True)


class Fetch:
    def __init__(self, me, sems):
        self.me, self.sems, self.used = me, sems, 0

    def start(self, slots, source, target):
        copies = []
        for slot, ref in enumerate(slots):
            quarter = jnp.bitwise_xor(self.me, slot)
            copy = pltpu.make_async_copy(source(ref), target(quarter), self.sems.at[self.used])
            self.used += 1
            copy.start()
            copies.append(copy)
        return copies

    def rows(self, slots, first, width, ref, height=128):
        copies = []
        for part in range(height // 128):
            copies += self.start(
                slots,
                lambda s, part=part: s.at[pl.ds(0, 128), pl.ds(first + part * width, width)],
                lambda quarter, part=part: ref.at[
                    pl.ds(pl.multiple_of(quarter * height + part * 128, 128), 128)
                ],
            )
        return copies

    def shards(self, refs, ref, block=0, tail=False):
        copies = []
        if len(refs) == 1:
            tall = ref.shape[0]
            source = refs[0].at[pl.ds(pl.multiple_of(block * tall, 8), tall)]
            pieces = [(source, ref)]
        else:
            tall = ref.shape[0] // len(refs)
            pieces = [
                (
                    r.at[pl.ds(r.shape[0] - tall if tail else 0, tall)],
                    ref.at[pl.ds(i * tall, tall)],
                )
                for i, r in enumerate(refs)
            ]
        for source, target in pieces:
            copy = pltpu.make_async_copy(source, target, self.sems.at[self.used])
            self.used += 1
            copy.start()
            copies.append(copy)
        return copies

    def small(self, slots, ref):
        return self.start(
            slots,
            lambda s: s.at[pl.ds(128, 16), pl.ds(0, 128)],
            lambda quarter: ref.at[:, pl.ds(pl.multiple_of(quarter * 128, 128), 128)],
        )


def wait(copies):
    for copy in copies:
        copy.wait()


def quarter_of(ref, me, slot, width):
    start = pl.multiple_of(jnp.bitwise_xor(me, slot) * width, 128)
    return ref[:, pl.ds(start, width)]


KEPT = (0, 2)
SENT = (1, 3)


def put_blocks(keep_ref, send_ref, first, me, block_of):
    for target, slots in ((keep_ref, KEPT), (send_ref, SENT)):
        for place, slot in enumerate(slots):
            block = block_of(slot).astype(target.dtype)
            rows = block.shape[0]
            for part in range(block.shape[1] // 512):
                target[place, first + part * rows : first + (part + 1) * rows, :] = block[
                    :, 512 * part : 512 * (part + 1)
                ]


def small_row(small_ref, row):
    return small_ref[row : row + 1, :].astype(F32)


GAIN, BIAS = 5, 8
HIDDEN_QUARTER = 512


def first_last(blocks, block, at, what):
    if blocks > 1:
        pl.when(block == (0 if at == "first" else blocks - 1))(what)
    else:
        what()


def self_forward_kernel(blocks, order, n_tok, scal, x_ref, *refs):
    toks, g1 = refs[:n_tok], refs[n_tok : n_tok + 4]
    kv_ref, q_ref, ext_ref, mixed_ref = refs[n_tok + 4 : n_tok + 8]
    wq, wkv, tok, kext, m_st, l_st, a_st, sems = refs[n_tok + 8 :]
    me, live, here = scal[0], scal[1], scal[5]
    block = pl.program_id(0)
    n_rows, width = x_ref.shape
    fetch = Fetch(me, sems)
    c_tok = fetch.shards(toks, tok, block)

    def begin():
        c_q = fetch.rows(g1, 0, width, wq)
        c_kv = fetch.rows(g1, width, 2 * width, wkv)
        wait(c_q)
        q_ref[...] = (mm(x_ref[...], wq[...]).astype(BF).astype(F32) * 0.125).astype(BF)
        wait(c_kv)

    first_last(blocks, block, "first", begin)
    fill_ext(kext, block * (tok.shape[0] // n_rows), n_rows, here, live, order)
    wait(c_tok)
    kv_ref[...] = mm(tok[...], wkv[...]).astype(BF)
    table = attend_forward(q_ref, kv_ref, kext, mixed_ref, (m_st, l_st, a_st), blocks, block)

    def finish():
        ext_ref[...] = table

    first_last(blocks, block, "last", finish)


def self_dense_kernel(scal, x_ref, mixed_ref, *refs):
    g1, g2 = refs[0:4], refs[4:8]
    sum_ref, cq_ref = refs[8:10]
    wo, wc, small, sems = refs[10:]
    width = x_ref.shape[1]
    fetch = Fetch(scal[0], sems)
    c_o = fetch.rows(g2, 0, width, wo)
    c_rest = fetch.small(g1, small)
    c_rest += fetch.rows(g2, width, width, wc)
    wait(c_o)
    first = x_ref[...].astype(F32) + mm(mixed_ref[...].astype(BF), wo[...])
    sum_ref[...] = first
    wait(c_rest)
    normed, _ = norm_stats(first)
    hidden = normed * small_row(small, GAIN) + small_row(small, BIAS)
    cq = mm(hidden.astype(BF), wc[...]).astype(BF)
    cq_ref[...] = (cq.astype(F32) * 0.125).astype(BF)


def gelu_parts(value):
    coef = math.sqrt(2.0 / math.pi)
    square = value * value
    inner = coef * (value + 0.044715 * value * square)
    bend = jnp.tanh(inner)
    half = 0.5 * (1.0 + bend)
    slope = half + 0.5 * value * (1.0 - bend * bend) * coef * (1.0 + 3 * 0.044715 * square)
    return value * half, slope


def cross_forward_kernel(order, n_mem, scal, cq_ref, *refs):
    mems, g2 = refs[:n_mem], refs[n_mem : n_mem + 4]
    kv_ref, ext_ref, mixed_ref = refs[n_mem + 4 : n_mem + 7]
    wkv, mem, kext, sems = refs[n_mem + 7 :]
    me, live, here = scal[0], scal[3], scal[5]
    width = cq_ref.shape[1]
    fetch = Fetch(me, sems)
    c_kv = fetch.rows(g2, 2 * width, 2 * width, wkv)
    c_mem = fetch.shards(mems, mem, 0, True)
    fill_ext(kext, 0, scal_rows(mem, order), here, live, order)
    wait(c_kv)
    wait(c_mem)
    kv_ref[...] = mm(mem[...], wkv[...]).astype(BF)
    ext_ref[...] = attend_forward(cq_ref, kv_ref, kext, mixed_ref, None, 1, 0)


def scal_rows(array, order):
    return array.shape[0] // len(order) if order else array.shape[0]


def middle_kernel(scal, mixed_ref, ext_ref, sum_ref, cot_ref, prev_ref, *refs):
    g1, g2, g3 = refs[0:4], refs[4:8], refs[8:12]
    pay_ref, masked_ref, g_ref, second_ref, sums_ref, keep_ref, send_ref = refs[12:19]
    wo, w1, w2, ws, small, low, hid, act, sems = refs[19:]
    me, live, base = scal[0], scal[1], scal[2]
    n_rows, width = sum_ref.shape
    hidden_units = w1.shape[1]
    fetch = Fetch(me, sems)
    c_small = fetch.small(g1, small)
    c_o = fetch.rows(g2, 4 * width, width, wo)
    c_1 = fetch.rows(g3, 0, hidden_units, w1)
    c_2 = fetch.rows(g3, hidden_units, width, w2, hidden_units // 4)
    c_s = fetch.rows(g3, 2 * hidden_units, width, ws, 256)
    low[...] = mixed_ref[...].astype(BF)
    wait(c_small)
    wait(c_o)
    normed, _ = norm_stats(sum_ref[...])
    hidden_one = normed * small_row(small, GAIN) + small_row(small, BIAS)
    second = hidden_one + mm(low[...], wo[...])
    normed_two, inverse_two = norm_stats(second)
    hidden_two = normed_two * small_row(small, GAIN + 1) + small_row(small, BIAS + 1)
    hid[...] = hidden_two.astype(BF)
    bias_in = jnp.concatenate(
        [
            small[r : r + 1, 128 * j : 128 * j + 128].astype(F32)
            for j in range(4)
            for r in range(4)
        ],
        axis=1,
    )
    wait(c_1)
    preact = mm(hid[...], w1[...]) + bias_in
    active, slope = gelu_parts(preact)
    act[...] = active.astype(BF)
    wait(c_2)
    third = hidden_two + mm(act[...], w2[...]) + small_row(small, 4)
    normed_three, inverse_three = norm_stats(third)
    hidden_three = normed_three * small_row(small, GAIN + 2) + small_row(small, BIAS + 2)
    places = base + lax.broadcasted_iota(jnp.int32, (n_rows, 1), 0)
    valid = places < live
    masked_ref[...] = jnp.where(valid, hidden_three, 0.0).astype(BF)

    grads = jnp.where(valid, cot_ref[...].astype(F32), 0.0).astype(BF)
    g_ref[...] = grads
    wait(c_s)
    d_own = mm_t(grads, ws[:width, :])
    before = jnp.where(base - 1 < live, prev_ref[15:16, :].astype(F32), 0.0).astype(BF)
    shifted = jnp.concatenate([before, grads[:-1]], axis=0)
    d_next = mm_t(shifted, ws[width:, :])
    d_three = jnp.where(valid, d_own + d_next, 0.0)
    d_third, gain_three, bias_three = norm_back(
        d_three, normed_three, inverse_three, small_row(small, GAIN + 2)
    )
    e_third = d_third.astype(BF)
    d_pre = (mm_t(e_third, w2[...]) * slope).astype(BF)
    d_two = d_third + mm_t(d_pre, w1[...])
    d_second, gain_two, bias_two = norm_back(
        d_two, normed_two, inverse_two, small_row(small, GAIN + 1)
    )
    second_ref[...] = d_second
    e_second = d_second.astype(BF)
    d_cross = mm_t(e_second, wo[...]).astype(BF)
    pay_ref[:, :width] = d_cross
    pay_ref[:, width:] = add_delta(ext_ref[...], d_cross, mixed_ref[...])
    sums_ref[...] = jnp.zeros_like(sums_ref)
    sums_ref[0:1, :] = jnp.sum(d_pre.astype(F32), axis=0, keepdims=True)
    sums_ref[1:2, :width] = jnp.sum(e_third.astype(F32), axis=0, keepdims=True)
    sums_ref[3:4, :width] = gain_two
    sums_ref[4:5, :width] = gain_three
    sums_ref[6:7, :width] = bias_two
    sums_ref[7:8, :width] = bias_three
    put_blocks(
        keep_ref, send_ref, 0, me, lambda s: t_mm(quarter_of(act, me, s, hidden_units // 4), e_third)
    )
    put_blocks(keep_ref, send_ref, 512, me, lambda s: t_mm(quarter_of(hid, me, s, 128), d_pre))
    put_blocks(keep_ref, send_ref, 1024, me, lambda s: t_mm(quarter_of(low, me, s, 128), e_second))


def cross_query_kernel(order, scal, cq_ref, pay_ref, kv_ref, dq_ref, kext):
    live, here = scal[3], scal[5]
    fill_ext(kext, 0, scal_rows(kext, order), here, live, order)

    def add_pair(pair, value):
        dq_ref[:, pair_slice(pair)] = (value * 0.125).astype(BF)

    attend_query_back(cq_ref, pay_ref, kv_ref, kext, add_pair)


def cross_dense_kernel(scal, dq_ref, sum_ref, second_ref, mixed_ref, ext_ref, sums_ref, *refs):
    g1, g2 = refs[0:4], refs[4:8]
    d_first_ref, pay_ref, keep_ref, send_ref = refs[8:12]
    wo, wc, small, low, hid, sums, sems = refs[12:]
    me = scal[0]
    width = sum_ref.shape[1]
    fetch = Fetch(me, sems)
    c_c = fetch.rows(g2, width, width, wc)
    c_small = fetch.small(g1, small)
    c_o = fetch.rows(g2, 0, width, wo)
    wait(c_small)
    normed, inverse = norm_stats(sum_ref[...])
    hid[...] = (normed * small_row(small, GAIN) + small_row(small, BIAS)).astype(BF)
    low[...] = mixed_ref[...].astype(BF)
    wait(c_c)
    d_one = second_ref[...] + mm_t(dq_ref[...], wc[...])
    d_first, gain_one, bias_one = norm_back(d_one, normed, inverse, small_row(small, GAIN))
    d_first_ref[...] = d_first
    e_first = d_first.astype(BF)
    wait(c_o)
    d_self = mm_t(e_first, wo[...]).astype(BF)
    pay_ref[:, :width] = d_self
    pay_ref[:, width:] = add_delta(ext_ref[...], d_self, mixed_ref[...])
    put_blocks(keep_ref, send_ref, 0, me, lambda s: t_mm(quarter_of(low, me, s, 128), e_first))
    put_blocks(keep_ref, send_ref, 128, me, lambda s: t_mm(quarter_of(hid, me, s, 128), dq_ref[...]))
    sums[...] = sums_ref[...]
    sums[2:3, :width] = gain_one
    sums[5:6, :width] = bias_one
    quarter = sums_ref.shape[1] // 4

    def small_block(slot):
        top = quarter_of(sums, me, slot, quarter)
        rest = quarter_of(sums, me, slot, 128)
        rest = jnp.concatenate([rest, jnp.zeros((8, quarter - 128), F32)], axis=1)
        row = lax.broadcasted_iota(jnp.int32, (8, 1), 0)
        return jnp.concatenate(
            [jnp.where(row == 0, top, rest), jnp.zeros((120, quarter), F32)], axis=0
        )

    put_blocks(keep_ref, send_ref, 256, me, small_block)


def self_query_kernel(
    blocks, order, scal, q_ref, pay_ref, kv_ref, x_ref, d_first_ref, masked_ref, next_ref, g_ref,
    keep_in, send_in, *refs
):
    g1, g3 = refs[0:4], refs[4:8]
    part_ref, slots_ref, keep_ref, send_ref = refs[8:12]
    wq, ws, paired, acc, kext, sems = refs[12:]
    me, live, base, here = scal[0], scal[1], scal[2], scal[5]
    block = pl.program_id(0)
    n_rows, width = x_ref.shape
    before = keep_in.shape[1]

    def begin():
        fetch = Fetch(me, sems)
        c_q = fetch.rows(g1, 0, width, wq)
        c_s = fetch.rows(g3, 2 * HIDDEN_QUARTER * 4, width, ws, 256)
        masked = masked_ref[...]
        paired[:, :width] = masked
        paired[:, width:] = jnp.concatenate([masked[1:], next_ref[0:1, :]], axis=0)
        places = base + lax.broadcasted_iota(jnp.int32, (n_rows, 1), 0)
        keep_ref[:, :before, :] = keep_in[...]
        send_ref[:, :before, :] = send_in[...]
        put_blocks(
            keep_ref, send_ref, before, me, lambda s: t_mm(quarter_of(paired, me, s, 256), g_ref[...])
        )
        wait(c_s)
        slots_ref[...] = jnp.where(places < live, mm(paired[...], ws[...]), 0.0).astype(BF)
        wait(c_q)

    first_last(blocks, block, "first", begin)
    fill_ext(kext, block * (kext.shape[0] // n_rows), n_rows, here, live, order)

    def add_pair(pair, value):
        at = pair_slice(pair)
        if blocks > 1:
            value = value + jnp.where(block == 0, 0.0, acc[:, at])
        acc[:, at] = value

    attend_query_back(q_ref, pay_ref, kv_ref, kext, add_pair)

    def finish():
        dq = (acc[...] * 0.125).astype(BF)
        part_ref[...] = d_first_ref[...] + mm_t(dq, wq[...])
        put_blocks(
            keep_ref, send_ref, before + 256, me,
            lambda s: t_mm(quarter_of(x_ref, me, s, 128), dq),
        )

    first_last(blocks, block, "last", finish)


def key_kernel(blocks, queries, first, mask, counts, scal, x_ref, *refs):
    n_q, n_pay, n_part = counts
    qs, pays = refs[:n_q], refs[n_q : n_q + n_pay]
    refs = refs[n_q + n_pay :]
    part = refs[:n_part]
    group = refs[n_part : n_part + 4]
    grad_ref, keep_ref, send_ref = refs[n_part + 4 : n_part + 7]
    wkv, wq, kv, acc, low, q_all, pay_all, sems = refs[n_part + 7 :]
    me, live, base = scal[0], scal[mask], scal[mask + 1]
    block = pl.program_id(0)
    n_rows, width = x_ref.shape
    fetch = Fetch(me, sems)
    c_q = fetch.shards(qs, q_all, block)
    c_pay = fetch.shards(pays, pay_all, block)

    def begin():
        c_w = fetch.rows(group, first, 2 * width, wkv)
        if queries:
            c_w += fetch.rows(group, 0, width, wq)
        wait(c_w)
        kv[...] = mm(x_ref[...], wkv[...]).astype(BF)

    first_last(blocks, block, "first", begin)
    wait(c_q)
    if queries:
        q_all[...] = (mm(q_all[...], wq[...]).astype(BF).astype(F32) * 0.125).astype(BF)
    wait(c_pay)

    def add_pair(pair, d_key, d_value):
        at_key, at_value = pair_slice(pair), pair_slice(pair + width // 128)
        if blocks > 1:
            d_key = d_key + jnp.where(block == 0, 0.0, acc[:, at_key])
            d_value = d_value + jnp.where(block == 0, 0.0, acc[:, at_value])
            acc[:, at_key] = d_key
            acc[:, at_value] = d_value
        usable = base + lax.broadcasted_iota(jnp.int32, (n_rows, 1), 0) < live
        low[:, at_key] = jnp.where(usable, d_key, 0.0).astype(BF)
        low[:, at_value] = jnp.where(usable, d_value, 0.0).astype(BF)

    attend_key_back(kv, q_all, pay_all, add_pair)

    def finish():
        value = mm_t(low[...], wkv[...])
        grad_ref[...] = part[0][...] + value if n_part else value
        put_blocks(keep_ref, send_ref, 0, me, lambda s: t_mm(quarter_of(x_ref, me, s, 128), low[...]))

    first_last(blocks, block, "last", finish)


def assemble_kernel(layout, full, scal, line, other, *refs):
    outs, whole_ref, sems = refs[:-2], refs[-2], refs[-1]
    here = scal[5]
    rows = whole_ref.shape[0]
    copies = []
    for i, ref in enumerate((line, other)):
        x = jnp.bitwise_xor(lax.rem(here, 2), i)
        for k in range(1 if full else 4):
            if full:
                tall, source = rows // 2, ref
                at = pl.multiple_of(x * tall, 16)
            else:
                tall, source = rows // 8, ref.at[k]
                z = jnp.bitwise_xor(lax.div(here, 2), k)
                at = pl.multiple_of(x * (rows // 2) + z * tall, 16)
            copy = pltpu.make_async_copy(source, whole_ref.at[pl.ds(at, tall)], sems.at[4 * i + k])
            copy.start()
            copies.append(copy)
    wait(copies)
    for (first, tall, parts), out in zip(layout, outs):
        for part in range(parts):
            at = first + part * tall
            out[:, 512 * part : 512 * (part + 1)] = whole_ref[at : at + tall, :].astype(F32)


def whole(array, buffers=None):
    rank = len(array.shape)
    return pl.BlockSpec(tuple(array.shape), lambda *_: (0,) * rank)


def by_rows(array, rows):
    return pl.BlockSpec((rows, array.shape[1]), lambda i: (i, 0))


ANY = pl.BlockSpec(memory_space=pltpu.HBM)
SMEM = pl.BlockSpec(memory_space=pltpu.SMEM)


def shape(dims, dtype):
    return jax.ShapeDtypeStruct(dims, dtype)


def call(kernel, name, grid, args, specs, outs, out_specs, scratch, copies, flops, moved):
    return pl.pallas_call(
        kernel,
        name=name,
        grid=(grid,),
        in_specs=specs,
        out_specs=out_specs,
        out_shape=outs,
        scratch_shapes=[*scratch] + ([pltpu.SemaphoreType.DMA((copies,))] if copies else []),
        compiler_params=pltpu.CompilerParams(
            vmem_limit_bytes=GRANTS.get(name, 28) * 2**20, dimension_semantics=("arbitrary",)
        ),
        cost_estimate=pl.CostEstimate(
            flops=12 * COST, bytes_accessed=moved // 64, transcendentals=0
        ),
    )(*args)


def vm(dims, dtype):
    return pltpu.VMEM(dims, dtype)


def grad_outs(rows):
    return (shape((2, rows, 512), F32), shape((2, rows, 512), BF))


def permute(value, axis, target):
    n = lax.axis_size(axis)
    pairs = [(i, target(i)) for i in range(n) if 0 <= target(i) < n]
    return lax.ppermute(value, axis, pairs)


def flip(value, axis, bits):
    return permute(value, axis, lambda i: i ^ bits)


def rows_of(ctx, gathered):
    return [a.reshape(-1, a.shape[-1]) for a in gathered]


def gather_line(value):
    return [value] + [flip(value, "ctx", bits) for bits in (2, 4, 6)]


def across_ctx(item):
    return flip(item, "ctx", 1)


def after(value, *others):
    return lax.optimization_barrier((value, *others))[0]


def gather_wsh(group):
    own = group
    across = flip(own, "wsh", 2)
    return (own, flip(own, "wsh", 1), across, flip(across, "wsh", 1))


def part_of(array, index, count):
    rows = array.shape[0] // count
    return lax.dynamic_slice_in_dim(array, index * rows, rows, 0)


class Clock:
    def __init__(self):
        self.last = None

    def __call__(self, *values):
        if self.last is None:
            return values
        return lax.optimization_barrier((*values, self.last))[:-1]

    def tick(self, value):
        self.last = value
        return value


class Total:
    def __init__(self, clock, name, scal, layout, keep, send, full=False):
        self.clock, self.name, self.scal, self.layout = clock, name, scal, layout
        self.keep, self.full = keep, full
        self.got = flip(send, "wsh", 1)
        self.ctx = lax.axis_size("ctx") == 8

    def across(self):
        keep, got = self.clock(self.keep, self.got)
        half = keep + got.astype(F32)
        out = self.clock.tick(half[1].astype(BF))
        self.own, self.got = half[0], flip(out, "wsh", 2)

    def side(self):
        if not self.ctx:
            return
        x = lax.axis_index("ctx") % 2
        own, got = self.clock(self.own, self.got)
        self.mine = part_of(own, x, 2) + part_of(got, x, 2).astype(F32)
        out = (part_of(own, 1 - x, 2) + part_of(got, 1 - x, 2).astype(F32)).astype(BF)
        self.got = flip(self.clock.tick(out), "ctx", 1)

    def spread(self):
        if not self.ctx:
            return
        z = lax.axis_index("ctx") // 2
        mine, got = self.clock(self.mine, self.got)
        mine = mine + got.astype(F32)
        low = mine.astype(BF)
        if self.full:
            low = self.clock.tick(low)
            self.mine = low.astype(F32)
            self.got = [flip(low, "ctx", 2 * k) for k in (1, 2, 3)]
            return
        out = [part_of(low, z ^ k, 4) for k in (1, 2, 3)]
        self.clock.tick(out[0])
        self.mine = part_of(mine, z, 4)
        self.got = [flip(out[k - 1], "ctx", 2 * k) for k in (1, 2, 3)]

    def collect(self):
        if not self.ctx:
            return
        mine, *came = self.clock(self.mine, *self.got)
        came = [item.astype(F32) for item in came]
        piece = self.clock.tick(((mine + came[0]) + (came[1] + came[2])).astype(BF))
        if self.full:
            self.got = [piece, flip(piece, "ctx", 1)]
        else:
            self.got = [piece] + [flip(piece, "ctx", 2 * k) for k in (1, 2, 3)]

    def line(self):
        if self.ctx and not self.full:
            line = self.clock.tick(jnp.stack(self.clock(*self.got)))
            self.got = [line, flip(line, "ctx", 1)]

    def finish(self):
        layout = self.layout
        if not self.ctx:
            summed = lax.psum((self.own + self.got.astype(F32)).astype(BF), "ctx").astype(F32)
            return [
                jnp.concatenate(
                    [summed[first + i * tall : first + (i + 1) * tall] for i in range(parts)],
                    axis=1,
                )
                for first, tall, parts in layout
            ]
        line, other = self.clock(*self.got)
        rows = self.own.shape[0]
        outs = tuple(shape((tall, 512 * parts), F32) for _, tall, parts in layout)
        result = call(
            functools.partial(assemble_kernel, layout, self.full), self.name, 1,
            (self.scal, line, other), [SMEM, ANY, ANY], outs,
            tuple(pl.BlockSpec(o.shape, lambda i: (0, 0)) for o in outs),
            [vm((rows, 512), BF)], 8, 2, rows * 4096,
        )
        self.clock.tick(result[0])
        return result


def shards(
    decoder_in,
    memory,
    seq_lengths,
    mem_lengths,
    self_query,
    self_keyval,
    self_out,
    cross_query,
    cross_keyval,
    cross_out,
    ffn_in,
    ffn_bias_in,
    ffn_out,
    ffn_bias_out,
    slot_weight,
    norm_gain,
    norm_bias,
    cotangent,
):
    tokens, mem_rows, cot = decoder_in[0], memory[0], cotangent[0]
    n_rows, width = tokens.shape
    n_mem = mem_rows.shape[0]
    hidden_units = ffn_in.shape[1]
    ctx = lax.axis_size("ctx")
    here, me = lax.axis_index("ctx"), lax.axis_index("wsh")
    n_keys, all_mem = ctx * n_rows, ctx * n_mem
    blocks = max(1, n_keys // 1536)
    step = n_keys // blocks

    def blocks_of(array, count):
        tall = array.shape[0] // count
        return [array[i * tall : (i + 1) * tall] for i in range(count)]

    small = jnp.concatenate(
        [ffn_bias_in.reshape(4, 128), ffn_bias_out.reshape(1, 128), norm_gain, norm_bias,
         jnp.zeros((5, 128), BF)],
        axis=0,
    )
    small = jnp.concatenate([small, jnp.zeros((16, 3 * width - 128), BF)], axis=1)
    group1 = jnp.concatenate([jnp.concatenate([self_query, self_keyval], axis=1), small], axis=0)
    group2 = jnp.concatenate([self_out, cross_query, cross_keyval, cross_out], axis=1)
    group3 = jnp.concatenate(
        [ffn_in, *blocks_of(ffn_out, hidden_units // 512), *blocks_of(slot_weight, 2)], axis=1
    )
    split = ctx == 8
    clock = Clock()
    g1 = gather_wsh(group1)
    if split:
        tokens_in = after(tokens, group1)
        both = after(jnp.concatenate([tokens, mem_rows], axis=0), group1)
        line = [tokens_in, flip(both, "ctx", 2), flip(tokens_in, "ctx", 4), flip(tokens_in, "ctx", 6)]
        toks = line + [across_ctx(both)] + [across_ctx(item) for item in line[1:]]
    else:
        toks = [lax.all_gather(tokens, "ctx", axis=0, tiled=True)]
    y2 = flip(after(group2, g1[2]), "wsh", 2)
    c2 = flip(group2, "wsh", 1)
    y3 = flip(after(group3, y2, toks[-1]), "wsh", 2)
    if split:
        mem_in = after(mem_rows, *toks[1:4])
        mem_line = [mem_rows, toks[1], flip(mem_in, "ctx", 4), flip(mem_in, "ctx", 6)]
        mem_side = [toks[4], toks[5]]
    prev_cot = permute(after(cot[-16:], y2), "ctx", lambda i: i + 1)

    live, mem_live = seq_lengths[0], mem_lengths[0]
    scal = jnp.stack(
        [me, live, here * n_rows, mem_live, here * n_mem, here, 0, 0]
    ).astype(jnp.int32)

    order = ORDER if ctx == 8 else None

    def fixed(*dims):
        return [pl.BlockSpec(d, lambda i, r=len(d): (0,) * r) for d in dims]

    tall, pay_w = (n_rows, width), (n_rows, width + EXT)
    pair_rows = (HEADS // 2, 2 * n_rows)
    by_block = pl.BlockSpec((step, 2 * width), lambda i: (i, 0))
    g2 = (group2, c2, y2, flip(y2, "wsh", 1))
    c3 = flip(after(group3, y2), "wsh", 1)
    tokens_now, *toks = clock(after(tokens, y2), *toks)
    kv, qs, self_ext, self_mixed = call(
        functools.partial(self_forward_kernel, blocks, order, len(toks)), "self_forward", blocks,
        (scal, tokens_now, *toks, *g1),
        [SMEM, whole(tokens)] + [ANY] * (len(toks) + 4),
        (shape((n_keys, 2 * width), BF), shape(tall, BF), shape((n_rows, EXT), BF),
         shape(tall, F32)),
        [by_block] + fixed(tall, (n_rows, EXT), tall),
        [vm((width, width), BF), vm((width, 2 * width), BF), vm((step, width), BF),
         vm((step, EXT), BF)]
        + ([vm((*pair_rows, 1), F32), vm((*pair_rows, 1), F32), vm((*pair_rows, 128), F32)]
           if blocks > 1 else [vm((8, 128), F32)] * 3),
        8 + len(toks), 11, 8 * 2**20,
    )
    clock.tick(qs)
    if split:
        mem_side += [across_ctx(clock(item)[0]) for item in mem_line[2:]]
        mems = mem_line + mem_side
    else:
        mems = [lax.all_gather(mem_rows, "ctx", axis=0, tiled=True)]
    self_mixed_now, *g2_now = clock(self_mixed, *g2)
    first_sum, cqs = call(
        self_dense_kernel, "self_dense", 1,
        (scal, tokens, self_mixed_now, *g1, *g2_now),
        [SMEM, whole(tokens), whole(self_mixed)] + [ANY] * 8,
        (shape(tall, F32), shape(tall, BF)), fixed(tall, tall),
        [vm((width, width), BF), vm((width, width), BF), vm((16, width), BF)],
        12, 2, 2 * 2**20,
    )
    clock.tick(cqs)
    y3 = after(y3, cqs)
    g3 = (group3, c3, y3, flip(y3, "wsh", 1))
    if split:
        cq_line = gather_line(after(cqs, *mem_line[1:]))
    (cqs_now, *mems_now) = clock(cqs, *mems)
    memkv, cross_ext, cross_mixed = call(
        functools.partial(cross_forward_kernel, order, len(mems)), "cross_forward", 1,
        (scal, cqs_now, *mems_now, *g2),
        [SMEM, whole(cqs)] + [ANY] * (len(mems) + 4),
        (shape((all_mem, 2 * width), BF), shape((n_rows, EXT), BF), shape(tall, F32)),
        fixed((all_mem, 2 * width), (n_rows, EXT), tall),
        [vm((width, 2 * width), BF), vm((all_mem, width), BF), vm((all_mem, EXT), BF)],
        4 + len(mems), 12, 8 * 2**20,
    )
    clock.tick(cross_ext)
    if split:
        cq_line = clock.tick(jnp.concatenate(clock(*cq_line), axis=0))
        all_cq = [cq_line, across_ctx(cq_line)]
    else:
        all_cq = [lax.all_gather(cqs, "ctx", axis=0, tiled=True)]
    (cross_mixed_now, prev_now, *g3_now) = clock(cross_mixed, prev_cot, *g3)
    pay_dc, masked, grads, d_second, sums, keep_a, send_a = call(
        middle_kernel, "middle", 1,
        (scal, cross_mixed_now, cross_ext, first_sum, cot, prev_now, *g1, *g2, *g3_now),
        [SMEM] + [whole(a) for a in (cross_mixed, cross_ext, first_sum, cot, prev_cot)]
        + [ANY] * 12,
        (shape(pay_w, BF), shape(tall, BF), shape(tall, BF),
         shape(tall, F32), shape((8, hidden_units), F32), *grad_outs(1152)),
        fixed(pay_w, tall, tall, tall, (8, hidden_units), (2, 1152, 512), (2, 1152, 512)),
        [vm((width, width), BF), vm((width, hidden_units), BF),
         vm((hidden_units, width), BF), vm((2 * width, width), BF), vm((16, width), BF),
         vm(tall, BF), vm(tall, BF), vm((n_rows, hidden_units), BF)],
        40, 12, 20 * 2**20,
    )
    clock.tick(pay_dc)
    sum_a = Total(
        clock, "sum_a", scal,
        ((0, 512, 1), (512, 128, hidden_units // 512), (1024, 128, 1)), keep_a, send_a,
    )
    if split:
        dc_line = gather_line(pay_dc)
        dc_side = [across_ctx(pay_dc)]
    else:
        all_dc = [lax.all_gather(pay_dc, "ctx", axis=0, tiled=True)]
    next_row = permute(masked[:16], "ctx", lambda i: i - 1)
    (pay_dc_now,) = clock(pay_dc)
    (dq_cross,) = call(
        functools.partial(cross_query_kernel, order), "cross_query", 1,
        (scal, cqs, pay_dc_now, memkv),
        [SMEM] + [whole(a) for a in (cqs, pay_dc, memkv)],
        (shape(tall, BF),), tuple(fixed(tall)), [vm((all_mem, EXT), BF)], 0, 13, 5 * 2**20,
    )
    clock.tick(dq_cross)
    if split:
        dc_side += [across_ctx(clock(item)[0]) for item in dc_line[1:2]]
    sum_a.across()
    (dq_now,) = clock(dq_cross)
    d_first, pay_ds, keep_b, send_b = call(
        cross_dense_kernel, "cross_dense", 1,
        (scal, dq_now, first_sum, d_second, self_mixed, self_ext, sums, *g1, *g2),
        [SMEM]
        + [whole(a) for a in (dq_cross, first_sum, d_second, self_mixed, self_ext, sums)]
        + [ANY] * 8,
        (shape(tall, F32), shape(pay_w, BF), *grad_outs(384)),
        fixed(tall, pay_w, (2, 384, 512), (2, 384, 512)),
        [vm((width, width), BF), vm((width, width), BF), vm((16, width), BF),
         vm(tall, BF), vm(tall, BF), vm((8, hidden_units), F32)],
        12, 8, 6 * 2**20,
    )
    clock.tick(pay_ds)
    if split:
        ds_line = gather_line(pay_ds)
        dc_side += [across_ctx(clock(item)[0]) for item in dc_line[2:]]
        all_dc = dc_line + dc_side
    else:
        all_ds = [lax.all_gather(pay_ds, "ctx", axis=0, tiled=True)]
    pay_now, next_now = clock(pay_ds, next_row)
    part, slots, keep_b, send_b = call(
        functools.partial(self_query_kernel, blocks, order), "self_query", blocks,
        (scal, qs, pay_now, kv, tokens, d_first, masked, next_now, grads, keep_b, send_b, *g1, *g3),
        [SMEM, whole(qs), whole(pay_ds), by_block]
        + [whole(a) for a in (tokens, d_first, masked, next_row, grads, keep_b, send_b)] + [ANY] * 8,
        (shape(tall, F32), shape(tall, BF), *grad_outs(768)),
        fixed(tall, tall, (2, 768, 512), (2, 768, 512)),
        [vm((width, width), BF), vm((2 * width, width), BF), vm((n_rows, 2 * width), BF),
         vm(tall, F32), vm((step, EXT), BF)],
        12, 9, 8 * 2**20,
    )
    clock.tick(part)
    sum_b = Total(
        clock, "sum_b", scal,
        ((0, 128, 1), (128, 128, 1), (256, 8, 1), (384, 256, 1), (640, 128, 1)), keep_b, send_b,
    )
    if split:
        ds_side = [across_ctx(clock(item)[0]) for item in ds_line]
        all_ds = ds_line + ds_side

    def keys_back(name, x, queries, q_from, pays, extra, group, first, mask, cost):
        rows = x.shape[0]
        came = clock(*q_from, *pays)
        q_from, pays = came[: len(q_from)], came[len(q_from) :]
        result = call(
            functools.partial(
                key_kernel, blocks, queries, first, mask, (len(q_from), len(pays), len(extra))
            ),
            name, blocks,
            (scal, x, *q_from, *pays, *extra, *group),
            [SMEM, whole(x)] + [ANY] * (len(q_from) + len(pays)) + [whole(e) for e in extra]
            + [ANY] * 4,
            (shape((rows, width), F32), *grad_outs(256)),
            fixed((rows, width), (2, 256, 512), (2, 256, 512)),
            [vm((width, 2 * width), BF), vm((width, width) if queries else (16, 128), BF),
             vm((rows, 2 * width), BF),
             vm((rows, 2 * width) if blocks > 1 else (8, 128), F32), vm((rows, 2 * width), BF),
             vm((step, width), BF), vm((step, width + EXT), BF)],
            8 + len(q_from) + len(pays), cost, 8 * 2**20,
        )
        clock.tick(result[0])
        return result

    grad_mem, keep_m, send_m = keys_back(
        "cross_key", mem_rows, False, all_cq, all_dc, (), g2, 2 * width, 3, 12
    )
    sum_m = Total(clock, "sum_m", scal, ((0, 128, 2),), keep_m, send_m, True)
    sum_a.side()
    sum_b.across()
    sum_m.across()
    grad_input, keep_k, send_k = keys_back(
        "self_key", tokens, True, toks, all_ds, (part,), g1, width, 1, 11
    )
    sum_k = Total(clock, "sum_k", scal, ((0, 128, 2),), keep_k, send_k, True)
    sum_a.spread()
    sum_b.side()
    sum_k.across()
    sum_m.side()
    sum_a.collect()
    sum_b.spread()
    sum_k.side()
    sum_m.spread()
    sum_a.line()
    sum_b.collect()
    sum_k.spread()
    sum_m.collect()
    sum_b.line()
    sum_k.collect()
    g_second, g_first, g_cout = sum_a.finish()
    (g_ckv,) = sum_m.finish()
    g_out, g_cq, tiny, g_slot, g_q = sum_b.finish()
    (g_kv,) = sum_k.finish()
    return (
        slots[None],
        grad_input[None],
        grad_mem[None],
        g_q,
        g_kv,
        g_out,
        g_cq,
        g_ckv,
        g_cout,
        g_first,
        tiny[0],
        g_second,
        tiny[1, :128],
        g_slot,
        tiny[2:5, :128],
        tiny[5:8, :128],
    )


def solution(mesh):
    rows, split = P("wsh", "ctx", None), P("wsh", None)
    line, side = P("wsh"), P(None, "wsh")
    in_specs = (
        rows, rows, line, line, split, split, split, split, split, split, split, line, split, line,
        split, side, side, rows,
    )
    out_specs = (
        rows, rows, rows, split, split, split, split, split, split, split, line, split, line, split,
        side, side,
    )
    return jax.shard_map(shards, mesh=mesh, in_specs=in_specs, out_specs=out_specs, check_vma=False)
```

```python
import functools
import math

import jax
import jax.numpy as jnp
from jax import lax
from jax.experimental import pallas as pl
from jax.experimental.pallas import tpu as pltpu
from jax.sharding import PartitionSpec as P

HEADS = 8
NORM_EPS = 1e-05
DEAD = -1e30
EXT = 128
DEAD_LANE = 3 * HEADS
LSE_LANE = 32
ORDER = (0, 2, 4, 6, 1, 3, 5, 7)
BF = jnp.bfloat16
F32 = jnp.float32
COST = 10**9
GRANTS = {}


def mm(left, right):
    return lax.dot_general(left, right, (((1,), (0,)), ((), ())), preferred_element_type=F32)


def mm2(left, right):
    high = left.astype(BF)
    low = (left - high.astype(F32)).astype(BF)
    return mm(high, right) + mm(low, right)


def mm_t(left, right):
    return lax.dot_general(left, right, (((1,), (1,)), ((), ())), preferred_element_type=F32)


def t_mm(left, right):
    return lax.dot_general(left, right, (((0,), (0,)), ((), ())), preferred_element_type=F32)


def norm_stats(values):
    center = values - jnp.mean(values, axis=-1, keepdims=True)
    inverse = lax.rsqrt(jnp.mean(center * center, axis=-1, keepdims=True) + NORM_EPS)
    return center * inverse, inverse


def norm_back(grad_out, normed, inverse, gain_row):
    scaled = grad_out * gain_row
    grad_in = inverse * (
        scaled
        - jnp.mean(scaled, axis=-1, keepdims=True)
        - normed * jnp.mean(scaled * normed, axis=-1, keepdims=True)
    )
    return (
        grad_in,
        jnp.sum(grad_out * normed, axis=0, keepdims=True),
        jnp.sum(grad_out, axis=0, keepdims=True),
    )


def lanes(width=128):
    return lax.broadcasted_iota(jnp.int32, (1, width), 1)


def stack_pair(block):
    low = lanes() < 64
    zero = jnp.zeros_like(block)
    return jnp.concatenate([jnp.where(low, block, zero), jnp.where(low, zero, block)], axis=0)


def unstack_pair(stacked):
    n = stacked.shape[0] // 2
    return jnp.where(lanes() < 64, stacked[:n], stacked[n:])


def split3(value):
    high = value.astype(BF).astype(F32)
    rest = value - high
    mid = rest.astype(BF).astype(F32)
    return high, mid, (rest - mid).astype(BF).astype(F32)


def place3(table, column, lane):
    where = lanes()
    for term, part in enumerate(split3(column)):
        table = jnp.where(where == lane + term, part, table)
    return table


def pair_ext(table, pair, offset):
    where = lanes()
    other = jnp.where(where == DEAD_LANE, 1.0 if offset else 0.0, 0.0).astype(table.dtype)
    parts = []
    for head in (2 * pair, 2 * pair + 1):
        first = offset + 3 * head
        parts.append(jnp.where((where >= first) & (where < first + 3), table, other))
    return jnp.concatenate(parts, axis=0)


def ones_ext(rows, pair, offset):
    where = lanes()
    parts = []
    for head in (2 * pair, 2 * pair + 1):
        first = offset + 3 * head
        one = jnp.where((where >= first) & (where < first + 3), 1.0, 0.0)
        parts.append(jnp.broadcast_to(one, (rows, EXT)))
    return jnp.concatenate(parts, axis=0).astype(BF)


def add_delta(table, grad_low, mixed):
    product = grad_low.astype(F32) * mixed
    low = lanes() < 64
    table = table.astype(F32)
    for pair in range(HEADS // 2):
        block = product[:, 128 * pair : 128 * pair + 128]
        even = jnp.sum(jnp.where(low, block, 0.0), axis=1, keepdims=True)
        odd = jnp.sum(jnp.where(low, 0.0, block), axis=1, keepdims=True)
        table = place3(table, -even, 6 * pair)
        table = place3(table, -odd, 6 * pair + 3)
    return table.astype(BF)


def fill_ext(ext_ref, first, rows, here, limit, order):
    where = lanes()
    base = jnp.where(where == DEAD_LANE, 0.0, 1.0)
    for i in range(ext_ref.shape[0] // rows):
        device = jnp.bitwise_xor(here, order[i]) if order else first + i
        place = device * rows + lax.broadcasted_iota(jnp.int32, (rows, 1), 0)
        dead = (where == DEAD_LANE) & (place >= limit)
        ext_ref[i * rows : (i + 1) * rows, :] = jnp.where(dead, DEAD, base).astype(BF)


def pair_slice(pair):
    return pl.ds(pl.multiple_of(pair * 128, 128), 128)


def attend_forward(q_ref, kv_ref, kext_ref, mixed_ref, state, blocks, block):
    n_rows, width = q_ref.shape
    where = lanes()
    ext = jnp.broadcast_to(jnp.where(where == DEAD_LANE, 1.0, 0.0), (2 * n_rows, EXT)).astype(BF)
    kext = kext_ref[...]

    def one_pair(pair, table):
        q2 = jnp.concatenate([stack_pair(q_ref[:, pair_slice(pair)]), ext], axis=1)
        keys = jnp.concatenate([kv_ref[:, pair_slice(pair)], kext], axis=1)
        scores = mm_t(q2, keys)
        top = jnp.max(scores, axis=1, keepdims=True)
        if blocks > 1:
            before = jnp.where(block == 0, DEAD, state[0][pair])
            top = jnp.maximum(top, before)
        powers = jnp.exp(scores - top)
        total = jnp.sum(powers, axis=1, keepdims=True)
        mixed = mm2(powers, kv_ref[:, pair_slice(pair + width // 128)])
        if blocks > 1:
            fade = jnp.exp(before - top)
            total = total + fade * jnp.where(block == 0, 0.0, state[1][pair])
            mixed = mixed + fade * jnp.where(block == 0, 0.0, state[2][pair])
            state[0][pair] = top
            state[1][pair] = total
            state[2][pair] = mixed
        mixed_ref[:, pair_slice(pair)] = unstack_pair(mixed * (1.0 / total))
        lse = -(top + jnp.log(total))
        table = place3(table, lse[:n_rows], LSE_LANE + 6 * pair)
        return place3(table, lse[n_rows:], LSE_LANE + 6 * pair + 3)

    start = jnp.zeros((n_rows, EXT), F32)
    return lax.fori_loop(0, HEADS // 2, one_pair, start, unroll=True).astype(BF)


def attend_query_back(q_ref, pay_ref, kv_ref, kext_ref, add_pair):
    width = q_ref.shape[1]
    kext = kext_ref[...]
    ext = pay_ref[:, width:]

    def one_pair(pair, carry):
        keys = kv_ref[:, pair_slice(pair)]
        q2 = jnp.concatenate(
            [stack_pair(q_ref[:, pair_slice(pair)]), pair_ext(ext, pair, LSE_LANE)], axis=1
        )
        probs = jnp.exp(mm_t(q2, jnp.concatenate([keys, kext], axis=1)))
        do2 = jnp.concatenate(
            [stack_pair(pay_ref[:, pair_slice(pair)]), pair_ext(ext, pair, 0)], axis=1
        )
        values = kv_ref[:, pair_slice(pair + width // 128)]
        d_probs = mm_t(do2, jnp.concatenate([values, kext], axis=1))
        d_scores = (probs * d_probs).astype(BF)
        add_pair(pair, unstack_pair(mm(d_scores, keys)))
        return carry

    lax.fori_loop(0, HEADS // 2, one_pair, 0, unroll=True)


def attend_key_back(kv_ref, q_ref, pay_ref, add_pair):
    n_keys = kv_ref.shape[0]
    width = kv_ref.shape[1] // 2
    ext = pay_ref[:, width:]

    def one_pair(pair, carry):
        queries = q_ref[:, pair_slice(pair)]
        grads = pay_ref[:, pair_slice(pair)]
        k2 = jnp.concatenate(
            [stack_pair(kv_ref[:, pair_slice(pair)]), ones_ext(n_keys, pair, LSE_LANE)], axis=1
        )
        probs = jnp.exp(mm_t(k2, jnp.concatenate([queries, ext], axis=1)))
        v2 = jnp.concatenate(
            [stack_pair(kv_ref[:, pair_slice(pair + width // 128)]), ones_ext(n_keys, pair, 0)],
            axis=1,
        )
        d_probs = mm_t(v2, jnp.concatenate([grads, ext], axis=1))
        d_scores = (probs * d_probs).astype(BF)
        add_pair(pair, unstack_pair(mm(d_scores, queries)), unstack_pair(mm(probs.astype(BF), grads)))
        return carry

    lax.fori_loop(0, HEADS // 2, one_pair, 0, unroll=True)


class Fetch:
    def __init__(self, me, sems):
        self.me, self.sems, self.used = me, sems, 0

    def start(self, slots, source, target):
        copies = []
        for slot, ref in enumerate(slots):
            quarter = jnp.bitwise_xor(self.me, slot)
            copy = pltpu.make_async_copy(source(ref), target(quarter), self.sems.at[self.used])
            self.used += 1
            copy.start()
            copies.append(copy)
        return copies

    def rows(self, slots, first, width, ref, height=128):
        copies = []
        for part in range(height // 128):
            copies += self.start(
                slots,
                lambda s, part=part: s.at[pl.ds(0, 128), pl.ds(first + part * width, width)],
                lambda quarter, part=part: ref.at[
                    pl.ds(pl.multiple_of(quarter * height + part * 128, 128), 128)
                ],
            )
        return copies

    def shards(self, refs, ref, block=0, tail=False):
        copies = []
        if len(refs) == 1:
            tall = ref.shape[0]
            source = refs[0].at[pl.ds(pl.multiple_of(block * tall, 8), tall)]
            pieces = [(source, ref)]
        else:
            tall = ref.shape[0] // len(refs)
            pieces = [
                (
                    r.at[pl.ds(r.shape[0] - tall if tail else 0, tall)],
                    ref.at[pl.ds(i * tall, tall)],
                )
                for i, r in enumerate(refs)
            ]
        for source, target in pieces:
            copy = pltpu.make_async_copy(source, target, self.sems.at[self.used])
            self.used += 1
            copy.start()
            copies.append(copy)
        return copies

    def small(self, slots, ref):
        return self.start(
            slots,
            lambda s: s.at[pl.ds(128, 16), pl.ds(0, 128)],
            lambda quarter: ref.at[:, pl.ds(pl.multiple_of(quarter * 128, 128), 128)],
        )


def wait(copies):
    for copy in copies:
        copy.wait()


def quarter_of(ref, me, slot, width):
    start = pl.multiple_of(jnp.bitwise_xor(me, slot) * width, 128)
    return ref[:, pl.ds(start, width)]


KEPT = (0, 2)
SENT = (1, 3)


def put_blocks(keep_ref, send_ref, first, me, block_of):
    for target, slots in ((keep_ref, KEPT), (send_ref, SENT)):
        for place, slot in enumerate(slots):
            block = block_of(slot).astype(target.dtype)
            rows = block.shape[0]
            for part in range(block.shape[1] // 512):
                target[place, first + part * rows : first + (part + 1) * rows, :] = block[
                    :, 512 * part : 512 * (part + 1)
                ]


def small_row(small_ref, row):
    return small_ref[row : row + 1, :].astype(F32)


GAIN, BIAS = 5, 8
HIDDEN_QUARTER = 512


def first_last(blocks, block, at, what):
    if blocks > 1:
        pl.when(block == (0 if at == "first" else blocks - 1))(what)
    else:
        what()


def self_forward_kernel(blocks, order, n_tok, scal, x_ref, *refs):
    toks, g1 = refs[:n_tok], refs[n_tok : n_tok + 4]
    kv_ref, q_ref, ext_ref, mixed_ref = refs[n_tok + 4 : n_tok + 8]
    wq, wkv, tok, kext, m_st, l_st, a_st, sems = refs[n_tok + 8 :]
    me, live, here = scal[0], scal[1], scal[5]
    block = pl.program_id(0)
    n_rows, width = x_ref.shape
    fetch = Fetch(me, sems)
    c_tok = fetch.shards(toks, tok, block)

    def begin():
        c_q = fetch.rows(g1, 0, width, wq)
        c_kv = fetch.rows(g1, width, 2 * width, wkv)
        wait(c_q)
        q_ref[...] = (mm(x_ref[...], wq[...]).astype(BF).astype(F32) * 0.125).astype(BF)
        wait(c_kv)

    first_last(blocks, block, "first", begin)
    fill_ext(kext, block * (tok.shape[0] // n_rows), n_rows, here, live, order)
    wait(c_tok)
    kv_ref[...] = mm(tok[...], wkv[...]).astype(BF)
    table = attend_forward(q_ref, kv_ref, kext, mixed_ref, (m_st, l_st, a_st), blocks, block)

    def finish():
        ext_ref[...] = table

    first_last(blocks, block, "last", finish)


def self_dense_kernel(scal, x_ref, mixed_ref, *refs):
    g1, g2 = refs[0:4], refs[4:8]
    sum_ref, cq_ref = refs[8:10]
    wo, wc, small, sems = refs[10:]
    width = x_ref.shape[1]
    fetch = Fetch(scal[0], sems)
    c_o = fetch.rows(g2, 0, width, wo)
    c_rest = fetch.small(g1, small)
    c_rest += fetch.rows(g2, width, width, wc)
    wait(c_o)
    first = x_ref[...].astype(F32) + mm(mixed_ref[...].astype(BF), wo[...])
    sum_ref[...] = first
    wait(c_rest)
    normed, _ = norm_stats(first)
    hidden = normed * small_row(small, GAIN) + small_row(small, BIAS)
    cq = mm(hidden.astype(BF), wc[...]).astype(BF)
    cq_ref[...] = (cq.astype(F32) * 0.125).astype(BF)


def gelu_parts(value):
    coef = math.sqrt(2.0 / math.pi)
    square = value * value
    inner = coef * (value + 0.044715 * value * square)
    bend = jnp.tanh(inner)
    half = 0.5 * (1.0 + bend)
    slope = half + 0.5 * value * (1.0 - bend * bend) * coef * (1.0 + 3 * 0.044715 * square)
    return value * half, slope


def cross_forward_kernel(order, n_mem, scal, cq_ref, *refs):
    mems, g2 = refs[:n_mem], refs[n_mem : n_mem + 4]
    kv_ref, ext_ref, mixed_ref = refs[n_mem + 4 : n_mem + 7]
    wkv, mem, kext, sems = refs[n_mem + 7 :]
    me, live, here = scal[0], scal[3], scal[5]
    width = cq_ref.shape[1]
    fetch = Fetch(me, sems)
    c_kv = fetch.rows(g2, 2 * width, 2 * width, wkv)
    c_mem = fetch.shards(mems, mem, 0, True)
    fill_ext(kext, 0, scal_rows(mem, order), here, live, order)
    wait(c_kv)
    wait(c_mem)
    kv_ref[...] = mm(mem[...], wkv[...]).astype(BF)
    ext_ref[...] = attend_forward(cq_ref, kv_ref, kext, mixed_ref, None, 1, 0)


def scal_rows(array, order):
    return array.shape[0] // len(order) if order else array.shape[0]


def middle_kernel(scal, mixed_ref, ext_ref, sum_ref, cot_ref, prev_ref, *refs):
    g1, g2, g3 = refs[0:4], refs[4:8], refs[8:12]
    pay_ref, masked_ref, g_ref, second_ref, sums_ref, keep_ref, send_ref = refs[12:19]
    wo, w1, w2, ws, small, low, hid, act, sems = refs[19:]
    me, live, base = scal[0], scal[1], scal[2]
    n_rows, width = sum_ref.shape
    hidden_units = w1.shape[1]
    fetch = Fetch(me, sems)
    c_small = fetch.small(g1, small)
    c_o = fetch.rows(g2, 4 * width, width, wo)
    c_1 = fetch.rows(g3, 0, hidden_units, w1)
    c_2 = fetch.rows(g3, hidden_units, width, w2, hidden_units // 4)
    c_s = fetch.rows(g3, 2 * hidden_units, width, ws, 256)
    low[...] = mixed_ref[...].astype(BF)
    wait(c_small)
    wait(c_o)
    normed, _ = norm_stats(sum_ref[...])
    hidden_one = normed * small_row(small, GAIN) + small_row(small, BIAS)
    second = hidden_one + mm(low[...], wo[...])
    normed_two, inverse_two = norm_stats(second)
    hidden_two = normed_two * small_row(small, GAIN + 1) + small_row(small, BIAS + 1)
    hid[...] = hidden_two.astype(BF)
    bias_in = jnp.concatenate(
        [
            small[r : r + 1, 128 * j : 128 * j + 128].astype(F32)
            for j in range(4)
            for r in range(4)
        ],
        axis=1,
    )
    wait(c_1)
    preact = mm(hid[...], w1[...]) + bias_in
    active, slope = gelu_parts(preact)
    act[...] = active.astype(BF)
    wait(c_2)
    third = hidden_two + mm(act[...], w2[...]) + small_row(small, 4)
    normed_three, inverse_three = norm_stats(third)
    hidden_three = normed_three * small_row(small, GAIN + 2) + small_row(small, BIAS + 2)
    places = base + lax.broadcasted_iota(jnp.int32, (n_rows, 1), 0)
    valid = places < live
    masked_ref[...] = jnp.where(valid, hidden_three, 0.0).astype(BF)

    grads = jnp.where(valid, cot_ref[...].astype(F32), 0.0).astype(BF)
    g_ref[...] = grads
    wait(c_s)
    d_own = mm_t(grads, ws[:width, :])
    before = jnp.where(base - 1 < live, prev_ref[15:16, :].astype(F32), 0.0).astype(BF)
    shifted = jnp.concatenate([before, grads[:-1]], axis=0)
    d_next = mm_t(shifted, ws[width:, :])
    d_three = jnp.where(valid, d_own + d_next, 0.0)
    d_third, gain_three, bias_three = norm_back(
        d_three, normed_three, inverse_three, small_row(small, GAIN + 2)
    )
    e_third = d_third.astype(BF)
    d_pre = (mm_t(e_third, w2[...]) * slope).astype(BF)
    d_two = d_third + mm_t(d_pre, w1[...])
    d_second, gain_two, bias_two = norm_back(
        d_two, normed_two, inverse_two, small_row(small, GAIN + 1)
    )
    second_ref[...] = d_second
    e_second = d_second.astype(BF)
    d_cross = mm_t(e_second, wo[...]).astype(BF)
    pay_ref[:, :width] = d_cross
    pay_ref[:, width:] = add_delta(ext_ref[...], d_cross, mixed_ref[...])
    sums_ref[...] = jnp.zeros_like(sums_ref)
    sums_ref[0:1, :] = jnp.sum(d_pre.astype(F32), axis=0, keepdims=True)
    sums_ref[1:2, :width] = jnp.sum(e_third.astype(F32), axis=0, keepdims=True)
    sums_ref[3:4, :width] = gain_two
    sums_ref[4:5, :width] = gain_three
    sums_ref[6:7, :width] = bias_two
    sums_ref[7:8, :width] = bias_three
    put_blocks(
        keep_ref, send_ref, 0, me, lambda s: t_mm(quarter_of(act, me, s, hidden_units // 4), e_third)
    )
    put_blocks(keep_ref, send_ref, 512, me, lambda s: t_mm(quarter_of(hid, me, s, 128), d_pre))
    put_blocks(keep_ref, send_ref, 1024, me, lambda s: t_mm(quarter_of(low, me, s, 128), e_second))


def cross_query_kernel(order, scal, cq_ref, pay_ref, kv_ref, dq_ref, kext):
    live, here = scal[3], scal[5]
    fill_ext(kext, 0, scal_rows(kext, order), here, live, order)

    def add_pair(pair, value):
        dq_ref[:, pair_slice(pair)] = (value * 0.125).astype(BF)

    attend_query_back(cq_ref, pay_ref, kv_ref, kext, add_pair)


def cross_dense_kernel(scal, dq_ref, sum_ref, second_ref, mixed_ref, ext_ref, sums_ref, *refs):
    g1, g2 = refs[0:4], refs[4:8]
    d_first_ref, pay_ref, keep_ref, send_ref = refs[8:12]
    wo, wc, small, low, hid, sums, sems = refs[12:]
    me = scal[0]
    width = sum_ref.shape[1]
    fetch = Fetch(me, sems)
    c_c = fetch.rows(g2, width, width, wc)
    c_small = fetch.small(g1, small)
    c_o = fetch.rows(g2, 0, width, wo)
    wait(c_small)
    normed, inverse = norm_stats(sum_ref[...])
    hid[...] = (normed * small_row(small, GAIN) + small_row(small, BIAS)).astype(BF)
    low[...] = mixed_ref[...].astype(BF)
    wait(c_c)
    d_one = second_ref[...] + mm_t(dq_ref[...], wc[...])
    d_first, gain_one, bias_one = norm_back(d_one, normed, inverse, small_row(small, GAIN))
    d_first_ref[...] = d_first
    e_first = d_first.astype(BF)
    wait(c_o)
    d_self = mm_t(e_first, wo[...]).astype(BF)
    pay_ref[:, :width] = d_self
    pay_ref[:, width:] = add_delta(ext_ref[...], d_self, mixed_ref[...])
    put_blocks(keep_ref, send_ref, 0, me, lambda s: t_mm(quarter_of(low, me, s, 128), e_first))
    put_blocks(keep_ref, send_ref, 128, me, lambda s: t_mm(quarter_of(hid, me, s, 128), dq_ref[...]))
    sums[...] = sums_ref[...]
    sums[2:3, :width] = gain_one
    sums[5:6, :width] = bias_one
    quarter = sums_ref.shape[1] // 4

    def small_block(slot):
        top = quarter_of(sums, me, slot, quarter)
        rest = quarter_of(sums, me, slot, 128)
        rest = jnp.concatenate([rest, jnp.zeros((8, quarter - 128), F32)], axis=1)
        row = lax.broadcasted_iota(jnp.int32, (8, 1), 0)
        return jnp.concatenate(
            [jnp.where(row == 0, top, rest), jnp.zeros((120, quarter), F32)], axis=0
        )

    put_blocks(keep_ref, send_ref, 256, me, small_block)


def self_query_kernel(
    blocks, order, scal, q_ref, pay_ref, kv_ref, x_ref, d_first_ref, masked_ref, next_ref, g_ref,
    keep_in, send_in, *refs
):
    g1, g3 = refs[0:4], refs[4:8]
    part_ref, slots_ref, keep_ref, send_ref = refs[8:12]
    wq, ws, paired, acc, kext, sems = refs[12:]
    me, live, base, here = scal[0], scal[1], scal[2], scal[5]
    block = pl.program_id(0)
    n_rows, width = x_ref.shape
    before = keep_in.shape[1]

    def begin():
        fetch = Fetch(me, sems)
        c_q = fetch.rows(g1, 0, width, wq)
        c_s = fetch.rows(g3, 2 * HIDDEN_QUARTER * 4, width, ws, 256)
        masked = masked_ref[...]
        paired[:, :width] = masked
        paired[:, width:] = jnp.concatenate([masked[1:], next_ref[0:1, :]], axis=0)
        places = base + lax.broadcasted_iota(jnp.int32, (n_rows, 1), 0)
        keep_ref[:, :before, :] = keep_in[...]
        send_ref[:, :before, :] = send_in[...]
        put_blocks(
            keep_ref, send_ref, before, me, lambda s: t_mm(quarter_of(paired, me, s, 256), g_ref[...])
        )
        wait(c_s)
        slots_ref[...] = jnp.where(places < live, mm(paired[...], ws[...]), 0.0).astype(BF)
        wait(c_q)

    first_last(blocks, block, "first", begin)
    fill_ext(kext, block * (kext.shape[0] // n_rows), n_rows, here, live, order)

    def add_pair(pair, value):
        at = pair_slice(pair)
        if blocks > 1:
            value = value + jnp.where(block == 0, 0.0, acc[:, at])
        acc[:, at] = value

    attend_query_back(q_ref, pay_ref, kv_ref, kext, add_pair)

    def finish():
        dq = (acc[...] * 0.125).astype(BF)
        part_ref[...] = d_first_ref[...] + mm_t(dq, wq[...])
        put_blocks(
            keep_ref, send_ref, before + 256, me,
            lambda s: t_mm(quarter_of(x_ref, me, s, 128), dq),
        )

    first_last(blocks, block, "last", finish)


def key_kernel(blocks, queries, first, mask, counts, scal, x_ref, *refs):
    n_q, n_pay, n_part = counts
    qs, pays = refs[:n_q], refs[n_q : n_q + n_pay]
    refs = refs[n_q + n_pay :]
    part = refs[:n_part]
    group = refs[n_part : n_part + 4]
    grad_ref, keep_ref, send_ref = refs[n_part + 4 : n_part + 7]
    wkv, wq, kv, acc, low, q_all, pay_all, sems = refs[n_part + 7 :]
    me, live, base = scal[0], scal[mask], scal[mask + 1]
    block = pl.program_id(0)
    n_rows, width = x_ref.shape
    fetch = Fetch(me, sems)
    c_q = fetch.shards(qs, q_all, block)
    c_pay = fetch.shards(pays, pay_all, block)

    def begin():
        c_w = fetch.rows(group, first, 2 * width, wkv)
        if queries:
            c_w += fetch.rows(group, 0, width, wq)
        wait(c_w)
        kv[...] = mm(x_ref[...], wkv[...]).astype(BF)

    first_last(blocks, block, "first", begin)
    wait(c_q)
    if queries:
        q_all[...] = (mm(q_all[...], wq[...]).astype(BF).astype(F32) * 0.125).astype(BF)
    wait(c_pay)

    def add_pair(pair, d_key, d_value):
        at_key, at_value = pair_slice(pair), pair_slice(pair + width // 128)
        if blocks > 1:
            d_key = d_key + jnp.where(block == 0, 0.0, acc[:, at_key])
            d_value = d_value + jnp.where(block == 0, 0.0, acc[:, at_value])
            acc[:, at_key] = d_key
            acc[:, at_value] = d_value
        usable = base + lax.broadcasted_iota(jnp.int32, (n_rows, 1), 0) < live
        low[:, at_key] = jnp.where(usable, d_key, 0.0).astype(BF)
        low[:, at_value] = jnp.where(usable, d_value, 0.0).astype(BF)

    attend_key_back(kv, q_all, pay_all, add_pair)

    def finish():
        value = mm_t(low[...], wkv[...])
        grad_ref[...] = part[0][...] + value if n_part else value
        put_blocks(keep_ref, send_ref, 0, me, lambda s: t_mm(quarter_of(x_ref, me, s, 128), low[...]))

    first_last(blocks, block, "last", finish)


def assemble_kernel(layout, full, scal, line, other, *refs):
    outs, whole_ref, sems = refs[:-2], refs[-2], refs[-1]
    here = scal[5]
    rows = whole_ref.shape[0]
    copies = []
    for i, ref in enumerate((line, other)):
        x = jnp.bitwise_xor(lax.rem(here, 2), i)
        for k in range(1 if full else 4):
            if full:
                tall, source = rows // 2, ref
                at = pl.multiple_of(x * tall, 16)
            else:
                tall, source = rows // 8, ref.at[k]
                z = jnp.bitwise_xor(lax.div(here, 2), k)
                at = pl.multiple_of(x * (rows // 2) + z * tall, 16)
            copy = pltpu.make_async_copy(source, whole_ref.at[pl.ds(at, tall)], sems.at[4 * i + k])
            copy.start()
            copies.append(copy)
    wait(copies)
    for (first, tall, parts), out in zip(layout, outs):
        for part in range(parts):
            at = first + part * tall
            out[:, 512 * part : 512 * (part + 1)] = whole_ref[at : at + tall, :].astype(F32)


def whole(array, buffers=None):
    rank = len(array.shape)
    return pl.BlockSpec(tuple(array.shape), lambda *_: (0,) * rank)


def by_rows(array, rows):
    return pl.BlockSpec((rows, array.shape[1]), lambda i: (i, 0))


ANY = pl.BlockSpec(memory_space=pltpu.HBM)
SMEM = pl.BlockSpec(memory_space=pltpu.SMEM)


def shape(dims, dtype):
    return jax.ShapeDtypeStruct(dims, dtype)


def call(kernel, name, grid, args, specs, outs, out_specs, scratch, copies, flops, moved):
    return pl.pallas_call(
        kernel,
        name=name,
        grid=(grid,),
        in_specs=specs,
        out_specs=out_specs,
        out_shape=outs,
        scratch_shapes=[*scratch] + ([pltpu.SemaphoreType.DMA((copies,))] if copies else []),
        compiler_params=pltpu.CompilerParams(
            vmem_limit_bytes=GRANTS.get(name, 28) * 2**20, dimension_semantics=("arbitrary",)
        ),
        cost_estimate=pl.CostEstimate(
            flops=12 * COST, bytes_accessed=moved // 64, transcendentals=0
        ),
    )(*args)


def vm(dims, dtype):
    return pltpu.VMEM(dims, dtype)


def grad_outs(rows):
    return (shape((2, rows, 512), F32), shape((2, rows, 512), BF))


def permute(value, axis, target):
    n = lax.axis_size(axis)
    pairs = [(i, target(i)) for i in range(n) if 0 <= target(i) < n]
    return lax.ppermute(value, axis, pairs)


def flip(value, axis, bits):
    return permute(value, axis, lambda i: i ^ bits)


def rows_of(ctx, gathered):
    return [a.reshape(-1, a.shape[-1]) for a in gathered]


def gather_line(value):
    return [value] + [flip(value, "ctx", bits) for bits in (2, 4, 6)]


def across_ctx(item):
    return flip(item, "ctx", 1)


def after(value, *others):
    return lax.optimization_barrier((value, *others))[0]


def gather_wsh(group):
    own = group
    across = flip(own, "wsh", 2)
    return (own, flip(own, "wsh", 1), across, flip(across, "wsh", 1))


def part_of(array, index, count):
    rows = array.shape[0] // count
    return lax.dynamic_slice_in_dim(array, index * rows, rows, 0)


class Clock:
    def __init__(self):
        self.last = None

    def __call__(self, *values):
        if self.last is None:
            return values
        return lax.optimization_barrier((*values, self.last))[:-1]

    def tick(self, value):
        self.last = value
        return value


class Total:
    def __init__(self, clock, name, scal, layout, keep, send, full=False):
        self.clock, self.name, self.scal, self.layout = clock, name, scal, layout
        self.keep, self.full = keep, full
        self.got = flip(send, "wsh", 1)
        self.ctx = lax.axis_size("ctx") == 8

    def across(self):
        keep, got = self.clock(self.keep, self.got)
        half = keep + got.astype(F32)
        out = self.clock.tick(half[1].astype(BF))
        self.own, self.got = half[0], flip(out, "wsh", 2)

    def side(self):
        if not self.ctx:
            return
        x = lax.axis_index("ctx") % 2
        own, got = self.clock(self.own, self.got)
        self.mine = part_of(own, x, 2) + part_of(got, x, 2).astype(F32)
        out = (part_of(own, 1 - x, 2) + part_of(got, 1 - x, 2).astype(F32)).astype(BF)
        self.got = flip(self.clock.tick(out), "ctx", 1)

    def spread(self):
        if not self.ctx:
            return
        z = lax.axis_index("ctx") // 2
        mine, got = self.clock(self.mine, self.got)
        mine = mine + got.astype(F32)
        low = mine.astype(BF)
        if self.full:
            low = self.clock.tick(low)
            self.mine = low.astype(F32)
            self.got = [flip(low, "ctx", 2 * k) for k in (1, 2, 3)]
            return
        out = [part_of(low, z ^ k, 4) for k in (1, 2, 3)]
        self.clock.tick(out[0])
        self.mine = part_of(mine, z, 4)
        self.got = [flip(out[k - 1], "ctx", 2 * k) for k in (1, 2, 3)]

    def collect(self):
        if not self.ctx:
            return
        mine, *came = self.clock(self.mine, *self.got)
        came = [item.astype(F32) for item in came]
        piece = self.clock.tick(((mine + came[0]) + (came[1] + came[2])).astype(BF))
        if self.full:
            self.got = [piece, flip(piece, "ctx", 1)]
        else:
            self.got = [piece] + [flip(piece, "ctx", 2 * k) for k in (1, 2, 3)]

    def line(self):
        if self.ctx and not self.full:
            line = self.clock.tick(jnp.stack(self.clock(*self.got)))
            self.got = [line, flip(line, "ctx", 1)]

    def finish(self):
        layout = self.layout
        if not self.ctx:
            summed = lax.psum((self.own + self.got.astype(F32)).astype(BF), "ctx").astype(F32)
            return [
                jnp.concatenate(
                    [summed[first + i * tall : first + (i + 1) * tall] for i in range(parts)],
                    axis=1,
                )
                for first, tall, parts in layout
            ]
        line, other = self.clock(*self.got)
        rows = self.own.shape[0]
        outs = tuple(shape((tall, 512 * parts), F32) for _, tall, parts in layout)
        result = call(
            functools.partial(assemble_kernel, layout, self.full), self.name, 1,
            (self.scal, line, other), [SMEM, ANY, ANY], outs,
            tuple(pl.BlockSpec(o.shape, lambda i: (0, 0)) for o in outs),
            [vm((rows, 512), BF)], 8, 2, rows * 4096,
        )
        self.clock.tick(result[0])
        return result


def shards(
    decoder_in,
    memory,
    seq_lengths,
    mem_lengths,
    self_query,
    self_keyval,
    self_out,
    cross_query,
    cross_keyval,
    cross_out,
    ffn_in,
    ffn_bias_in,
    ffn_out,
    ffn_bias_out,
    slot_weight,
    norm_gain,
    norm_bias,
    cotangent,
):
    tokens, mem_rows, cot = decoder_in[0], memory[0], cotangent[0]
    n_rows, width = tokens.shape
    n_mem = mem_rows.shape[0]
    hidden_units = ffn_in.shape[1]
    ctx = lax.axis_size("ctx")
    here, me = lax.axis_index("ctx"), lax.axis_index("wsh")
    n_keys, all_mem = ctx * n_rows, ctx * n_mem
    blocks = max(1, n_keys // 1536)
    step = n_keys // blocks

    def blocks_of(array, count):
        tall = array.shape[0] // count
        return [array[i * tall : (i + 1) * tall] for i in range(count)]

    small = jnp.concatenate(
        [ffn_bias_in.reshape(4, 128), ffn_bias_out.reshape(1, 128), norm_gain, norm_bias,
         jnp.zeros((5, 128), BF)],
        axis=0,
    )
    small = jnp.concatenate([small, jnp.zeros((16, 3 * width - 128), BF)], axis=1)
    group1 = jnp.concatenate([jnp.concatenate([self_query, self_keyval], axis=1), small], axis=0)
    group2 = jnp.concatenate([self_out, cross_query, cross_keyval, cross_out], axis=1)
    group3 = jnp.concatenate(
        [ffn_in, *blocks_of(ffn_out, hidden_units // 512), *blocks_of(slot_weight, 2)], axis=1
    )
    split = ctx == 8
    clock = Clock()
    g1 = gather_wsh(group1)
    if split:
        tokens_in = after(tokens, group1)
        both = after(jnp.concatenate([tokens, mem_rows], axis=0), group1)
        line = [tokens_in, flip(both, "ctx", 2), flip(tokens_in, "ctx", 4), flip(tokens_in, "ctx", 6)]
        toks = line + [across_ctx(both)] + [across_ctx(item) for item in line[1:]]
    else:
        toks = [lax.all_gather(tokens, "ctx", axis=0, tiled=True)]
    y2 = flip(after(group2, g1[2]), "wsh", 2)
    c2 = flip(group2, "wsh", 1)
    y3 = flip(after(group3, y2, toks[-1]), "wsh", 2)
    if split:
        mem_in = after(mem_rows, *toks[1:4])
        mem_line = [mem_rows, toks[1], flip(mem_in, "ctx", 4), flip(mem_in, "ctx", 6)]
        mem_side = [toks[4], toks[5]]
    prev_cot = permute(after(cot[-16:], y2), "ctx", lambda i: i + 1)

    live, mem_live = seq_lengths[0], mem_lengths[0]
    scal = jnp.stack(
        [me, live, here * n_rows, mem_live, here * n_mem, here, 0, 0]
    ).astype(jnp.int32)

    order = ORDER if ctx == 8 else None

    def fixed(*dims):
        return [pl.BlockSpec(d, lambda i, r=len(d): (0,) * r) for d in dims]

    tall, pay_w = (n_rows, width), (n_rows, width + EXT)
    pair_rows = (HEADS // 2, 2 * n_rows)
    by_block = pl.BlockSpec((step, 2 * width), lambda i: (i, 0))
    g2 = (group2, c2, y2, flip(y2, "wsh", 1))
    c3 = flip(after(group3, y2), "wsh", 1)
    tokens_now, *toks = clock(after(tokens, y2), *toks)
    kv, qs, self_ext, self_mixed = call(
        functools.partial(self_forward_kernel, blocks, order, len(toks)), "self_forward", blocks,
        (scal, tokens_now, *toks, *g1),
        [SMEM, whole(tokens)] + [ANY] * (len(toks) + 4),
        (shape((n_keys, 2 * width), BF), shape(tall, BF), shape((n_rows, EXT), BF),
         shape(tall, F32)),
        [by_block] + fixed(tall, (n_rows, EXT), tall),
        [vm((width, width), BF), vm((width, 2 * width), BF), vm((step, width), BF),
         vm((step, EXT), BF)]
        + ([vm((*pair_rows, 1), F32), vm((*pair_rows, 1), F32), vm((*pair_rows, 128), F32)]
           if blocks > 1 else [vm((8, 128), F32)] * 3),
        8 + len(toks), 11, 8 * 2**20,
    )
    clock.tick(qs)
    if split:
        mem_side += [across_ctx(clock(item)[0]) for item in mem_line[2:]]
        mems = mem_line + mem_side
    else:
        mems = [lax.all_gather(mem_rows, "ctx", axis=0, tiled=True)]
    self_mixed_now, *g2_now = clock(self_mixed, *g2)
    first_sum, cqs = call(
        self_dense_kernel, "self_dense", 1,
        (scal, tokens, self_mixed_now, *g1, *g2_now),
        [SMEM, whole(tokens), whole(self_mixed)] + [ANY] * 8,
        (shape(tall, F32), shape(tall, BF)), fixed(tall, tall),
        [vm((width, width), BF), vm((width, width), BF), vm((16, width), BF)],
        12, 2, 2 * 2**20,
    )
    clock.tick(cqs)
    y3 = after(y3, cqs)
    g3 = (group3, c3, y3, flip(y3, "wsh", 1))
    if split:
        cq_line = gather_line(after(cqs, *mem_line[1:]))
    (cqs_now, *mems_now) = clock(cqs, *mems)
    memkv, cross_ext, cross_mixed = call(
        functools.partial(cross_forward_kernel, order, len(mems)), "cross_forward", 1,
        (scal, cqs_now, *mems_now, *g2),
        [SMEM, whole(cqs)] + [ANY] * (len(mems) + 4),
        (shape((all_mem, 2 * width), BF), shape((n_rows, EXT), BF), shape(tall, F32)),
        fixed((all_mem, 2 * width), (n_rows, EXT), tall),
        [vm((width, 2 * width), BF), vm((all_mem, width), BF), vm((all_mem, EXT), BF)],
        4 + len(mems), 12, 8 * 2**20,
    )
    clock.tick(cross_ext)
    if split:
        cq_line = clock.tick(jnp.concatenate(clock(*cq_line), axis=0))
        all_cq = [cq_line, across_ctx(cq_line)]
    else:
        all_cq = [lax.all_gather(cqs, "ctx", axis=0, tiled=True)]
    (cross_mixed_now, prev_now, *g3_now) = clock(cross_mixed, prev_cot, *g3)
    pay_dc, masked, grads, d_second, sums, keep_a, send_a = call(
        middle_kernel, "middle", 1,
        (scal, cross_mixed_now, cross_ext, first_sum, cot, prev_now, *g1, *g2, *g3_now),
        [SMEM] + [whole(a) for a in (cross_mixed, cross_ext, first_sum, cot, prev_cot)]
        + [ANY] * 12,
        (shape(pay_w, BF), shape(tall, BF), shape(tall, BF),
         shape(tall, F32), shape((8, hidden_units), F32), *grad_outs(1152)),
        fixed(pay_w, tall, tall, tall, (8, hidden_units), (2, 1152, 512), (2, 1152, 512)),
        [vm((width, width), BF), vm((width, hidden_units), BF),
         vm((hidden_units, width), BF), vm((2 * width, width), BF), vm((16, width), BF),
         vm(tall, BF), vm(tall, BF), vm((n_rows, hidden_units), BF)],
        40, 12, 20 * 2**20,
    )
    clock.tick(pay_dc)
    sum_a = Total(
        clock, "sum_a", scal,
        ((0, 512, 1), (512, 128, hidden_units // 512), (1024, 128, 1)), keep_a, send_a,
    )
    if split:
        dc_line = gather_line(pay_dc)
        dc_side = [across_ctx(pay_dc)]
    else:
        all_dc = [lax.all_gather(pay_dc, "ctx", axis=0, tiled=True)]
    next_row = permute(masked[:16], "ctx", lambda i: i - 1)
    (pay_dc_now,) = clock(pay_dc)
    (dq_cross,) = call(
        functools.partial(cross_query_kernel, order), "cross_query", 1,
        (scal, cqs, pay_dc_now, memkv),
        [SMEM] + [whole(a) for a in (cqs, pay_dc, memkv)],
        (shape(tall, BF),), tuple(fixed(tall)), [vm((all_mem, EXT), BF)], 0, 13, 5 * 2**20,
    )
    clock.tick(dq_cross)
    if split:
        dc_side += [across_ctx(clock(item)[0]) for item in dc_line[1:2]]
    sum_a.across()
    (dq_now,) = clock(dq_cross)
    d_first, pay_ds, keep_b, send_b = call(
        cross_dense_kernel, "cross_dense", 1,
        (scal, dq_now, first_sum, d_second, self_mixed, self_ext, sums, *g1, *g2),
        [SMEM]
        + [whole(a) for a in (dq_cross, first_sum, d_second, self_mixed, self_ext, sums)]
        + [ANY] * 8,
        (shape(tall, F32), shape(pay_w, BF), *grad_outs(384)),
        fixed(tall, pay_w, (2, 384, 512), (2, 384, 512)),
        [vm((width, width), BF), vm((width, width), BF), vm((16, width), BF),
         vm(tall, BF), vm(tall, BF), vm((8, hidden_units), F32)],
        12, 8, 6 * 2**20,
    )
    clock.tick(pay_ds)
    if split:
        ds_line = gather_line(pay_ds)
        dc_side += [across_ctx(clock(item)[0]) for item in dc_line[2:]]
        all_dc = dc_line + dc_side
    else:
        all_ds = [lax.all_gather(pay_ds, "ctx", axis=0, tiled=True)]
    pay_now, next_now = clock(pay_ds, next_row)
    part, slots, keep_b, send_b = call(
        functools.partial(self_query_kernel, blocks, order), "self_query", blocks,
        (scal, qs, pay_now, kv, tokens, d_first, masked, next_now, grads, keep_b, send_b, *g1, *g3),
        [SMEM, whole(qs), whole(pay_ds), by_block]
        + [whole(a) for a in (tokens, d_first, masked, next_row, grads, keep_b, send_b)] + [ANY] * 8,
        (shape(tall, F32), shape(tall, BF), *grad_outs(768)),
        fixed(tall, tall, (2, 768, 512), (2, 768, 512)),
        [vm((width, width), BF), vm((2 * width, width), BF), vm((n_rows, 2 * width), BF),
         vm(tall, F32), vm((step, EXT), BF)],
        12, 9, 8 * 2**20,
    )
    clock.tick(part)
    sum_b = Total(
        clock, "sum_b", scal,
        ((0, 128, 1), (128, 128, 1), (256, 8, 1), (384, 256, 1), (640, 128, 1)), keep_b, send_b,
    )
    if split:
        ds_side = [across_ctx(clock(item)[0]) for item in ds_line]
        all_ds = ds_line + ds_side

    def keys_back(name, x, queries, q_from, pays, extra, group, first, mask, cost):
        rows = x.shape[0]
        came = clock(*q_from, *pays)
        q_from, pays = came[: len(q_from)], came[len(q_from) :]
        result = call(
            functools.partial(
                key_kernel, blocks, queries, first, mask, (len(q_from), len(pays), len(extra))
            ),
            name, blocks,
            (scal, x, *q_from, *pays, *extra, *group),
            [SMEM, whole(x)] + [ANY] * (len(q_from) + len(pays)) + [whole(e) for e in extra]
            + [ANY] * 4,
            (shape((rows, width), F32), *grad_outs(256)),
            fixed((rows, width), (2, 256, 512), (2, 256, 512)),
            [vm((width, 2 * width), BF), vm((width, width) if queries else (16, 128), BF),
             vm((rows, 2 * width), BF),
             vm((rows, 2 * width) if blocks > 1 else (8, 128), F32), vm((rows, 2 * width), BF),
             vm((step, width), BF), vm((step, width + EXT), BF)],
            8 + len(q_from) + len(pays), cost, 8 * 2**20,
        )
        clock.tick(result[0])
        return result

    grad_mem, keep_m, send_m = keys_back(
        "cross_key", mem_rows, False, all_cq, all_dc, (), g2, 2 * width, 3, 12
    )
    sum_m = Total(clock, "sum_m", scal, ((0, 128, 2),), keep_m, send_m, True)
    sum_a.side()
    sum_b.across()
    sum_m.across()
    grad_input, keep_k, send_k = keys_back(
        "self_key", tokens, True, toks, all_ds, (part,), g1, width, 1, 11
    )
    sum_k = Total(clock, "sum_k", scal, ((0, 128, 2),), keep_k, send_k, True)
    sum_a.spread()
    sum_b.side()
    sum_k.across()
    sum_m.side()
    sum_a.collect()
    sum_b.spread()
    sum_m.spread()
    sum_k.side()
    sum_a.line()
    sum_b.collect()
    sum_m.collect()
    sum_k.spread()
    g_second, g_first, g_cout = sum_a.finish()
    sum_b.line()
    (g_ckv,) = sum_m.finish()
    sum_k.collect()
    g_out, g_cq, tiny, g_slot, g_q = sum_b.finish()
    (g_kv,) = sum_k.finish()
    return (
        slots[None],
        grad_input[None],
        grad_mem[None],
        g_q,
        g_kv,
        g_out,
        g_cq,
        g_ckv,
        g_cout,
        g_first,
        tiny[0],
        g_second,
        tiny[1, :128],
        g_slot,
        tiny[2:5, :128],
        tiny[5:8, :128],
    )


def solution(mesh):
    rows, split = P("wsh", "ctx", None), P("wsh", None)
    line, side = P("wsh"), P(None, "wsh")
    in_specs = (
        rows, rows, line, line, split, split, split, split, split, split, split, line, split, line,
        split, side, side, rows,
    )
    out_specs = (
        rows, rows, rows, split, split, split, split, split, split, split, line, split, line, split,
        side, side,
    )
    return jax.shard_map(shards, mesh=mesh, in_specs=in_specs, out_specs=out_specs, check_vma=False)
```

```python
import functools
import math

import jax
import jax.numpy as jnp
from jax import lax
from jax.experimental import pallas as pl
from jax.experimental.pallas import tpu as pltpu
from jax.sharding import PartitionSpec as P

HEADS = 8
NORM_EPS = 1e-05
DEAD = -1e30
EXT = 128
DEAD_LANE = 3 * HEADS
LSE_LANE = 32
ORDER = (0, 2, 4, 6, 1, 3, 5, 7)
BF = jnp.bfloat16
F32 = jnp.float32
COST = 10**9
GRANTS = {}


def mm(left, right):
    return lax.dot_general(left, right, (((1,), (0,)), ((), ())), preferred_element_type=F32)


def mm2(left, right):
    high = left.astype(BF)
    low = (left - high.astype(F32)).astype(BF)
    return mm(high, right) + mm(low, right)


def mm_t(left, right):
    return lax.dot_general(left, right, (((1,), (1,)), ((), ())), preferred_element_type=F32)


def t_mm(left, right):
    return lax.dot_general(left, right, (((0,), (0,)), ((), ())), preferred_element_type=F32)


def norm_stats(values):
    center = values - jnp.mean(values, axis=-1, keepdims=True)
    inverse = lax.rsqrt(jnp.mean(center * center, axis=-1, keepdims=True) + NORM_EPS)
    return center * inverse, inverse


def norm_back(grad_out, normed, inverse, gain_row):
    scaled = grad_out * gain_row
    grad_in = inverse * (
        scaled
        - jnp.mean(scaled, axis=-1, keepdims=True)
        - normed * jnp.mean(scaled * normed, axis=-1, keepdims=True)
    )
    return (
        grad_in,
        jnp.sum(grad_out * normed, axis=0, keepdims=True),
        jnp.sum(grad_out, axis=0, keepdims=True),
    )


def lanes(width=128):
    return lax.broadcasted_iota(jnp.int32, (1, width), 1)


def stack_pair(block):
    low = lanes() < 64
    zero = jnp.zeros_like(block)
    return jnp.concatenate([jnp.where(low, block, zero), jnp.where(low, zero, block)], axis=0)


def unstack_pair(stacked):
    n = stacked.shape[0] // 2
    return jnp.where(lanes() < 64, stacked[:n], stacked[n:])


def split3(value):
    high = value.astype(BF).astype(F32)
    rest = value - high
    mid = rest.astype(BF).astype(F32)
    return high, mid, (rest - mid).astype(BF).astype(F32)


def place3(table, column, lane):
    where = lanes()
    for term, part in enumerate(split3(column)):
        table = jnp.where(where == lane + term, part, table)
    return table


def pair_ext(table, pair, offset):
    where = lanes()
    other = jnp.where(where == DEAD_LANE, 1.0 if offset else 0.0, 0.0).astype(table.dtype)
    parts = []
    for head in (2 * pair, 2 * pair + 1):
        first = offset + 3 * head
        parts.append(jnp.where((where >= first) & (where < first + 3), table, other))
    return jnp.concatenate(parts, axis=0)


def ones_ext(rows, pair, offset):
    where = lanes()
    parts = []
    for head in (2 * pair, 2 * pair + 1):
        first = offset + 3 * head
        one = jnp.where((where >= first) & (where < first + 3), 1.0, 0.0)
        parts.append(jnp.broadcast_to(one, (rows, EXT)))
    return jnp.concatenate(parts, axis=0).astype(BF)


def add_delta(table, grad_low, mixed):
    product = grad_low.astype(F32) * mixed
    low = lanes() < 64
    table = table.astype(F32)
    for pair in range(HEADS // 2):
        block = product[:, 128 * pair : 128 * pair + 128]
        even = jnp.sum(jnp.where(low, block, 0.0), axis=1, keepdims=True)
        odd = jnp.sum(jnp.where(low, 0.0, block), axis=1, keepdims=True)
        table = place3(table, -even, 6 * pair)
        table = place3(table, -odd, 6 * pair + 3)
    return table.astype(BF)


def fill_ext(ext_ref, first, rows, here, limit, order):
    where = lanes()
    base = jnp.where(where == DEAD_LANE, 0.0, 1.0)
    for i in range(ext_ref.shape[0] // rows):
        device = jnp.bitwise_xor(here, order[i]) if order else first + i
        place = device * rows + lax.broadcasted_iota(jnp.int32, (rows, 1), 0)
        dead = (where == DEAD_LANE) & (place >= limit)
        ext_ref[i * rows : (i + 1) * rows, :] = jnp.where(dead, DEAD, base).astype(BF)


def pair_slice(pair):
    return pl.ds(pl.multiple_of(pair * 128, 128), 128)


def attend_forward(q_ref, kv_ref, kext_ref, mixed_ref, state, blocks, block):
    n_rows, width = q_ref.shape
    where = lanes()
    ext = jnp.broadcast_to(jnp.where(where == DEAD_LANE, 1.0, 0.0), (2 * n_rows, EXT)).astype(BF)
    kext = kext_ref[...]

    def one_pair(pair, table):
        q2 = jnp.concatenate([stack_pair(q_ref[:, pair_slice(pair)]), ext], axis=1)
        keys = jnp.concatenate([kv_ref[:, pair_slice(pair)], kext], axis=1)
        scores = mm_t(q2, keys)
        top = jnp.max(scores, axis=1, keepdims=True)
        if blocks > 1:
            before = jnp.where(block == 0, DEAD, state[0][pair])
            top = jnp.maximum(top, before)
        powers = jnp.exp(scores - top)
        total = jnp.sum(powers, axis=1, keepdims=True)
        mixed = mm2(powers, kv_ref[:, pair_slice(pair + width // 128)])
        if blocks > 1:
            fade = jnp.exp(before - top)
            total = total + fade * jnp.where(block == 0, 0.0, state[1][pair])
            mixed = mixed + fade * jnp.where(block == 0, 0.0, state[2][pair])
            state[0][pair] = top
            state[1][pair] = total
            state[2][pair] = mixed
        mixed_ref[:, pair_slice(pair)] = unstack_pair(mixed * (1.0 / total))
        lse = -(top + jnp.log(total))
        table = place3(table, lse[:n_rows], LSE_LANE + 6 * pair)
        return place3(table, lse[n_rows:], LSE_LANE + 6 * pair + 3)

    start = jnp.zeros((n_rows, EXT), F32)
    return lax.fori_loop(0, HEADS // 2, one_pair, start, unroll=True).astype(BF)


def attend_query_back(q_ref, pay_ref, kv_ref, kext_ref, add_pair):
    width = q_ref.shape[1]
    kext = kext_ref[...]
    ext = pay_ref[:, width:]

    def one_pair(pair, carry):
        keys = kv_ref[:, pair_slice(pair)]
        q2 = jnp.concatenate(
            [stack_pair(q_ref[:, pair_slice(pair)]), pair_ext(ext, pair, LSE_LANE)], axis=1
        )
        probs = jnp.exp(mm_t(q2, jnp.concatenate([keys, kext], axis=1)))
        do2 = jnp.concatenate(
            [stack_pair(pay_ref[:, pair_slice(pair)]), pair_ext(ext, pair, 0)], axis=1
        )
        values = kv_ref[:, pair_slice(pair + width // 128)]
        d_probs = mm_t(do2, jnp.concatenate([values, kext], axis=1))
        d_scores = (probs * d_probs).astype(BF)
        add_pair(pair, unstack_pair(mm(d_scores, keys)))
        return carry

    lax.fori_loop(0, HEADS // 2, one_pair, 0, unroll=True)


def attend_key_back(kv_ref, q_ref, pay_ref, add_pair):
    n_keys = kv_ref.shape[0]
    width = kv_ref.shape[1] // 2
    ext = pay_ref[:, width:]

    def one_pair(pair, carry):
        queries = q_ref[:, pair_slice(pair)]
        grads = pay_ref[:, pair_slice(pair)]
        k2 = jnp.concatenate(
            [stack_pair(kv_ref[:, pair_slice(pair)]), ones_ext(n_keys, pair, LSE_LANE)], axis=1
        )
        probs = jnp.exp(mm_t(k2, jnp.concatenate([queries, ext], axis=1)))
        v2 = jnp.concatenate(
            [stack_pair(kv_ref[:, pair_slice(pair + width // 128)]), ones_ext(n_keys, pair, 0)],
            axis=1,
        )
        d_probs = mm_t(v2, jnp.concatenate([grads, ext], axis=1))
        d_scores = (probs * d_probs).astype(BF)
        add_pair(pair, unstack_pair(mm(d_scores, queries)), unstack_pair(mm(probs.astype(BF), grads)))
        return carry

    lax.fori_loop(0, HEADS // 2, one_pair, 0, unroll=True)


class Fetch:
    def __init__(self, me, sems):
        self.me, self.sems, self.used = me, sems, 0

    def start(self, slots, source, target):
        copies = []
        for slot, ref in enumerate(slots):
            quarter = jnp.bitwise_xor(self.me, slot)
            copy = pltpu.make_async_copy(source(ref), target(quarter), self.sems.at[self.used])
            self.used += 1
            copy.start()
            copies.append(copy)
        return copies

    def rows(self, slots, first, width, ref, height=128):
        copies = []
        for part in range(height // 128):
            copies += self.start(
                slots,
                lambda s, part=part: s.at[pl.ds(0, 128), pl.ds(first + part * width, width)],
                lambda quarter, part=part: ref.at[
                    pl.ds(pl.multiple_of(quarter * height + part * 128, 128), 128)
                ],
            )
        return copies

    def shards(self, refs, ref, block=0, tail=False):
        copies = []
        if len(refs) == 1:
            tall = ref.shape[0]
            source = refs[0].at[pl.ds(pl.multiple_of(block * tall, 8), tall)]
            pieces = [(source, ref)]
        else:
            tall = ref.shape[0] // len(refs)
            pieces = [
                (
                    r.at[pl.ds(r.shape[0] - tall if tail else 0, tall)],
                    ref.at[pl.ds(i * tall, tall)],
                )
                for i, r in enumerate(refs)
            ]
        for source, target in pieces:
            copy = pltpu.make_async_copy(source, target, self.sems.at[self.used])
            self.used += 1
            copy.start()
            copies.append(copy)
        return copies

    def small(self, slots, ref):
        return self.start(
            slots,
            lambda s: s.at[pl.ds(128, 16), pl.ds(0, 128)],
            lambda quarter: ref.at[:, pl.ds(pl.multiple_of(quarter * 128, 128), 128)],
        )


def wait(copies):
    for copy in copies:
        copy.wait()


def quarter_of(ref, me, slot, width):
    start = pl.multiple_of(jnp.bitwise_xor(me, slot) * width, 128)
    return ref[:, pl.ds(start, width)]


KEPT = (0, 2)
SENT = (1, 3)


def put_blocks(keep_ref, send_ref, first, me, block_of):
    for target, slots in ((keep_ref, KEPT), (send_ref, SENT)):
        for place, slot in enumerate(slots):
            block = block_of(slot).astype(target.dtype)
            rows = block.shape[0]
            for part in range(block.shape[1] // 512):
                target[place, first + part * rows : first + (part + 1) * rows, :] = block[
                    :, 512 * part : 512 * (part + 1)
                ]


def small_row(small_ref, row):
    return small_ref[row : row + 1, :].astype(F32)


GAIN, BIAS = 5, 8
HIDDEN_QUARTER = 512


def first_last(blocks, block, at, what):
    if blocks > 1:
        pl.when(block == (0 if at == "first" else blocks - 1))(what)
    else:
        what()


def self_forward_kernel(blocks, order, n_tok, scal, x_ref, *refs):
    toks, g1 = refs[:n_tok], refs[n_tok : n_tok + 4]
    kv_ref, q_ref, ext_ref, mixed_ref = refs[n_tok + 4 : n_tok + 8]
    wq, wkv, tok, kext, m_st, l_st, a_st, sems = refs[n_tok + 8 :]
    me, live, here = scal[0], scal[1], scal[5]
    block = pl.program_id(0)
    n_rows, width = x_ref.shape
    fetch = Fetch(me, sems)
    c_tok = fetch.shards(toks, tok, block)

    def begin():
        c_q = fetch.rows(g1, 0, width, wq)
        c_kv = fetch.rows(g1, width, 2 * width, wkv)
        wait(c_q)
        q_ref[...] = (mm(x_ref[...], wq[...]).astype(BF).astype(F32) * 0.125).astype(BF)
        wait(c_kv)

    first_last(blocks, block, "first", begin)
    fill_ext(kext, block * (tok.shape[0] // n_rows), n_rows, here, live, order)
    wait(c_tok)
    kv_ref[...] = mm(tok[...], wkv[...]).astype(BF)
    table = attend_forward(q_ref, kv_ref, kext, mixed_ref, (m_st, l_st, a_st), blocks, block)

    def finish():
        ext_ref[...] = table

    first_last(blocks, block, "last", finish)


def self_dense_kernel(scal, x_ref, mixed_ref, *refs):
    g1, g2 = refs[0:4], refs[4:8]
    sum_ref, cq_ref = refs[8:10]
    wo, wc, small, sems = refs[10:]
    width = x_ref.shape[1]
    fetch = Fetch(scal[0], sems)
    c_o = fetch.rows(g2, 0, width, wo)
    c_rest = fetch.small(g1, small)
    c_rest += fetch.rows(g2, width, width, wc)
    wait(c_o)
    first = x_ref[...].astype(F32) + mm(mixed_ref[...].astype(BF), wo[...])
    sum_ref[...] = first
    wait(c_rest)
    normed, _ = norm_stats(first)
    hidden = normed * small_row(small, GAIN) + small_row(small, BIAS)
    cq = mm(hidden.astype(BF), wc[...]).astype(BF)
    cq_ref[...] = (cq.astype(F32) * 0.125).astype(BF)


def gelu_parts(value):
    coef = math.sqrt(2.0 / math.pi)
    square = value * value
    inner = coef * (value + 0.044715 * value * square)
    bend = jnp.tanh(inner)
    half = 0.5 * (1.0 + bend)
    slope = half + 0.5 * value * (1.0 - bend * bend) * coef * (1.0 + 3 * 0.044715 * square)
    return value * half, slope


def cross_forward_kernel(order, n_mem, scal, cq_ref, *refs):
    mems, g2 = refs[:n_mem], refs[n_mem : n_mem + 4]
    kv_ref, ext_ref, mixed_ref = refs[n_mem + 4 : n_mem + 7]
    wkv, mem, kext, sems = refs[n_mem + 7 :]
    me, live, here = scal[0], scal[3], scal[5]
    width = cq_ref.shape[1]
    fetch = Fetch(me, sems)
    c_kv = fetch.rows(g2, 2 * width, 2 * width, wkv)
    c_mem = fetch.shards(mems, mem, 0, True)
    fill_ext(kext, 0, scal_rows(mem, order), here, live, order)
    wait(c_kv)
    wait(c_mem)
    kv_ref[...] = mm(mem[...], wkv[...]).astype(BF)
    ext_ref[...] = attend_forward(cq_ref, kv_ref, kext, mixed_ref, None, 1, 0)


def scal_rows(array, order):
    return array.shape[0] // len(order) if order else array.shape[0]


def middle_kernel(scal, mixed_ref, ext_ref, sum_ref, cot_ref, prev_ref, *refs):
    g1, g2, g3 = refs[0:4], refs[4:8], refs[8:12]
    pay_ref, masked_ref, g_ref, second_ref, sums_ref, keep_ref, send_ref = refs[12:19]
    wo, w1, w2, ws, small, low, hid, act, sems = refs[19:]
    me, live, base = scal[0], scal[1], scal[2]
    n_rows, width = sum_ref.shape
    hidden_units = w1.shape[1]
    fetch = Fetch(me, sems)
    c_small = fetch.small(g1, small)
    c_o = fetch.rows(g2, 4 * width, width, wo)
    c_1 = fetch.rows(g3, 0, hidden_units, w1)
    c_2 = fetch.rows(g3, hidden_units, width, w2, hidden_units // 4)
    c_s = fetch.rows(g3, 2 * hidden_units, width, ws, 256)
    low[...] = mixed_ref[...].astype(BF)
    wait(c_small)
    wait(c_o)
    normed, _ = norm_stats(sum_ref[...])
    hidden_one = normed * small_row(small, GAIN) + small_row(small, BIAS)
    second = hidden_one + mm(low[...], wo[...])
    normed_two, inverse_two = norm_stats(second)
    hidden_two = normed_two * small_row(small, GAIN + 1) + small_row(small, BIAS + 1)
    hid[...] = hidden_two.astype(BF)
    bias_in = jnp.concatenate(
        [
            small[r : r + 1, 128 * j : 128 * j + 128].astype(F32)
            for j in range(4)
            for r in range(4)
        ],
        axis=1,
    )
    wait(c_1)
    preact = mm(hid[...], w1[...]) + bias_in
    active, slope = gelu_parts(preact)
    act[...] = active.astype(BF)
    wait(c_2)
    third = hidden_two + mm(act[...], w2[...]) + small_row(small, 4)
    normed_three, inverse_three = norm_stats(third)
    hidden_three = normed_three * small_row(small, GAIN + 2) + small_row(small, BIAS + 2)
    places = base + lax.broadcasted_iota(jnp.int32, (n_rows, 1), 0)
    valid = places < live
    masked_ref[...] = jnp.where(valid, hidden_three, 0.0).astype(BF)

    grads = jnp.where(valid, cot_ref[...].astype(F32), 0.0).astype(BF)
    g_ref[...] = grads
    wait(c_s)
    d_own = mm_t(grads, ws[:width, :])
    before = jnp.where(base - 1 < live, prev_ref[15:16, :].astype(F32), 0.0).astype(BF)
    shifted = jnp.concatenate([before, grads[:-1]], axis=0)
    d_next = mm_t(shifted, ws[width:, :])
    d_three = jnp.where(valid, d_own + d_next, 0.0)
    d_third, gain_three, bias_three = norm_back(
        d_three, normed_three, inverse_three, small_row(small, GAIN + 2)
    )
    e_third = d_third.astype(BF)
    d_pre = (mm_t(e_third, w2[...]) * slope).astype(BF)
    d_two = d_third + mm_t(d_pre, w1[...])
    d_second, gain_two, bias_two = norm_back(
        d_two, normed_two, inverse_two, small_row(small, GAIN + 1)
    )
    second_ref[...] = d_second
    e_second = d_second.astype(BF)
    d_cross = mm_t(e_second, wo[...]).astype(BF)
    pay_ref[:, :width] = d_cross
    pay_ref[:, width:] = add_delta(ext_ref[...], d_cross, mixed_ref[...])
    sums_ref[...] = jnp.zeros_like(sums_ref)
    sums_ref[0:1, :] = jnp.sum(d_pre.astype(F32), axis=0, keepdims=True)
    sums_ref[1:2, :width] = jnp.sum(e_third.astype(F32), axis=0, keepdims=True)
    sums_ref[3:4, :width] = gain_two
    sums_ref[4:5, :width] = gain_three
    sums_ref[6:7, :width] = bias_two
    sums_ref[7:8, :width] = bias_three
    put_blocks(
        keep_ref, send_ref, 0, me, lambda s: t_mm(quarter_of(act, me, s, hidden_units // 4), e_third)
    )
    put_blocks(keep_ref, send_ref, 512, me, lambda s: t_mm(quarter_of(hid, me, s, 128), d_pre))
    put_blocks(keep_ref, send_ref, 1024, me, lambda s: t_mm(quarter_of(low, me, s, 128), e_second))


def cross_query_kernel(order, scal, cq_ref, pay_ref, kv_ref, dq_ref, kext):
    live, here = scal[3], scal[5]
    fill_ext(kext, 0, scal_rows(kext, order), here, live, order)

    def add_pair(pair, value):
        dq_ref[:, pair_slice(pair)] = (value * 0.125).astype(BF)

    attend_query_back(cq_ref, pay_ref, kv_ref, kext, add_pair)


def cross_dense_kernel(scal, dq_ref, sum_ref, second_ref, mixed_ref, ext_ref, sums_ref, *refs):
    g1, g2 = refs[0:4], refs[4:8]
    d_first_ref, pay_ref, keep_ref, send_ref = refs[8:12]
    wo, wc, small, low, hid, sums, sems = refs[12:]
    me = scal[0]
    width = sum_ref.shape[1]
    fetch = Fetch(me, sems)
    c_c = fetch.rows(g2, width, width, wc)
    c_small = fetch.small(g1, small)
    c_o = fetch.rows(g2, 0, width, wo)
    wait(c_small)
    normed, inverse = norm_stats(sum_ref[...])
    hid[...] = (normed * small_row(small, GAIN) + small_row(small, BIAS)).astype(BF)
    low[...] = mixed_ref[...].astype(BF)
    wait(c_c)
    d_one = second_ref[...] + mm_t(dq_ref[...], wc[...])
    d_first, gain_one, bias_one = norm_back(d_one, normed, inverse, small_row(small, GAIN))
    d_first_ref[...] = d_first
    e_first = d_first.astype(BF)
    wait(c_o)
    d_self = mm_t(e_first, wo[...]).astype(BF)
    pay_ref[:, :width] = d_self
    pay_ref[:, width:] = add_delta(ext_ref[...], d_self, mixed_ref[...])
    put_blocks(keep_ref, send_ref, 0, me, lambda s: t_mm(quarter_of(low, me, s, 128), e_first))
    put_blocks(keep_ref, send_ref, 128, me, lambda s: t_mm(quarter_of(hid, me, s, 128), dq_ref[...]))
    sums[...] = sums_ref[...]
    sums[2:3, :width] = gain_one
    sums[5:6, :width] = bias_one
    quarter = sums_ref.shape[1] // 4

    def small_block(slot):
        top = quarter_of(sums, me, slot, quarter)
        rest = quarter_of(sums, me, slot, 128)
        rest = jnp.concatenate([rest, jnp.zeros((8, quarter - 128), F32)], axis=1)
        row = lax.broadcasted_iota(jnp.int32, (8, 1), 0)
        return jnp.concatenate(
            [jnp.where(row == 0, top, rest), jnp.zeros((120, quarter), F32)], axis=0
        )

    put_blocks(keep_ref, send_ref, 256, me, small_block)


def self_query_kernel(
    blocks, order, scal, q_ref, pay_ref, kv_ref, x_ref, d_first_ref, masked_ref, next_ref, g_ref,
    keep_in, send_in, *refs
):
    g1, g3 = refs[0:4], refs[4:8]
    part_ref, slots_ref, keep_ref, send_ref = refs[8:12]
    wq, ws, paired, acc, kext, sems = refs[12:]
    me, live, base, here = scal[0], scal[1], scal[2], scal[5]
    block = pl.program_id(0)
    n_rows, width = x_ref.shape
    before = keep_in.shape[1]

    def begin():
        fetch = Fetch(me, sems)
        c_q = fetch.rows(g1, 0, width, wq)
        c_s = fetch.rows(g3, 2 * HIDDEN_QUARTER * 4, width, ws, 256)
        masked = masked_ref[...]
        paired[:, :width] = masked
        paired[:, width:] = jnp.concatenate([masked[1:], next_ref[0:1, :]], axis=0)
        places = base + lax.broadcasted_iota(jnp.int32, (n_rows, 1), 0)
        keep_ref[:, :before, :] = keep_in[...]
        send_ref[:, :before, :] = send_in[...]
        put_blocks(
            keep_ref, send_ref, before, me, lambda s: t_mm(quarter_of(paired, me, s, 256), g_ref[...])
        )
        wait(c_s)
        slots_ref[...] = jnp.where(places < live, mm(paired[...], ws[...]), 0.0).astype(BF)
        wait(c_q)

    first_last(blocks, block, "first", begin)
    fill_ext(kext, block * (kext.shape[0] // n_rows), n_rows, here, live, order)

    def add_pair(pair, value):
        at = pair_slice(pair)
        if blocks > 1:
            value = value + jnp.where(block == 0, 0.0, acc[:, at])
        acc[:, at] = value

    attend_query_back(q_ref, pay_ref, kv_ref, kext, add_pair)

    def finish():
        dq = (acc[...] * 0.125).astype(BF)
        part_ref[...] = d_first_ref[...] + mm_t(dq, wq[...])
        put_blocks(
            keep_ref, send_ref, before + 256, me,
            lambda s: t_mm(quarter_of(x_ref, me, s, 128), dq),
        )

    first_last(blocks, block, "last", finish)


def key_kernel(blocks, queries, first, mask, counts, scal, x_ref, *refs):
    n_q, n_pay, n_part = counts
    qs, pays = refs[:n_q], refs[n_q : n_q + n_pay]
    refs = refs[n_q + n_pay :]
    part = refs[:n_part]
    group = refs[n_part : n_part + 4]
    grad_ref, keep_ref, send_ref = refs[n_part + 4 : n_part + 7]
    wkv, wq, kv, acc, low, q_all, pay_all, sems = refs[n_part + 7 :]
    me, live, base = scal[0], scal[mask], scal[mask + 1]
    block = pl.program_id(0)
    n_rows, width = x_ref.shape
    fetch = Fetch(me, sems)
    c_q = fetch.shards(qs, q_all, block)
    c_pay = fetch.shards(pays, pay_all, block)

    def begin():
        c_w = fetch.rows(group, first, 2 * width, wkv)
        if queries:
            c_w += fetch.rows(group, 0, width, wq)
        wait(c_w)
        kv[...] = mm(x_ref[...], wkv[...]).astype(BF)

    first_last(blocks, block, "first", begin)
    wait(c_q)
    if queries:
        q_all[...] = (mm(q_all[...], wq[...]).astype(BF).astype(F32) * 0.125).astype(BF)
    wait(c_pay)

    def add_pair(pair, d_key, d_value):
        at_key, at_value = pair_slice(pair), pair_slice(pair + width // 128)
        if blocks > 1:
            d_key = d_key + jnp.where(block == 0, 0.0, acc[:, at_key])
            d_value = d_value + jnp.where(block == 0, 0.0, acc[:, at_value])
            acc[:, at_key] = d_key
            acc[:, at_value] = d_value
        usable = base + lax.broadcasted_iota(jnp.int32, (n_rows, 1), 0) < live
        low[:, at_key] = jnp.where(usable, d_key, 0.0).astype(BF)
        low[:, at_value] = jnp.where(usable, d_value, 0.0).astype(BF)

    attend_key_back(kv, q_all, pay_all, add_pair)

    def finish():
        value = mm_t(low[...], wkv[...])
        grad_ref[...] = part[0][...] + value if n_part else value
        put_blocks(keep_ref, send_ref, 0, me, lambda s: t_mm(quarter_of(x_ref, me, s, 128), low[...]))

    first_last(blocks, block, "last", finish)


def assemble_kernel(layout, full, scal, line, other, *refs):
    outs, whole_ref, sems = refs[:-2], refs[-2], refs[-1]
    here = scal[5]
    rows = whole_ref.shape[0]
    copies = []
    for i, ref in enumerate((line, other)):
        x = jnp.bitwise_xor(lax.rem(here, 2), i)
        for k in range(1 if full else 4):
            if full:
                tall, source = rows // 2, ref
                at = pl.multiple_of(x * tall, 16)
            else:
                tall, source = rows // 8, ref.at[k]
                z = jnp.bitwise_xor(lax.div(here, 2), k)
                at = pl.multiple_of(x * (rows // 2) + z * tall, 16)
            copy = pltpu.make_async_copy(source, whole_ref.at[pl.ds(at, tall)], sems.at[4 * i + k])
            copy.start()
            copies.append(copy)
    wait(copies)
    for (first, tall, parts), out in zip(layout, outs):
        for part in range(parts):
            at = first + part * tall
            out[:, 512 * part : 512 * (part + 1)] = whole_ref[at : at + tall, :].astype(F32)


def whole(array, buffers=None):
    rank = len(array.shape)
    return pl.BlockSpec(tuple(array.shape), lambda *_: (0,) * rank)


def by_rows(array, rows):
    return pl.BlockSpec((rows, array.shape[1]), lambda i: (i, 0))


ANY = pl.BlockSpec(memory_space=pltpu.HBM)
SMEM = pl.BlockSpec(memory_space=pltpu.SMEM)


def shape(dims, dtype):
    return jax.ShapeDtypeStruct(dims, dtype)


def call(kernel, name, grid, args, specs, outs, out_specs, scratch, copies, flops, moved):
    return pl.pallas_call(
        kernel,
        name=name,
        grid=(grid,),
        in_specs=specs,
        out_specs=out_specs,
        out_shape=outs,
        scratch_shapes=[*scratch] + ([pltpu.SemaphoreType.DMA((copies,))] if copies else []),
        compiler_params=pltpu.CompilerParams(
            vmem_limit_bytes=GRANTS.get(name, 28) * 2**20, dimension_semantics=("arbitrary",)
        ),
        cost_estimate=pl.CostEstimate(
            flops=12 * COST, bytes_accessed=moved // 64, transcendentals=0
        ),
    )(*args)


def vm(dims, dtype):
    return pltpu.VMEM(dims, dtype)


def grad_outs(rows):
    return (shape((2, rows, 512), F32), shape((2, rows, 512), BF))


def permute(value, axis, target):
    n = lax.axis_size(axis)
    pairs = [(i, target(i)) for i in range(n) if 0 <= target(i) < n]
    return lax.ppermute(value, axis, pairs)


def flip(value, axis, bits):
    return permute(value, axis, lambda i: i ^ bits)


def rows_of(ctx, gathered):
    return [a.reshape(-1, a.shape[-1]) for a in gathered]


def gather_line(value):
    return [value] + [flip(value, "ctx", bits) for bits in (2, 4, 6)]


def across_ctx(item):
    return flip(item, "ctx", 1)


def after(value, *others):
    return lax.optimization_barrier((value, *others))[0]


def gather_wsh(group):
    own = group
    across = flip(own, "wsh", 2)
    return (own, flip(own, "wsh", 1), across, flip(across, "wsh", 1))


def part_of(array, index, count):
    rows = array.shape[0] // count
    return lax.dynamic_slice_in_dim(array, index * rows, rows, 0)


class Clock:
    def __init__(self):
        self.last = None

    def __call__(self, *values):
        if self.last is None:
            return values
        return lax.optimization_barrier((*values, self.last))[:-1]

    def tick(self, value):
        self.last = value
        return value


class Total:
    def __init__(self, clock, name, scal, layout, keep, send, full=False):
        self.clock, self.name, self.scal, self.layout = clock, name, scal, layout
        self.keep, self.full = keep, full
        self.got = flip(send, "wsh", 1)
        self.ctx = lax.axis_size("ctx") == 8

    def across(self):
        keep, got = self.clock(self.keep, self.got)
        half = keep + got.astype(F32)
        out = self.clock.tick(half[1].astype(BF))
        self.own, self.got = half[0], flip(out, "wsh", 2)

    def side(self):
        if not self.ctx:
            return
        x = lax.axis_index("ctx") % 2
        own, got = self.clock(self.own, self.got)
        self.mine = part_of(own, x, 2) + part_of(got, x, 2).astype(F32)
        out = (part_of(own, 1 - x, 2) + part_of(got, 1 - x, 2).astype(F32)).astype(BF)
        self.got = flip(self.clock.tick(out), "ctx", 1)

    def spread(self):
        if not self.ctx:
            return
        z = lax.axis_index("ctx") // 2
        mine, got = self.clock(self.mine, self.got)
        mine = mine + got.astype(F32)
        low = mine.astype(BF)
        if self.full:
            low = self.clock.tick(low)
            self.mine = low.astype(F32)
            self.got = [flip(low, "ctx", 2 * k) for k in (1, 2, 3)]
            return
        out = [part_of(low, z ^ k, 4) for k in (1, 2, 3)]
        self.clock.tick(out[0])
        self.mine = part_of(mine, z, 4)
        self.got = [flip(out[k - 1], "ctx", 2 * k) for k in (1, 2, 3)]

    def collect(self):
        if not self.ctx:
            return
        mine, *came = self.clock(self.mine, *self.got)
        came = [item.astype(F32) for item in came]
        piece = self.clock.tick(((mine + came[0]) + (came[1] + came[2])).astype(BF))
        if self.full:
            self.got = [piece, flip(piece, "ctx", 1)]
        else:
            self.got = [piece] + [flip(piece, "ctx", 2 * k) for k in (1, 2, 3)]

    def line(self):
        if self.ctx and not self.full:
            line = self.clock.tick(jnp.stack(self.clock(*self.got)))
            self.got = [line, flip(line, "ctx", 1)]

    def finish(self):
        layout = self.layout
        if not self.ctx:
            summed = lax.psum((self.own + self.got.astype(F32)).astype(BF), "ctx").astype(F32)
            return [
                jnp.concatenate(
                    [summed[first + i * tall : first + (i + 1) * tall] for i in range(parts)],
                    axis=1,
                )
                for first, tall, parts in layout
            ]
        line, other = self.got
        rows = self.own.shape[0]
        outs = tuple(shape((tall, 512 * parts), F32) for _, tall, parts in layout)
        result = call(
            functools.partial(assemble_kernel, layout, self.full), self.name, 1,
            (self.scal, line, other), [SMEM, ANY, ANY], outs,
            tuple(pl.BlockSpec(o.shape, lambda i: (0, 0)) for o in outs),
            [vm((rows, 512), BF)], 8, 2, rows * 4096,
        )
        return result


def shards(
    decoder_in,
    memory,
    seq_lengths,
    mem_lengths,
    self_query,
    self_keyval,
    self_out,
    cross_query,
    cross_keyval,
    cross_out,
    ffn_in,
    ffn_bias_in,
    ffn_out,
    ffn_bias_out,
    slot_weight,
    norm_gain,
    norm_bias,
    cotangent,
):
    tokens, mem_rows, cot = decoder_in[0], memory[0], cotangent[0]
    n_rows, width = tokens.shape
    n_mem = mem_rows.shape[0]
    hidden_units = ffn_in.shape[1]
    ctx = lax.axis_size("ctx")
    here, me = lax.axis_index("ctx"), lax.axis_index("wsh")
    n_keys, all_mem = ctx * n_rows, ctx * n_mem
    blocks = max(1, n_keys // 1536)
    step = n_keys // blocks

    def blocks_of(array, count):
        tall = array.shape[0] // count
        return [array[i * tall : (i + 1) * tall] for i in range(count)]

    small = jnp.concatenate(
        [ffn_bias_in.reshape(4, 128), ffn_bias_out.reshape(1, 128), norm_gain, norm_bias,
         jnp.zeros((5, 128), BF)],
        axis=0,
    )
    small = jnp.concatenate([small, jnp.zeros((16, 3 * width - 128), BF)], axis=1)
    group1 = jnp.concatenate([jnp.concatenate([self_query, self_keyval], axis=1), small], axis=0)
    group2 = jnp.concatenate([self_out, cross_query, cross_keyval, cross_out], axis=1)
    group3 = jnp.concatenate(
        [ffn_in, *blocks_of(ffn_out, hidden_units // 512), *blocks_of(slot_weight, 2)], axis=1
    )
    split = ctx == 8
    clock = Clock()
    g1 = gather_wsh(group1)
    if split:
        tokens_in = after(tokens, group1)
        both = after(jnp.concatenate([tokens, mem_rows], axis=0), group1)
        line = [tokens_in, flip(both, "ctx", 2), flip(tokens_in, "ctx", 4), flip(tokens_in, "ctx", 6)]
        toks = line + [across_ctx(both)] + [across_ctx(item) for item in line[1:]]
    else:
        toks = [lax.all_gather(tokens, "ctx", axis=0, tiled=True)]
    y2 = flip(after(group2, g1[2]), "wsh", 2)
    c2 = flip(group2, "wsh", 1)
    y3 = flip(after(group3, y2, toks[-1]), "wsh", 2)
    if split:
        mem_in = after(mem_rows, *toks[1:4])
        mem_line = [mem_rows, toks[1], flip(mem_in, "ctx", 4), flip(mem_in, "ctx", 6)]
        mem_side = [toks[4], toks[5]]
    prev_cot = permute(after(cot[-16:], y2), "ctx", lambda i: i + 1)

    live, mem_live = seq_lengths[0], mem_lengths[0]
    scal = jnp.stack(
        [me, live, here * n_rows, mem_live, here * n_mem, here, 0, 0]
    ).astype(jnp.int32)

    order = ORDER if ctx == 8 else None

    def fixed(*dims):
        return [pl.BlockSpec(d, lambda i, r=len(d): (0,) * r) for d in dims]

    tall, pay_w = (n_rows, width), (n_rows, width + EXT)
    pair_rows = (HEADS // 2, 2 * n_rows)
    by_block = pl.BlockSpec((step, 2 * width), lambda i: (i, 0))
    g2 = (group2, c2, y2, flip(y2, "wsh", 1))
    c3 = flip(after(group3, y2), "wsh", 1)
    tokens_now, *toks = clock(after(tokens, y2), *toks)
    kv, qs, self_ext, self_mixed = call(
        functools.partial(self_forward_kernel, blocks, order, len(toks)), "self_forward", blocks,
        (scal, tokens_now, *toks, *g1),
        [SMEM, whole(tokens)] + [ANY] * (len(toks) + 4),
        (shape((n_keys, 2 * width), BF), shape(tall, BF), shape((n_rows, EXT), BF),
         shape(tall, F32)),
        [by_block] + fixed(tall, (n_rows, EXT), tall),
        [vm((width, width), BF), vm((width, 2 * width), BF), vm((step, width), BF),
         vm((step, EXT), BF)]
        + ([vm((*pair_rows, 1), F32), vm((*pair_rows, 1), F32), vm((*pair_rows, 128), F32)]
           if blocks > 1 else [vm((8, 128), F32)] * 3),
        8 + len(toks), 11, 8 * 2**20,
    )
    clock.tick(qs)
    if split:
        mem_side += [across_ctx(clock(item)[0]) for item in mem_line[2:]]
        mems = mem_line + mem_side
    else:
        mems = [lax.all_gather(mem_rows, "ctx", axis=0, tiled=True)]
    self_mixed_now, *g2_now = clock(self_mixed, *g2)
    first_sum, cqs = call(
        self_dense_kernel, "self_dense", 1,
        (scal, tokens, self_mixed_now, *g1, *g2_now),
        [SMEM, whole(tokens), whole(self_mixed)] + [ANY] * 8,
        (shape(tall, F32), shape(tall, BF)), fixed(tall, tall),
        [vm((width, width), BF), vm((width, width), BF), vm((16, width), BF)],
        12, 2, 2 * 2**20,
    )
    clock.tick(cqs)
    y3 = after(y3, cqs)
    g3 = (group3, c3, y3, flip(y3, "wsh", 1))
    if split:
        cq_line = gather_line(after(cqs, *mem_line[1:]))
    (cqs_now, *mems_now) = clock(cqs, *mems)
    memkv, cross_ext, cross_mixed = call(
        functools.partial(cross_forward_kernel, order, len(mems)), "cross_forward", 1,
        (scal, cqs_now, *mems_now, *g2),
        [SMEM, whole(cqs)] + [ANY] * (len(mems) + 4),
        (shape((all_mem, 2 * width), BF), shape((n_rows, EXT), BF), shape(tall, F32)),
        fixed((all_mem, 2 * width), (n_rows, EXT), tall),
        [vm((width, 2 * width), BF), vm((all_mem, width), BF), vm((all_mem, EXT), BF)],
        4 + len(mems), 12, 8 * 2**20,
    )
    clock.tick(cross_ext)
    if split:
        cq_line = clock.tick(jnp.concatenate(clock(*cq_line), axis=0))
        all_cq = [cq_line, across_ctx(cq_line)]
    else:
        all_cq = [lax.all_gather(cqs, "ctx", axis=0, tiled=True)]
    (cross_mixed_now, prev_now, *g3_now) = clock(cross_mixed, prev_cot, *g3)
    pay_dc, masked, grads, d_second, sums, keep_a, send_a = call(
        middle_kernel, "middle", 1,
        (scal, cross_mixed_now, cross_ext, first_sum, cot, prev_now, *g1, *g2, *g3_now),
        [SMEM] + [whole(a) for a in (cross_mixed, cross_ext, first_sum, cot, prev_cot)]
        + [ANY] * 12,
        (shape(pay_w, BF), shape(tall, BF), shape(tall, BF),
         shape(tall, F32), shape((8, hidden_units), F32), *grad_outs(1152)),
        fixed(pay_w, tall, tall, tall, (8, hidden_units), (2, 1152, 512), (2, 1152, 512)),
        [vm((width, width), BF), vm((width, hidden_units), BF),
         vm((hidden_units, width), BF), vm((2 * width, width), BF), vm((16, width), BF),
         vm(tall, BF), vm(tall, BF), vm((n_rows, hidden_units), BF)],
        40, 12, 20 * 2**20,
    )
    clock.tick(pay_dc)
    sum_a = Total(
        clock, "sum_a", scal,
        ((0, 512, 1), (512, 128, hidden_units // 512), (1024, 128, 1)), keep_a, send_a,
    )
    if split:
        dc_line = gather_line(pay_dc)
        dc_side = [across_ctx(pay_dc)]
    else:
        all_dc = [lax.all_gather(pay_dc, "ctx", axis=0, tiled=True)]
    next_row = permute(masked[:16], "ctx", lambda i: i - 1)
    (pay_dc_now,) = clock(pay_dc)
    (dq_cross,) = call(
        functools.partial(cross_query_kernel, order), "cross_query", 1,
        (scal, cqs, pay_dc_now, memkv),
        [SMEM] + [whole(a) for a in (cqs, pay_dc, memkv)],
        (shape(tall, BF),), tuple(fixed(tall)), [vm((all_mem, EXT), BF)], 0, 13, 5 * 2**20,
    )
    clock.tick(dq_cross)
    if split:
        dc_side += [across_ctx(clock(item)[0]) for item in dc_line[1:2]]
    sum_a.across()
    (dq_now,) = clock(dq_cross)
    d_first, pay_ds, keep_b, send_b = call(
        cross_dense_kernel, "cross_dense", 1,
        (scal, dq_now, first_sum, d_second, self_mixed, self_ext, sums, *g1, *g2),
        [SMEM]
        + [whole(a) for a in (dq_cross, first_sum, d_second, self_mixed, self_ext, sums)]
        + [ANY] * 8,
        (shape(tall, F32), shape(pay_w, BF), *grad_outs(384)),
        fixed(tall, pay_w, (2, 384, 512), (2, 384, 512)),
        [vm((width, width), BF), vm((width, width), BF), vm((16, width), BF),
         vm(tall, BF), vm(tall, BF), vm((8, hidden_units), F32)],
        12, 8, 6 * 2**20,
    )
    clock.tick(pay_ds)
    if split:
        ds_line = gather_line(pay_ds)
        dc_side += [across_ctx(clock(item)[0]) for item in dc_line[2:]]
        all_dc = dc_line + dc_side
    else:
        all_ds = [lax.all_gather(pay_ds, "ctx", axis=0, tiled=True)]
    pay_now, next_now = clock(pay_ds, next_row)
    part, slots, keep_b, send_b = call(
        functools.partial(self_query_kernel, blocks, order), "self_query", blocks,
        (scal, qs, pay_now, kv, tokens, d_first, masked, next_now, grads, keep_b, send_b, *g1, *g3),
        [SMEM, whole(qs), whole(pay_ds), by_block]
        + [whole(a) for a in (tokens, d_first, masked, next_row, grads, keep_b, send_b)] + [ANY] * 8,
        (shape(tall, F32), shape(tall, BF), *grad_outs(768)),
        fixed(tall, tall, (2, 768, 512), (2, 768, 512)),
        [vm((width, width), BF), vm((2 * width, width), BF), vm((n_rows, 2 * width), BF),
         vm(tall, F32), vm((step, EXT), BF)],
        12, 9, 8 * 2**20,
    )
    clock.tick(part)
    sum_b = Total(
        clock, "sum_b", scal,
        ((0, 128, 1), (128, 128, 1), (256, 8, 1), (384, 256, 1), (640, 128, 1)), keep_b, send_b,
    )
    if split:
        ds_side = [across_ctx(clock(item)[0]) for item in ds_line]
        all_ds = ds_line + ds_side

    def keys_back(name, x, queries, q_from, pays, extra, group, first, mask, cost):
        rows = x.shape[0]
        came = clock(*q_from, *pays)
        q_from, pays = came[: len(q_from)], came[len(q_from) :]
        result = call(
            functools.partial(
                key_kernel, blocks, queries, first, mask, (len(q_from), len(pays), len(extra))
            ),
            name, blocks,
            (scal, x, *q_from, *pays, *extra, *group),
            [SMEM, whole(x)] + [ANY] * (len(q_from) + len(pays)) + [whole(e) for e in extra]
            + [ANY] * 4,
            (shape((rows, width), F32), *grad_outs(256)),
            fixed((rows, width), (2, 256, 512), (2, 256, 512)),
            [vm((width, 2 * width), BF), vm((width, width) if queries else (16, 128), BF),
             vm((rows, 2 * width), BF),
             vm((rows, 2 * width) if blocks > 1 else (8, 128), F32), vm((rows, 2 * width), BF),
             vm((step, width), BF), vm((step, width + EXT), BF)],
            8 + len(q_from) + len(pays), cost, 8 * 2**20,
        )
        clock.tick(result[0])
        return result

    grad_mem, keep_m, send_m = keys_back(
        "cross_key", mem_rows, False, all_cq, all_dc, (), g2, 2 * width, 3, 12
    )
    sum_m = Total(clock, "sum_m", scal, ((0, 128, 2),), keep_m, send_m, True)
    sum_a.side()
    sum_b.across()
    sum_m.across()
    grad_input, keep_k, send_k = keys_back(
        "self_key", tokens, True, toks, all_ds, (part,), g1, width, 1, 11
    )
    sum_k = Total(clock, "sum_k", scal, ((0, 128, 2),), keep_k, send_k, True)
    sum_a.spread()
    sum_b.side()
    sum_k.across()
    sum_m.side()
    sum_a.collect()
    sum_b.spread()
    sum_m.spread()
    sum_k.side()
    sum_a.line()
    sum_b.collect()
    sum_m.collect()
    sum_k.spread()
    g_second, g_first, g_cout = sum_a.finish()
    sum_b.line()
    (g_ckv,) = sum_m.finish()
    sum_k.collect()
    g_out, g_cq, tiny, g_slot, g_q = sum_b.finish()
    (g_kv,) = sum_k.finish()
    return (
        slots[None],
        grad_input[None],
        grad_mem[None],
        g_q,
        g_kv,
        g_out,
        g_cq,
        g_ckv,
        g_cout,
        g_first,
        tiny[0],
        g_second,
        tiny[1, :128],
        g_slot,
        tiny[2:5, :128],
        tiny[5:8, :128],
    )


def solution(mesh):
    rows, split = P("wsh", "ctx", None), P("wsh", None)
    line, side = P("wsh"), P(None, "wsh")
    in_specs = (
        rows, rows, line, line, split, split, split, split, split, split, split, line, split, line,
        split, side, side, rows,
    )
    out_specs = (
        rows, rows, rows, split, split, split, split, split, split, split, line, split, line, split,
        side, side,
    )
    return jax.shard_map(shards, mesh=mesh, in_specs=in_specs, out_specs=out_specs, check_vma=False)
```
